128 devices in a mesh: batch: 4 (over z_hi, core), centers: 32 (over x, y, z_lo).
Axes of the slice: x: 4, y: 4, z: 4 (z_hi: 2, z_lo: 2; z = z_hi * 2 + z_lo), core: 2. Of those that a mesh axis runs over, the one named last changes fastest.
Arguments:
- pool_features: float32 [131072, 128], P(('batch', 'centers')), may hold values from -14 to 14
- pool_targets: float32 [131072, 64], P(('batch', 'centers')), may hold values from -6 to 6
- batch_index: int32 [8192], P(('batch', 'centers')), may hold values from 0 to 1023
- centers: float32 [16384, 128], P('centers'), may hold values from -14 to 14
- weights: float32 [16384, 64], P('centers'), as said below
- eig_vectors: float32 [16384, 1024], P(('batch', 'centers')), may hold values from -0.046875 to 0.046875
- eig_scale: float32 [1024], replicated, may hold values from 0.5 to 4
- nys_owner: int32 [16384, 1], P(('batch', 'centers')), may hold values from 0 to 31; in each aligned block of 128 rows (0 to 127, 128 to 255, ...) at most 8 rows name the same one
- nys_offset: int32 [16384], P(('batch', 'centers')), may hold values from 0 to 511
Outputs:
- residual_out: float32 [8192, 64], P(('batch', 'centers'))
- update: float32 [16384, 64], P('centers')
The draws below stay inside these ranges and needn't reach their ends.
Inputs may be any that keep to these rules, and one draw needn't show every extreme that they name: `nys_owner`: among the 128 rows of one device no owner is named more than 8 times; on some devices one owner is named exactly 8 times. `weights`: every column sums to zero.
All inputs are finite; a program needn't handle non-finite values.
Results may differ from the reference program's by a relative error of at most 0.0003.
Values sent between devices are 32-bit elements; how exact they have to be, the bound alone decides.
No kernel may reach another device: no remote copies, remote signals or barrier semaphores. Data moves between devices by JAX's collectives and lax.ppermute only.
A program may use at most 64 MiB of HBM per device.

```python
import math
import jax
import jax.numpy as jnp
import numpy as np
from jax import lax

D = 128
OUT = 64
Q = 1024
DEPTH = 3
NYS_DEV = 128
POOL_DEV = 1024
ROWS_LOC = 64
CDEV = 512
CAP = 8
M = 8192
P_SIZE = 16384
S = 16384
POOL = 131072
N_CENTERS = 32


def cluster_means(key):
    means = jax.random.truncated_normal(jax.random.fold_in(key, 101), -4.0, 4.0, (16, D), jnp.float32)
    return means


def noisy_points(key, count, salt):
    means = cluster_means(key)
    label = jax.random.randint(jax.random.fold_in(key, salt), (count,), 0, means.shape[0])
    level = jnp.exp(jax.random.uniform(jax.random.fold_in(key, salt + 1), (count, 1), jnp.float32, math.log(0.15), math.log(2.0)))
    noise = jax.random.truncated_normal(jax.random.fold_in(key, salt + 2), -4.0, 4.0, (count, D), jnp.float32)
    return means[label] + level * noise


def draw_pool_features(key, part):
    return noisy_points(key, POOL, 301)


def draw_centers(key, part):
    return noisy_points(key, P_SIZE, 401)


def draw_weights(key, part):
    base = jax.random.normal(jax.random.fold_in(key, 501), (P_SIZE, OUT), jnp.float32)
    base = base - jnp.mean(base, axis=0, keepdims=True)
    return base * (0.3 / math.sqrt(P_SIZE))


def set_ends(values, rng, smallest, high):
    longest = values.shape.index(max(values.shape))
    spots = []
    for shift in (0, 1):
        where = [jax.random.randint(jax.random.fold_in(rng, axis), (), 0, length) for axis, length in enumerate(values.shape)]
        where[longest] = (where[longest] + shift) % values.shape[longest]
        spots.append(tuple(where))
    return values.at[spots[0]].set(smallest).at[spots[1]].set(high)


def steps_of(stream_key, extent, shards, low, largest):
    factor_of, own = 1.0, jax.random.fold_in(stream_key, 6)
    for position, blocks in shards:
        draws = jnp.exp(jax.random.uniform(jax.random.fold_in(own, position), (blocks,), jnp.float32, low / len(shards), largest / len(shards)))
        factor_of = factor_of * jnp.repeat(draws, extent[position] // blocks).reshape([-1 if axis == position else 1 for axis in range(len(extent))])
    return factor_of


def routed_block(own_key, own, number, rows, number_of, top, bound, slope):
    sequence = jax.random.permutation(own_key, number_of)
    crowded, common = load_shares(number_of, rows * top, bound, slope, True), load_shares(number_of, rows * top, bound, slope, False)
    places = jnp.arange(number_of)

    def named(lengths, turn):
        used = int((lengths > 0).sum())
        fixed = max(1, used // 4)
        moved = fixed + (places - fixed + turn * (used - fixed)) % max(1, number_of - fixed)
        return jnp.zeros((number_of,), jnp.int32).at[sequence[jnp.where(places < fixed, places, moved)]].set(jnp.asarray(lengths, jnp.int32))

    lengths = jnp.where(number % 4 == 0, named(crowded, number // 4), named(common, number - number // 4 - 1))
    mixed = jax.random.permutation(jax.random.fold_in(own, 3), number_of)
    donor, receiver = mixed[0:number_of // 2 * 2:2], mixed[1:number_of // 2 * 2:2]
    slack = jnp.minimum(lengths[donor] - 1, bound - lengths[receiver]) // 2
    slack = jnp.where((donor == sequence[0]) | (receiver == sequence[0]) | (lengths[receiver] == 0), 0, jnp.maximum(slack, 0))
    moved = jax.random.randint(jax.random.fold_in(own, 4), (number_of // 2,), 0, 1 << 20) % (slack + 1)
    lengths = lengths.at[donor].add(-moved).at[receiver].add(moved)
    members = jnp.searchsorted(jnp.cumsum(lengths), jnp.arange(rows * top), side="right").astype(jnp.int32)
    listing = members.reshape(top, rows).T
    listing = listing[jax.random.permutation(jax.random.fold_in(own, 1), rows)]
    turn = jax.random.randint(jax.random.fold_in(own, 2), (rows, 1), 0, top)
    return jnp.take_along_axis(listing, (jnp.arange(top)[None, :] + turn) % top, axis=1)


def load_shares(number_of, total, reach, lean, full):
    weights = [(1 << 20) // math.isqrt(standing ** lean) + 1 for standing in range(1, number_of + 1)]
    largest = reach if full else min(reach, max(-(-total // number_of), total * weights[0] // sum(weights)))
    least = 1 if total - largest >= number_of - 1 else 0
    holding, surplus = [largest] + [least] * (number_of - 1), total - largest - least * (number_of - 1)
    while surplus > 0:
        movable = [i for i in range(1, number_of) if holding[i] < largest] or [i for i in range(1, number_of) if holding[i] < reach]
        whole, left = sum([weights[i] for i in movable]), surplus
        for i in movable:
            extra = min(reach - holding[i], max(1, left * weights[i] // whole), surplus)
            holding[i] = holding[i] + extra
            surplus = surplus - extra
    return np.array(holding)


def normal_values(stream_key, shape, deviation, bound, cuts=(), kind=jnp.bfloat16):
    values = jax.random.normal(stream_key, shape, jnp.float32) * deviation
    if len(cuts) > 0:
        values = steps_of(stream_key, shape, cuts, -0.22, 0.18) * values
    return jnp.clip(values, min=-bound, max=bound).astype(kind)


def setup_inputs(seed: int = 0) -> dict:
    key_list = jax.random.split(jax.random.key(seed), 10)
    pool_features = draw_pool_features(jax.random.fold_in(key_list[9], 71), 0)
    pool_targets = normal_values(key_list[1], (POOL, OUT), 1.0, 6.0, ((0, 128),), jnp.float32)
    batch_index = set_ends(jax.random.randint(key_list[2], (M,), 0, POOL_DEV), jax.random.fold_in(key_list[2], 1), 0, POOL_DEV - 1).astype(jnp.int32)
    centers = draw_centers(jax.random.fold_in(key_list[9], 71), 0)
    weights = draw_weights(jax.random.fold_in(key_list[9], 71), 0)
    eig_vectors = normal_values(key_list[5], (S, Q), S ** -0.5, 0.046875, ((0, 128),), jnp.float32)
    eig_scale = jnp.clip(jnp.exp(jax.random.uniform(key_list[6], (Q,), jnp.float32, math.log(0.5), math.log(4.0))), 0.5, 4.0)
    nys_owner_keys = jax.random.split(jax.random.fold_in(key_list[7], 1), S // NYS_DEV)
    nys_owner_turns = jax.random.permutation(jax.random.fold_in(key_list[7], 3), S // NYS_DEV)
    nys_owner = jax.vmap(lambda own, number: routed_block(jax.random.fold_in(key_list[7], 2), own, number, NYS_DEV, N_CENTERS, 1, CAP, 2))(nys_owner_keys, nys_owner_turns).reshape((S, 1))
    nys_offset = set_ends(jax.random.randint(key_list[8], (S,), 0, CDEV), jax.random.fold_in(key_list[8], 1), 0, CDEV - 1).astype(jnp.int32)
    return {"pool_features": pool_features, "pool_targets": pool_targets, "batch_index": batch_index, "centers": centers, "weights": weights, "eig_vectors": eig_vectors, "eig_scale": eig_scale, "nys_owner": nys_owner, "nys_offset": nys_offset}


epsilon = 1e-06
highest = lax.Precision.HIGHEST

def kernel_rows(row_block, center_block, center_norm):
    inner_prod = lax.dot_general(row_block, center_block, (((1,), (1,)), ((), ())), precision=highest, preferred_element_type=jnp.float32) / row_block.shape[1]
    row_norm = lax.optimization_barrier(jnp.mean(row_block * row_block, axis=1)) + epsilon
    norm_scale = jnp.sqrt(row_norm[:, None] * center_norm[None, :])
    sigma_now = inner_prod
    tangent = inner_prod
    for depth_step in range(DEPTH):
        cosine = sigma_now / norm_scale
        arc_angle = jnp.arccos(cosine)
        remain = (math.pi - arc_angle) / math.pi
        sigma_now = norm_scale * (jnp.sqrt(1.0 - cosine * cosine) + (math.pi - arc_angle) * cosine) / math.pi
        tangent = sigma_now + tangent * remain
    return tangent

def reference(pool_features, pool_targets, batch_index, centers, weights, eig_vectors, eig_scale, nys_owner, nys_offset):
    rows_total = batch_index.shape[0]
    block_of = jnp.arange(rows_total, dtype=jnp.int32) // ROWS_LOC
    picked = (block_of * POOL_DEV + batch_index).astype(jnp.int32)
    features = pool_features[picked]
    targets = pool_targets[picked]
    center_norm = lax.optimization_barrier(jnp.mean(centers * centers, axis=1)) + epsilon
    block_size = math.gcd(512, rows_total)
    block_count = rows_total // block_size
    feat_blocks = features.reshape(block_count, block_size, features.shape[1])
    targ_blocks = targets.reshape(block_count, block_size, targets.shape[1])

    def step_block(accum, pieces):
        feat, targ = pieces
        kern = kernel_rows(feat, centers, center_norm)
        pred = jnp.dot(kern, weights, precision=highest, preferred_element_type=jnp.float32)
        resid = pred - targ
        accum = accum + lax.dot_general(kern, resid, (((0,), (0,)), ((), ())), precision=highest, preferred_element_type=jnp.float32)
        return (accum, resid)
    total, resid_blocks = lax.scan(step_block, jnp.zeros((centers.shape[0], weights.shape[1]), jnp.float32), (feat_blocks, targ_blocks))
    residual_out = resid_blocks.reshape(rows_total, weights.shape[1])
    grads = total / math.sqrt(rows_total)
    nys = (nys_owner[:, 0] * CDEV + nys_offset).astype(jnp.int32)
    coeff = lax.dot_general(eig_vectors, grads[nys], (((0,), (0,)), ((), ())), precision=highest, preferred_element_type=jnp.float32)
    corr_rows = jnp.dot(eig_vectors, eig_scale[:, None] * coeff, precision=highest, preferred_element_type=jnp.float32)
    correction = jnp.zeros((centers.shape[0], weights.shape[1]), jnp.float32).at[nys].add(corr_rows)
    return (residual_out, correction - grads)
```

```python
import itertools
import math

import jax
import jax.numpy as jnp
from jax import lax
from jax.experimental import pallas as pl
from jax.experimental.pallas import tpu as pltpu
from jax.sharding import Mesh, PartitionSpec as P

EPS = 1e-06
CAP = 8
BF = jnp.bfloat16
F32 = jnp.float32
SIZES = {"zh": 2, "core": 2, "x": 4, "y": 4, "zl": 2}
ALL = ("zh", "core", "x", "y", "zl")
CENTERS = ("x", "y", "zl")
VMEM = pl.BlockSpec(memory_space=pltpu.VMEM)

ACOS_FULL = (
    0.4999999701976776, -0.31830424070358276, 0.24984024465084076, -0.210431307554245,
    0.17730562388896942, -0.13514360785484314, 0.0806083083152771, -0.031184406951069832,
    0.005619336850941181,
)
ACOS_HIGH = (
    0.4999392330646515, -0.3173876106739044, 0.24387668073177338, -0.18864932656288147,
    0.12859871983528137, -0.06701970100402832, 0.02248113788664341, -0.003529248759150505,
)

NN = (((1,), (0,)), ((), ()))
NT = (((1,), (1,)), ((), ()))


def mm(a, b, dims):
    return lax.dot_general(a, b, dims, preferred_element_type=F32)


def split2(x):
    hi = x.astype(BF)
    return hi, (x - hi.astype(F32)).astype(BF)


def split3(x):
    hi = x.astype(BF)
    rest = x - hi.astype(F32)
    mid = rest.astype(BF)
    return hi, mid, (rest - mid.astype(F32)).astype(BF)


def pick(onehot, x, dims, flip=False):
    parts = split3(x)
    prods = [mm(p, onehot, dims) if flip else mm(onehot, p, dims) for p in parts]
    return prods[0] + prods[1] + prods[2]


def full_nt(a, b):
    a1, a2, a3 = split3(a)
    b1, b2, b3 = split3(b)
    return (
        mm(a1, b1, NT) + (mm(a1, b2, NT) + mm(a2, b1, NT))
        + (mm(a2, b2, NT) + mm(a1, b3, NT) + mm(a3, b1, NT))
    )


def horner(coefs, x):
    acc = coefs[-1] * x + coefs[-2]
    for c in coefs[-3::-1]:
        acc = acc * x + c
    return acc


def ntk_over_scale(c):
    c = jnp.clip(c, -1.0, 1.0)
    inv_pi = 1.0 / math.pi
    ntk = c
    for layer in range(3):
        w = jnp.maximum(1.0 - c * c, 1e-30)
        root = w * lax.rsqrt(w)
        arg = jnp.abs(c) if layer == 0 else c
        angle = root * horner(ACOS_HIGH if layer == 2 else ACOS_FULL, arg)
        remain = 1.0 - angle
        if layer == 0:
            remain = jnp.where(c < 0.0, angle, remain)
        c = root * inv_pi + remain * c
        ntk = c + ntk * remain
    return ntk


def prep_body(pool_f, pool_t, index, eig, owner_row, owner_col, offset_row, send, targ, scale):
    rows, pool = index.shape[0], pool_f.shape[0]
    hot = (index[...] == lax.broadcasted_iota(jnp.int32, (rows, pool), 1)).astype(BF)
    feats = pick(hot, pool_f[...], NN)
    targets = pick(hot, pool_t[...], NN)
    sa = jnp.sqrt(jnp.mean(feats * feats, axis=1, keepdims=True) + EPS)
    unit = feats / sa
    half = rows // 2
    targ[...] = jnp.concatenate([targets[:half], targets[half:]], axis=1)
    wide = jnp.broadcast_to(sa, targets.shape)
    scale[...] = jnp.concatenate([wide[:half], wide[half:]], axis=1)
    count, q = eig.shape
    peers = send.shape[0]
    same = (owner_col[...] == owner_row[...]).astype(jnp.int32)
    earlier = lax.broadcasted_iota(jnp.int32, (count, count), 0) < lax.broadcasted_iota(
        jnp.int32, (count, count), 1
    )
    rank = jnp.sum(jnp.where(earlier, same, 0), axis=0, keepdims=True)
    slot = owner_row[...] * CAP + rank
    place = slot == lax.broadcasted_iota(jnp.int32, (peers * CAP, count), 0)
    offs = jnp.sum(jnp.where(place, offset_row[...].astype(F32), 0.0), axis=1, keepdims=True)
    offs = jnp.broadcast_to(offs, (peers * CAP, 128))
    vectors = pick(place.astype(BF), eig[...], NN)
    for o in range(peers):
        send[o, 0:rows, :] = unit
        own = slice(o * CAP, (o + 1) * CAP)
        for j in range(q // 128):
            send[o, rows + CAP * j : rows + CAP * (j + 1), :] = vectors[own, 128 * j : 128 * (j + 1)]
        send[o, rows + CAP * (q // 128) :, :] = offs[own]


def kernel_body(recv, centers, weights, khi_out, klo_out, pred, cen, wts, cos):
    step = pl.program_id(0)
    src, rows, dim = recv.shape
    out = weights.shape[1]

    @pl.when(step == 0)
    def _():
        b = centers[...]
        sb = jnp.sqrt(jnp.mean(b * b, axis=1, keepdims=True) + EPS)
        b1, b2, b3 = split3(b / sb)
        cen[0] = jnp.concatenate([b1, b1], axis=1)
        cen[1] = jnp.concatenate([b2, b2], axis=1)
        cen[2] = jnp.concatenate([b3, b1], axis=1)
        w1, w2 = split2(weights[...] * sb)
        wts[...] = jnp.concatenate([w1, w2], axis=1)

    a1, a2, a3 = split3(recv[...].reshape(src * rows, dim))
    near = jnp.concatenate([a1, a2], axis=1)
    far = jnp.concatenate([a1, a3], axis=1)
    cos[...] = (mm(near, cen[0], NT) + (mm(near, cen[1], NT) + mm(far, cen[2], NT))) * (1.0 / dim)
    sub = 32

    def body(i, _):
        at = pl.ds(pl.multiple_of(i * sub, sub), sub)
        hi, lo = split2(ntk_over_scale(cos[at, :]))
        khi_out[at, :] = hi
        klo_out[at, :] = lo
        return 0

    lax.fori_loop(0, src * rows // sub, body, 0)
    both = mm(khi_out[...], wts[...], NN) + mm(klo_out[...], wts[...], NN)
    total = (both[:, :out] + both[:, out:]).reshape(src, 2, rows // 2, out)
    pred[...] = jnp.concatenate([total[:, 0], total[:, 1]], axis=2)


def residual_body(parts, targ, scale, resid, send, *, norm):
    value = scale[...] * jnp.sum(parts[...], axis=0) - targ[...]
    half, out = value.shape[0], value.shape[1] // 2
    resid[0:half, :] = value[:, :out]
    resid[half:, :] = value[:, out:]
    ready = value * scale[...] * norm
    for o in range(send.shape[0]):
        send[o] = ready


def grads_body(resid, khi, klo, centers, grads):
    src, half, wide = resid.shape
    out = wide // 2
    r = resid[...]
    r = jnp.concatenate([r[:, :, :out], r[:, :, out:]], axis=1).reshape(src * half * 2, out)
    r1, r2 = split2(r.T)
    rr = jnp.concatenate([r1, r2], axis=0)
    both = mm(rr, khi[...], NN) + mm(rr, klo[...], NN)
    b = centers[...]
    nb = full_nt(jnp.ones((8, b.shape[1]), F32), b * b)[0:1] * (1.0 / b.shape[1]) + EPS
    grads[...] = (both[:out] + both[out:]) * jnp.sqrt(nb)


def spread_of(recv, rows, total):
    peers = recv.shape[0]
    offs = recv[:, rows:, :].reshape(peers * CAP, 128)
    cols = lax.broadcasted_iota(jnp.int32, (peers * CAP, 128), 1).astype(F32)
    return jnp.concatenate(
        [(offs == cols + float(128 * k)).astype(BF) for k in range(total // 128)], axis=1
    )


def coeff_body(recv, grads, coeff):
    peers, height = recv.shape[0], recv.shape[1]
    q = coeff.shape[1]
    first = height - CAP * (q // 128 + 1)
    hot = spread_of(recv, height - CAP, grads.shape[1])
    g1, g2 = split2(pick(hot, grads[...], NT, flip=True))
    gg = jnp.concatenate([g1, g2], axis=0)
    out = grads.shape[0]
    for j in range(q // 128):
        block = recv[:, first + CAP * j : first + CAP * (j + 1), :].reshape(peers * CAP, 128)
        e1, e2 = split2(block)
        both = mm(gg, e1, NN) + mm(gg, e2, NN)
        coeff[:, 128 * j : 128 * (j + 1)] = both[:out] + both[out:]


def corr_body(recv, coeff, eig_scale, corr):
    peers, height = recv.shape[0], recv.shape[1]
    out, q = coeff.shape
    first = height - CAP * (q // 128 + 1)
    hot = spread_of(recv, height - CAP, corr.shape[1])
    total = jnp.zeros((2 * out, peers * CAP), F32)
    for j in range(q // 128):
        at = slice(128 * j, 128 * (j + 1))
        block = recv[:, first + CAP * j : first + CAP * (j + 1), :].reshape(peers * CAP, 128)
        e1, e2 = split2(block)
        c1, c2 = split2(coeff[:, at] * eig_scale[:, at])
        cc = jnp.concatenate([c1, c2], axis=0)
        total = total + mm(cc, e1, NT) + mm(cc, e2, NT)
    corr[...] = pick(hot, total[:out] + total[out:], NN, flip=True)


def finish_body(a, b, grads, update):
    update[...] = (a[...] + b[...] - grads[...]).T


def shape(*dims, dtype=F32):
    return jax.ShapeDtypeStruct(dims, dtype)


def params(mib=32):
    return pltpu.CompilerParams(vmem_limit_bytes=mib << 20)


def call(body, outs, *args, mib=32, **kw):
    many = isinstance(outs, (list, tuple))
    return pl.pallas_call(
        body,
        out_shape=outs,
        in_specs=[VMEM] * len(args),
        out_specs=[VMEM] * len(outs) if many else VMEM,
        compiler_params=params(mib),
        **kw,
    )(*args)


def shifts(axis):
    n = SIZES[axis]
    return [[(i, (i + s) % n) for i in range(n)] for s in range(1, n)]


def exchange(v, axes):
    sizes = [SIZES[a] for a in axes]
    spots = list(itertools.product(*[range(s) for s in sizes]))
    flat = {p: i for i, p in enumerate(spots)}
    total = v
    for off in spots[1:]:
        perm = [
            (flat[p], flat[tuple((i + o) % s for i, o, s in zip(p, off, sizes))]) for p in spots
        ]
        total = total + lax.ppermute(v, axes, perm)
    return total


def per_device(
    pool_features, pool_targets, batch_index, centers, weights,
    eig_vectors, eig_scale, nys_owner, nys_offset,
):
    rows, dim = batch_index.shape[0], pool_features.shape[1]
    peers = SIZES["x"] * SIZES["y"] * SIZES["zl"]
    cdev, out = weights.shape
    count, q = eig_vectors.shape
    half = rows // 2
    height = rows + CAP * (q // 128 + 1)
    norm = 1.0 / math.sqrt(rows * peers * SIZES["zh"] * SIZES["core"])

    send, targ, scale = call(
        prep_body,
        [shape(peers, height, dim), shape(half, 2 * out), shape(half, 2 * out)],
        pool_features, pool_targets, batch_index[:, None], eig_vectors,
        nys_owner.reshape(1, count), nys_owner, nys_offset[None, :],
    )
    recv = lax.all_to_all(send, CENTERS, split_axis=0, concat_axis=0, tiled=True)

    group = 8
    khi, klo, pred = pl.pallas_call(
        kernel_body,
        grid=(peers // group,),
        in_specs=[
            pl.BlockSpec((group, rows, dim), lambda i: (i, 0, 0)),
            pl.BlockSpec((cdev, dim), lambda i: (0, 0)),
            pl.BlockSpec((cdev, out), lambda i: (0, 0)),
        ],
        out_specs=[
            pl.BlockSpec((group * rows, cdev), lambda i: (i, 0)),
            pl.BlockSpec((group * rows, cdev), lambda i: (i, 0)),
            pl.BlockSpec((group, half, 2 * out), lambda i: (i, 0, 0)),
        ],
        out_shape=[
            shape(peers * rows, cdev, dtype=BF),
            shape(peers * rows, cdev, dtype=BF),
            shape(peers, half, 2 * out),
        ],
        scratch_shapes=[
            pltpu.VMEM((3, cdev, 2 * dim), BF),
            pltpu.VMEM((cdev, 2 * out), BF),
            pltpu.VMEM((group * rows, cdev), F32),
        ],
        compiler_params=params(),
    )(recv, centers, weights)

    parts = lax.all_to_all(pred, CENTERS, split_axis=0, concat_axis=0, tiled=True)
    resid, ready = call(
        lambda *refs: residual_body(*refs, norm=norm),
        [shape(rows, out), shape(peers, half, 2 * out)],
        parts, targ, scale,
    )
    every = lax.all_to_all(ready, CENTERS, split_axis=0, concat_axis=0, tiled=True)
    grads = call(grads_body, shape(out, cdev), every, khi, klo, centers)
    grads = exchange(grads, ("core",))
    grads = exchange(grads, ("zh",))
    coeff = call(coeff_body, shape(out, q), recv, grads)
    coeff = exchange(coeff, ("core",))
    me = lax.axis_index("core")
    mine = lax.dynamic_slice_in_dim(coeff, me * (out // 2), out // 2, 0)
    mine = exchange(mine, ("x",))
    mine = exchange(mine, ("y",))
    mine = exchange(mine, ("zh", "zl"))
    other = lax.ppermute(mine, "core", [(0, 1), (1, 0)])
    coeff = jnp.where(
        me == 0, jnp.concatenate([mine, other], 0), jnp.concatenate([other, mine], 0)
    )
    corr = call(corr_body, shape(out, cdev), recv, coeff, eig_scale[None, :])
    corr = exchange(corr, ("core",))
    far = lax.ppermute(corr, "zh", [(0, 1), (1, 0)])
    update = call(finish_body, shape(cdev, out), corr, far, grads)
    return resid, update


def solution(mesh):
    fine = Mesh(mesh.devices.reshape(tuple(SIZES[a] for a in ALL)), ALL)
    placed = (
        P(ALL, None),
        P(ALL, None),
        P(ALL),
        P(CENTERS, None),
        P(CENTERS, None),
        P(ALL, None),
        P(),
        P(ALL, None),
        P(ALL),
    )
    return jax.shard_map(
        per_device,
        mesh=fine,
        in_specs=placed,
        out_specs=(P(ALL, None), P(CENTERS, None)),
        check_vma=False,
    )
```

```python
import functools
import itertools
import math

import jax
import jax.numpy as jnp
from jax import lax
from jax.experimental import pallas as pl
from jax.experimental.pallas import tpu as pltpu
from jax.sharding import Mesh, PartitionSpec as P

EPS = 1e-06
CAP = 8
BF = jnp.bfloat16
F32 = jnp.float32
SIZES = {"zh": 2, "core": 2, "x": 4, "y": 4, "zl": 2}
ALL = ("zh", "core", "x", "y", "zl")
CENTERS = ("x", "y", "zl")
VMEM = pl.BlockSpec(memory_space=pltpu.VMEM)

ACOS_FULL = (
    0.4999999701976776, -0.31830424070358276, 0.24984024465084076, -0.210431307554245,
    0.17730562388896942, -0.13514360785484314, 0.0806083083152771, -0.031184406951069832,
    0.005619336850941181,
)
ACOS_HIGH = (
    0.4999392330646515, -0.3173876106739044, 0.24387668073177338, -0.18864932656288147,
    0.12859871983528137, -0.06701970100402832, 0.02248113788664341, -0.003529248759150505,
)

NN = (((1,), (0,)), ((), ()))
NT = (((1,), (1,)), ((), ()))


def mm(a, b, dims):
    return lax.dot_general(a, b, dims, preferred_element_type=F32)


def split2(x):
    hi = x.astype(BF)
    return hi, (x - hi.astype(F32)).astype(BF)


def split3(x):
    hi = x.astype(BF)
    rest = x - hi.astype(F32)
    mid = rest.astype(BF)
    return hi, mid, (rest - mid.astype(F32)).astype(BF)


def pick(onehot, x, dims, flip=False):
    parts = split3(x)
    prods = [mm(p, onehot, dims) if flip else mm(onehot, p, dims) for p in parts]
    return prods[0] + prods[1] + prods[2]


def full_nt(a, b):
    a1, a2, a3 = split3(a)
    b1, b2, b3 = split3(b)
    return (
        mm(a1, b1, NT) + (mm(a1, b2, NT) + mm(a2, b1, NT))
        + (mm(a2, b2, NT) + mm(a1, b3, NT) + mm(a3, b1, NT))
    )


def horner(coefs, x):
    acc = coefs[-1] * x + coefs[-2]
    for c in coefs[-3::-1]:
        acc = acc * x + c
    return acc


def ntk_over_scale(c):
    inv_pi = 1.0 / math.pi
    ntk = c
    for layer in range(3):
        w = jnp.maximum(1.0 - c * c, 1e-30)
        root = w * lax.rsqrt(w)
        arg = jnp.abs(c) if layer == 0 else c
        angle = root * horner(ACOS_HIGH if layer == 2 else ACOS_FULL, arg)
        remain = jnp.where(c < 0.0, angle, 1.0 - angle) if layer == 0 else 1.0 - angle
        if layer == 2:
            return root * inv_pi + remain * (c + ntk)
        c = root * inv_pi + remain * c
        ntk = c + ntk * remain


def rows_hot(index, width):
    n = index.shape[1]
    col = jnp.broadcast_to(index.astype(F32), (128, n)).T
    lane = lax.broadcasted_iota(jnp.int32, (n, 128), 1).astype(F32)
    return jnp.concatenate(
        [(col == lane + float(128 * k)).astype(BF) for k in range(width // 128)], axis=1
    )


def features_body(pool_f, index, send, scale):
    rows = index.shape[1]
    feats = pick(rows_hot(index[...], pool_f.shape[0]), pool_f[...], NN)
    sa = jnp.sqrt(jnp.mean(feats * feats, axis=1, keepdims=True) + EPS)
    unit = feats / sa
    half, wide = scale.shape
    sa = jnp.broadcast_to(sa, (rows, wide // 2))
    scale[...] = jnp.concatenate([sa[:half], sa[half:]], axis=1)
    for o in range(send.shape[0]):
        send[o] = unit


def vectors_body(core, pool_t, index, eig, mate_eig, nys, mate_nys, send, targ, *, cdev):
    hot = rows_hot(index[...], pool_t.shape[1])
    targets = pick(hot, pool_t[...], NT, flip=True).T
    half = targets.shape[0] // 2
    targ[...] = jnp.concatenate([targets[:half], targets[half:]], axis=1)
    count, q = eig.shape
    part = q // 2
    peers = send.shape[0]
    blocks = part // 128
    mine = pl.ds(pl.multiple_of(core[0] * part, part), part)
    earlier = lax.broadcasted_iota(jnp.int32, (count, count), 0) < lax.broadcasted_iota(
        jnp.int32, (count, count), 1
    )
    for table, (vec, where) in enumerate(((eig, nys), (mate_eig, mate_nys))):
        owner = where[...] // cdev
        offset = where[...] - owner * cdev
        row = jnp.broadcast_to(owner.astype(F32), (count, count))
        same = jnp.where(row.T == row, 1.0, 0.0)
        rank = jnp.sum(jnp.where(earlier, same, 0.0), axis=0, keepdims=True).astype(jnp.int32)
        place = owner * CAP + rank == lax.broadcasted_iota(jnp.int32, (peers * CAP, count), 0)
        offs = jnp.sum(jnp.where(place, offset.astype(F32), 0.0), axis=1, keepdims=True)
        offs = jnp.broadcast_to(offs, (peers * CAP, 128))
        vectors = pick(place.astype(BF), vec[:, mine], NN)
        for o in range(peers):
            own = slice(o * CAP, (o + 1) * CAP)
            for j in range(blocks):
                at = CAP * (2 * j + table)
                send[o, at : at + CAP, :] = vectors[own, 128 * j : 128 * (j + 1)]
            at = CAP * (2 * blocks + table)
            send[o, at : at + CAP, :] = offs[own]


def kernel_body(recv, centers, weights, kern, pred, cen, wts, cos_a, cos_b, lhs, *, block, sub):
    src, rows, dim = recv.shape
    out, count = weights.shape
    b = centers[...]
    sb = jnp.sqrt(jnp.mean(b * b, axis=1, keepdims=True) + EPS)
    b1, b2, b3 = split3(b / sb * (1.0 / dim))
    cen[...] = jnp.concatenate([b1, b1, b2, b2, b3, b1], axis=1)
    w1, w2 = split2(weights[...].T * sb)
    w = jnp.concatenate([w1, w2], axis=1)
    wts[...] = jnp.concatenate([w, w], axis=0)
    blocks, group = src * rows // block, block // rows

    def stage(i):
        a1, a2, a3 = split3(recv[pl.ds(i * group, group)].reshape(block, dim))
        lhs[...] = jnp.concatenate([a1, a2, a1, a2, a1, a3], axis=1)

    def cosines(dst, n):
        at = slice(n * (count // 2), (n + 1) * (count // 2))
        dst[:, at] = mm(lhs[...], cen[at, :], NT)

    def elementwise(i, values, n):
        at = pl.ds(pl.multiple_of(i * block + n * sub, sub), sub)
        hi, lo = split2(ntk_over_scale(values[n * sub : (n + 1) * sub, :]))
        kern[at, :count] = hi
        kern[at, count:] = lo

    def predict(i):
        both = mm(kern[pl.ds(pl.multiple_of(i * block, block), block), :], wts[...], NN)
        total = (both[:, :out] + both[:, out:]).reshape(group, 2, rows // 2, out)
        pred[pl.ds(i * group, group)] = jnp.concatenate([total[:, 0], total[:, 1]], axis=2)

    def step(i, before, now, later):
        elems = [functools.partial(elementwise, i, now, n) for n in range(block // sub)]
        others = [
            functools.partial(cosines, later, 0),
            functools.partial(cosines, later, 1),
            functools.partial(predict, before),
        ]
        stage(jnp.minimum(i + 1, blocks - 1))
        every = len(elems) // len(others)
        for n, f in enumerate(elems):
            if n % every == 0 and others:
                others.pop(0)()
            f()

    stage(0)
    cosines(cos_a, 0)
    cosines(cos_a, 1)

    def pair(h, _):
        step(2 * h, jnp.maximum(2 * h - 1, 0), cos_a, cos_b)
        step(2 * h + 1, 2 * h, cos_b, cos_a)
        return 0

    lax.fori_loop(0, blocks // 2, pair, 0)
    predict(blocks - 1)


def residual_body(parts, targ, scale, resid, send, *, norm):
    value = scale[...] * jnp.sum(parts[...], axis=0) - targ[...]
    half, out = value.shape[0], value.shape[1] // 2
    resid[0:half, :] = value[:, :out]
    resid[half:, :] = value[:, out:]
    ready = value * scale[...] * norm
    for o in range(send.shape[0]):
        send[o] = ready


def grads_body(resid, kern, centers, grads):
    src, half, wide = resid.shape
    out, count = grads.shape
    r = resid[...]
    r = jnp.concatenate([r[:, :, :out], r[:, :, out:]], axis=1).reshape(src * half * 2, out)
    r1, r2 = split2(r.T)
    both = mm(jnp.concatenate([r1, r2], axis=0), kern[...], NN)
    both = both[:out] + both[out:]
    b = centers[...]
    nb = full_nt(jnp.ones((8, b.shape[1]), F32), b * b)[0:1] * (1.0 / b.shape[1]) + EPS
    grads[...] = (both[:, :count] + both[:, count:]) * jnp.sqrt(nb)


def unpack(recv, n):
    peers = recv.shape[0]
    return recv[:, 2 * CAP * n : 2 * CAP * (n + 1), :].reshape(peers * 2 * CAP, 128)


def points_hot(tables, blocks, width):
    offs = jnp.concatenate([unpack(t, blocks) for t in tables], axis=0)
    lane = lax.broadcasted_iota(jnp.int32, offs.shape, 1).astype(F32)
    return jnp.concatenate(
        [(offs == lane + float(128 * k)).astype(BF) for k in range(width // 128)], axis=1
    )


def coeff_body(near, far, grads, coeff):
    out, part = coeff.shape
    blocks = part // 128
    hot = points_hot((near, far), blocks, grads.shape[1])
    g1, g2 = split2(pick(hot, grads[...], NT, flip=True))
    gg = jnp.concatenate([g1, g2], axis=0)
    for j in range(blocks):
        e1, e2 = split2(jnp.concatenate([unpack(near, j), unpack(far, j)], axis=0))
        both = mm(gg, e1, NN) + mm(gg, e2, NN)
        coeff[:, 128 * j : 128 * (j + 1)] = both[:out] + both[out:]


def corr_body(core, near, far, coeff, eig_scale, corr):
    out, part = coeff.shape
    blocks = part // 128
    hot = points_hot((near, far), blocks, corr.shape[1])
    total = jnp.zeros((2 * out, hot.shape[0]), F32)
    for j in range(blocks):
        at = slice(128 * j, 128 * (j + 1))
        e1, e2 = split2(jnp.concatenate([unpack(near, j), unpack(far, j)], axis=0))
        scale = eig_scale[:, pl.ds(pl.multiple_of(core[0] * part + 128 * j, 128), 128)]
        c1, c2 = split2(coeff[:, at] * scale)
        cc = jnp.concatenate([c1, c2], axis=0)
        total = total + mm(cc, e1, NT) + mm(cc, e2, NT)
    corr[...] = pick(hot, total[:out] + total[out:], NN, flip=True)


def shape(*dims, dtype=F32):
    return jax.ShapeDtypeStruct(dims, dtype)


def params(mib=16):
    return pltpu.CompilerParams(vmem_limit_bytes=mib << 20)


def call(body, outs, *args, mib=16, scalars=0, **kw):
    many = isinstance(outs, (list, tuple))
    smem = pl.BlockSpec(memory_space=pltpu.SMEM)
    return pl.pallas_call(
        body,
        out_shape=outs,
        in_specs=[smem] * scalars + [VMEM] * (len(args) - scalars),
        out_specs=[VMEM] * len(outs) if many else VMEM,
        compiler_params=params(mib),
        **kw,
    )(*args)


def exchange(v, axes):
    sizes = [SIZES[a] for a in axes]
    spots = list(itertools.product(*[range(s) for s in sizes]))
    flat = {p: i for i, p in enumerate(spots)}
    total = v
    for off in spots[1:]:
        perm = [
            (flat[p], flat[tuple((i + o) % s for i, o, s in zip(p, off, sizes))]) for p in spots
        ]
        total = total + lax.ppermute(v, axes, perm)
    return total


def per_device(
    pool_features, pool_targets, batch_index, centers, weights,
    eig_vectors, eig_scale, nys_owner, nys_offset,
):
    rows, dim = batch_index.shape[0], pool_features.shape[1]
    peers = SIZES["x"] * SIZES["y"] * SIZES["zl"]
    cdev, out = weights.shape
    count, q = eig_vectors.shape
    half = rows // 2
    norm = 1.0 / math.sqrt(rows * peers * SIZES["zh"] * SIZES["core"])
    swap = [(0, 1), (1, 0)]
    core = lax.axis_index("core").astype(jnp.int32)[None]
    index = batch_index.reshape(1, rows)
    nys = (nys_owner.reshape(count) * cdev + nys_offset).reshape(1, count)

    send, scale = call(
        features_body,
        [shape(peers, rows, dim), shape(half, 2 * out)],
        pool_features, index,
    )
    recv = lax.all_to_all(send, CENTERS, split_axis=0, concat_axis=0, tiled=True)

    mate_eig = lax.ppermute(eig_vectors, "core", swap)
    mate_nys = lax.ppermute(nys, "core", swap)
    piece = 2 * CAP * (q // 256 + 1)
    points, targ = call(
        functools.partial(vectors_body, cdev=cdev),
        [shape(peers, piece, 128), shape(half, 2 * out)],
        core, pool_targets.T, index, eig_vectors, mate_eig, nys, mate_nys,
        scalars=1,
    )
    points, recv = lax.optimization_barrier((points, recv))
    near = lax.all_to_all(points, CENTERS, split_axis=0, concat_axis=0, tiled=True)

    block = 4 * rows
    kern, pred = call(
        functools.partial(kernel_body, block=block, sub=32),
        [shape(peers * rows, 2 * cdev, dtype=BF), shape(peers, half, 2 * out)],
        recv, centers, weights.T,
        scratch_shapes=[
            pltpu.VMEM((cdev, 6 * dim), BF),
            pltpu.VMEM((2 * cdev, 2 * out), BF),
            pltpu.VMEM((block, cdev), F32),
            pltpu.VMEM((block, cdev), F32),
            pltpu.VMEM((block, 6 * dim), BF),
        ],
        cost_estimate=pl.CostEstimate(
            flops=40_000_000_000, bytes_accessed=1 << 22, transcendentals=0
        ),
    )

    near, pred = lax.optimization_barrier((near, pred))
    far = lax.ppermute(near, "zh", swap)
    parts = lax.all_to_all(pred, CENTERS, split_axis=0, concat_axis=0, tiled=True)
    resid, ready = call(
        functools.partial(residual_body, norm=norm),
        [shape(rows, out), shape(peers, half, 2 * out)],
        parts, targ, scale,
    )
    every = lax.all_to_all(ready, CENTERS, split_axis=0, concat_axis=0, tiled=True)
    grads = call(grads_body, shape(out, cdev), every, kern, centers)
    grads = exchange(grads, ("core",))
    coeff = call(coeff_body, shape(out, q // 2), near, far, grads)
    coeff = exchange(coeff, ("x",))
    coeff = exchange(coeff, ("y",))
    coeff = exchange(coeff, ("zh", "zl"))
    corr = call(
        corr_body, shape(out, cdev), core, near, far, coeff, eig_scale[None, :], scalars=1
    )
    update = exchange(corr, ("core",)) - exchange(grads, ("zh",))
    return resid, update.T


def solution(mesh):
    fine = Mesh(mesh.devices.reshape(tuple(SIZES[a] for a in ALL)), ALL)
    placed = (
        P(ALL, None),
        P(ALL, None),
        P(ALL),
        P(CENTERS, None),
        P(CENTERS, None),
        P(ALL, None),
        P(),
        P(ALL, None),
        P(ALL),
    )
    return jax.shard_map(
        per_device,
        mesh=fine,
        in_specs=placed,
        out_specs=(P(ALL, None), P(CENTERS, None)),
        check_vma=False,
    )
```

```python
import functools
import itertools
import math

import jax
import jax.numpy as jnp
from jax import lax
from jax.experimental import pallas as pl
from jax.experimental.pallas import tpu as pltpu
from jax.sharding import Mesh, PartitionSpec as P

EPS = 1e-06
CAP = 8
BF = jnp.bfloat16
F32 = jnp.float32
SIZES = {"zh": 2, "core": 2, "x": 4, "y": 4, "zl": 2}
ALL = ("zh", "core", "x", "y", "zl")
CENTERS = ("x", "y", "zl")
GROUP = ("zh", "core")
VMEM = pl.BlockSpec(memory_space=pltpu.VMEM)

ACOS_FULL = (
    0.4999999701976776, -0.31830424070358276, 0.24984024465084076, -0.210431307554245,
    0.17730562388896942, -0.13514360785484314, 0.0806083083152771, -0.031184406951069832,
    0.005619336850941181,
)
ACOS_HIGH = (
    0.4999392330646515, -0.3173876106739044, 0.24387668073177338, -0.18864932656288147,
    0.12859871983528137, -0.06701970100402832, 0.02248113788664341, -0.003529248759150505,
)

NN = (((1,), (0,)), ((), ()))
NT = (((1,), (1,)), ((), ()))


def mm(a, b, dims):
    return lax.dot_general(a, b, dims, preferred_element_type=F32)


def split2(x):
    hi = x.astype(BF)
    return hi, (x - hi.astype(F32)).astype(BF)


def split3(x):
    hi = x.astype(BF)
    rest = x - hi.astype(F32)
    mid = rest.astype(BF)
    return hi, mid, (rest - mid.astype(F32)).astype(BF)


def pick(onehot, x, dims, flip=False):
    parts = split3(x)
    prods = [mm(p, onehot, dims) if flip else mm(onehot, p, dims) for p in parts]
    return prods[0] + prods[1] + prods[2]


def full_nt(a, b):
    a1, a2, a3 = split3(a)
    b1, b2, b3 = split3(b)
    return (
        mm(a1, b1, NT) + (mm(a1, b2, NT) + mm(a2, b1, NT))
        + (mm(a2, b2, NT) + mm(a1, b3, NT) + mm(a3, b1, NT))
    )


def horner(coefs, x):
    acc = coefs[-1] * x + coefs[-2]
    for c in coefs[-3::-1]:
        acc = acc * x + c
    return acc


def ntk_over_scale(c):
    inv_pi = 1.0 / math.pi
    ntk = c
    for layer in range(3):
        w = jnp.maximum(1.0 - c * c, 1e-30)
        root = w * lax.rsqrt(w)
        arg = jnp.abs(c) if layer == 0 else c
        angle = root * horner(ACOS_HIGH if layer == 2 else ACOS_FULL, arg)
        remain = jnp.where(c < 0.0, angle, 1.0 - angle) if layer == 0 else 1.0 - angle
        if layer == 2:
            return root * inv_pi + remain * (c + ntk)
        c = root * inv_pi + remain * c
        ntk = c + ntk * remain


def rows_hot(index, width):
    n = index.shape[1]
    col = jnp.broadcast_to(index.astype(F32), (128, n)).T
    lane = lax.broadcasted_iota(jnp.int32, (n, 128), 1).astype(F32)
    return jnp.concatenate(
        [(col == lane + float(128 * k)).astype(BF) for k in range(width // 128)], axis=1
    )


def features_body(pool_f, index, send, scale):
    rows = index.shape[1]
    feats = pick(rows_hot(index[...], pool_f.shape[0]), pool_f[...], NN)
    sa = jnp.sqrt(jnp.mean(feats * feats, axis=1, keepdims=True) + EPS)
    unit = feats / sa
    half, wide = scale.shape
    sa = jnp.broadcast_to(sa, (rows, wide // 2))
    scale[...] = jnp.concatenate([sa[:half], sa[half:]], axis=1)
    for o in range(send.shape[0]):
        send[o] = unit


def quarters_body(member, eig, nys, *outs):
    count, q = eig.shape
    part = q // len(outs)
    row = jnp.broadcast_to(nys[...].astype(F32), (8, count))
    row = jnp.concatenate([row] * (part // count), axis=1)
    for o, out in enumerate(outs):
        mate = member[0] ^ o
        out[0:count, :] = eig[:, pl.ds(pl.multiple_of(mate * part, part), part)]
        out[count:, :] = row


def vectors_body(pool_t, index, *refs, cdev):
    tables, (send, targ) = refs[:-2], refs[-2:]
    hot = rows_hot(index[...], pool_t.shape[1])
    targets = pick(hot, pool_t[...], NT, flip=True).T
    half = targets.shape[0] // 2
    targ[...] = jnp.concatenate([targets[:half], targets[half:]], axis=1)
    count, part = tables[0].shape[0] - 8, tables[0].shape[1]
    peers = send.shape[0]
    blocks, group, lanes = part // 128, CAP * len(tables), 128 // len(tables)
    earlier = lax.broadcasted_iota(jnp.int32, (count, count), 0) < lax.broadcasted_iota(
        jnp.int32, (count, count), 1
    )
    shared = []
    for t, table in enumerate(tables):
        nys = table[count : count + 1, 0:count].astype(jnp.int32)
        owner = nys // cdev
        offset = nys - owner * cdev
        row = jnp.broadcast_to(owner.astype(F32), (count, count))
        same = jnp.where(row.T == row, 1.0, 0.0)
        rank = jnp.sum(jnp.where(earlier, same, 0.0), axis=0, keepdims=True).astype(jnp.int32)
        place = owner * CAP + rank == lax.broadcasted_iota(jnp.int32, (peers * CAP, count), 0)
        offs = jnp.sum(jnp.where(place, offset.astype(F32), 0.0), axis=1, keepdims=True)
        shared.append(jnp.broadcast_to(offs, (peers * CAP, lanes)))
        vectors = pick(place.astype(BF), table[0:count, :], NN)
        for o in range(peers):
            own = slice(o * CAP, (o + 1) * CAP)
            for j in range(blocks):
                at = group * j + CAP * t
                send[o, at : at + CAP, :] = vectors[own, 128 * j : 128 * (j + 1)]
    shared = jnp.concatenate(shared, axis=1)
    for o in range(peers):
        send[o, group * blocks :, :] = shared[o * CAP : (o + 1) * CAP]


def kernel_body(recv, centers, weights, khi, klo, pred, cen, wts, cos_a, cos_b, lhs, *, block, sub):
    src, rows, dim = recv.shape
    out, count = weights.shape
    b = centers[...]
    sb = jnp.sqrt(jnp.mean(b * b, axis=1, keepdims=True) + EPS)
    b1, b2, b3 = split3(b / sb * (1.0 / dim))
    cen[...] = jnp.concatenate([b1, b1, b2, b2, b3, b1], axis=1)
    w1, w2 = split2(weights[...].T * sb)
    w = jnp.concatenate([w1, w2], axis=1)
    wts[...] = w
    blocks, group = src * rows // block, block // rows

    def stage(i):
        a1, a2, a3 = split3(recv[pl.ds(i * group, group)].reshape(block, dim))
        lhs[...] = jnp.concatenate([a1, a2, a1, a2, a1, a3], axis=1)

    def cosines(dst, n):
        at = slice(n * (count // 2), (n + 1) * (count // 2))
        dst[:, at] = mm(lhs[...], cen[at, :], NT)

    def elementwise(i, values, n):
        at = pl.ds(pl.multiple_of(i * block + n * sub, sub), sub)
        hi, lo = split2(ntk_over_scale(values[n * sub : (n + 1) * sub, :]))
        khi[at, :] = hi
        klo[at, :] = lo

    def predict(i):
        at = pl.ds(pl.multiple_of(i * block, block), block)
        both = mm(khi[at, :], wts[...], NN) + mm(klo[at, :], wts[...], NN)
        total = (both[:, :out] + both[:, out:]).reshape(group, 2, rows // 2, out)
        pred[pl.ds(i * group, group)] = jnp.concatenate([total[:, 0], total[:, 1]], axis=2)

    def step(i, before, now, later):
        elems = [functools.partial(elementwise, i, now, n) for n in range(block // sub)]
        others = [
            functools.partial(cosines, later, 0),
            functools.partial(cosines, later, 1),
            functools.partial(predict, before),
        ]
        stage(jnp.minimum(i + 1, blocks - 1))
        every = len(elems) // len(others)
        for n, f in enumerate(elems):
            if n % every == 0 and others:
                others.pop(0)()
            f()

    stage(0)
    cosines(cos_a, 0)
    cosines(cos_a, 1)

    def pair(h, _):
        step(2 * h, jnp.maximum(2 * h - 1, 0), cos_a, cos_b)
        step(2 * h + 1, 2 * h, cos_b, cos_a)
        return 0

    lax.fori_loop(0, blocks // 2, pair, 0)
    predict(blocks - 1)


def residual_body(parts, targ, scale, resid, send, *, norm):
    value = scale[...] * jnp.sum(parts[...], axis=0) - targ[...]
    half, out = value.shape[0], value.shape[1] // 2
    resid[0:half, :] = value[:, :out]
    resid[half:, :] = value[:, out:]
    ready = value * scale[...] * norm
    for o in range(send.shape[0]):
        send[o] = ready


def grads_body(resid, khi, klo, centers, grads):
    src, half, wide = resid.shape
    out = grads.shape[0]
    r = resid[...]
    r = jnp.concatenate([r[:, :, :out], r[:, :, out:]], axis=1).reshape(src * half * 2, out)
    r1, r2 = split2(r.T)
    rr = jnp.concatenate([r1, r2], axis=0)
    both = mm(rr, khi[...], NN) + mm(rr, klo[...], NN)
    b = centers[...]
    nb = full_nt(jnp.ones((8, b.shape[1]), F32), b * b)[0:1] * (1.0 / b.shape[1]) + EPS
    grads[...] = (both[:out] + both[out:]) * jnp.sqrt(nb)


def block_of(points, j, tables):
    peers, group = points.shape[0], CAP * tables
    return points[:, group * j : group * (j + 1), :].reshape(peers * group, 128)


def points_hot(points, blocks, tables, width):
    peers, lanes = points.shape[0], 128 // tables
    offs = points[:, CAP * tables * blocks :, :]
    offs = jnp.concatenate(
        [
            jnp.broadcast_to(offs[:, :, lanes * t : lanes * t + 1], (peers, CAP, 128))
            for t in range(tables)
        ],
        axis=1,
    ).reshape(peers * CAP * tables, 128)
    lane = lax.broadcasted_iota(jnp.int32, offs.shape, 1).astype(F32)
    return jnp.concatenate(
        [(offs == lane + float(128 * k)).astype(BF) for k in range(width // 128)], axis=1
    )


def coeff_body(points, grads, coeff, *, tables):
    out, part = coeff.shape
    blocks = part // 128
    hot = points_hot(points, blocks, tables, grads.shape[1])
    g1, g2 = split2(pick(hot, grads[...], NT, flip=True))
    gg = jnp.concatenate([g1, g2], axis=0)
    for j in range(blocks):
        e1, e2 = split2(block_of(points, j, tables))
        both = mm(gg, e1, NN) + mm(gg, e2, NN)
        coeff[:, 128 * j : 128 * (j + 1)] = both[:out] + both[out:]


def corr_body(member, points, coeff, eig_scale, corr, *, tables):
    out, part = coeff.shape
    blocks = part // 128
    hot = points_hot(points, blocks, tables, corr.shape[1])
    total = jnp.zeros((2 * out, hot.shape[0]), F32)
    for j in range(blocks):
        at = slice(128 * j, 128 * (j + 1))
        e1, e2 = split2(block_of(points, j, tables))
        scale = eig_scale[:, pl.ds(pl.multiple_of(member[0] * part + 128 * j, 128), 128)]
        c1, c2 = split2(coeff[:, at] * scale)
        cc = jnp.concatenate([c1, c2], axis=0)
        total = total + mm(cc, e1, NT) + mm(cc, e2, NT)
    corr[...] = pick(hot, total[:out] + total[out:], NN, flip=True)


def shape(*dims, dtype=F32):
    return jax.ShapeDtypeStruct(dims, dtype)


def params(mib=16):
    return pltpu.CompilerParams(vmem_limit_bytes=mib << 20)


def call(body, outs, *args, mib=16, scalars=0, **kw):
    many = isinstance(outs, (list, tuple))
    smem = pl.BlockSpec(memory_space=pltpu.SMEM)
    return pl.pallas_call(
        body,
        out_shape=outs,
        in_specs=[smem] * scalars + [VMEM] * (len(args) - scalars),
        out_specs=[VMEM] * len(outs) if many else VMEM,
        compiler_params=params(mib),
        **kw,
    )(*args)


def exchange(v, axes):
    sizes = [SIZES[a] for a in axes]
    spots = list(itertools.product(*[range(s) for s in sizes]))
    flat = {p: i for i, p in enumerate(spots)}
    total = v
    for off in spots[1:]:
        perm = [
            (flat[p], flat[tuple((i + o) % s for i, o, s in zip(p, off, sizes))]) for p in spots
        ]
        total = total + lax.ppermute(v, axes, perm)
    return total


def per_device(
    pool_features, pool_targets, batch_index, centers, weights,
    eig_vectors, eig_scale, nys_owner, nys_offset,
):
    rows, dim = batch_index.shape[0], pool_features.shape[1]
    peers = SIZES["x"] * SIZES["y"] * SIZES["zl"]
    cdev, out = weights.shape
    count, q = eig_vectors.shape
    half = rows // 2
    norm = 1.0 / math.sqrt(rows * peers * SIZES["zh"] * SIZES["core"])
    index = batch_index.reshape(1, rows)
    nys = (nys_owner.reshape(count) * cdev + nys_offset).reshape(1, count)
    tables = SIZES[GROUP[0]] * SIZES[GROUP[1]]
    member = lax.axis_index(GROUP).astype(jnp.int32)[None]

    send, scale = call(
        features_body,
        [shape(peers, rows, dim), shape(half, 2 * out)],
        pool_features, index,
    )
    recv = lax.all_to_all(send, CENTERS, split_axis=0, concat_axis=0, tiled=True)

    parted = call(
        quarters_body, [shape(count + 8, q // tables)] * tables,
        member, eig_vectors, nys, scalars=1,
    )
    parted = [parted[0]] + [
        lax.ppermute(part, GROUP, [(i, i ^ o) for i in range(tables)])
        for o, part in enumerate(parted) if o
    ]
    piece = CAP * (tables * (q // tables // 128) + 1)
    points, targ = call(
        functools.partial(vectors_body, cdev=cdev),
        [shape(peers, piece, 128), shape(half, 2 * out)],
        pool_targets.T, index, *parted,
    )
    points, recv = lax.optimization_barrier((points, recv))
    points = lax.all_to_all(points, CENTERS, split_axis=0, concat_axis=0, tiled=True)

    block = 4 * rows
    khi, klo, pred = call(
        functools.partial(kernel_body, block=block, sub=32),
        [shape(peers * rows, cdev, dtype=BF)] * 2 + [shape(peers, half, 2 * out)],
        recv, centers, weights.T,
        scratch_shapes=[
            pltpu.VMEM((cdev, 6 * dim), BF),
            pltpu.VMEM((cdev, 2 * out), BF),
            pltpu.VMEM((block, cdev), F32),
            pltpu.VMEM((block, cdev), F32),
            pltpu.VMEM((block, 6 * dim), BF),
        ],
        cost_estimate=pl.CostEstimate(
            flops=40_000_000_000, bytes_accessed=1 << 22, transcendentals=0
        ),
    )

    points, pred = lax.optimization_barrier((points, pred))
    parts = lax.all_to_all(pred, CENTERS, split_axis=0, concat_axis=0, tiled=True)
    resid, ready = call(
        functools.partial(residual_body, norm=norm),
        [shape(rows, out), shape(peers, half, 2 * out)],
        parts, targ, scale,
    )
    every = lax.all_to_all(ready, CENTERS, split_axis=0, concat_axis=0, tiled=True)
    grads = call(grads_body, shape(out, cdev), every, khi, klo, centers)
    for axis in GROUP[::-1]:
        grads = exchange(grads, (axis,))
    coeff = call(
        functools.partial(coeff_body, tables=tables), shape(out, q // tables), points, grads
    )
    for axis in CENTERS:
        coeff = exchange(coeff, (axis,))
    corr = call(
        functools.partial(corr_body, tables=tables),
        shape(out, cdev), member, points, coeff, eig_scale[None, :],
        scalars=1,
    )
    for axis in GROUP[::-1]:
        corr = exchange(corr, (axis,))
    return resid, (corr - grads).T


def solution(mesh):
    fine = Mesh(mesh.devices.reshape(tuple(SIZES[a] for a in ALL)), ALL)
    placed = (
        P(ALL, None),
        P(ALL, None),
        P(ALL),
        P(CENTERS, None),
        P(CENTERS, None),
        P(ALL, None),
        P(),
        P(ALL, None),
        P(ALL),
    )
    return jax.shard_map(
        per_device,
        mesh=fine,
        in_specs=placed,
        out_specs=(P(ALL, None), P(CENTERS, None)),
        check_vma=False,
    )
```

```python
import functools
import math

import jax
import jax.numpy as jnp
from jax import lax
from jax.experimental import pallas as pl
from jax.experimental.pallas import tpu as pltpu
from jax.sharding import Mesh, PartitionSpec as P

EPS = 1e-06
CAP = 8
BF = jnp.bfloat16
F32 = jnp.float32
SIZES = {"zh": 2, "core": 2, "x": 4, "y": 4, "zl": 2}
ALL = ("zh", "core", "x", "y", "zl")
CENTERS = ("x", "y", "zl")
PLANES = ("zh", "zl")
OWNERS = ("x", "y", "core")
VMEM = pl.BlockSpec(memory_space=pltpu.VMEM)

ACOS_FULL = (
    0.4999999701976776, -0.31830424070358276, 0.24984024465084076, -0.210431307554245,
    0.17730562388896942, -0.13514360785484314, 0.0806083083152771, -0.031184406951069832,
    0.005619336850941181,
)
ACOS_HIGH = (
    0.4999392330646515, -0.3173876106739044, 0.24387668073177338, -0.18864932656288147,
    0.12859871983528137, -0.06701970100402832, 0.02248113788664341, -0.003529248759150505,
)

NN = (((1,), (0,)), ((), ()))
NT = (((1,), (1,)), ((), ()))


def mm(a, b, dims):
    return lax.dot_general(a, b, dims, preferred_element_type=F32)


def split2(x):
    hi = x.astype(BF)
    return hi, (x - hi.astype(F32)).astype(BF)


def split3(x):
    hi = x.astype(BF)
    rest = x - hi.astype(F32)
    mid = rest.astype(BF)
    return hi, mid, (rest - mid.astype(F32)).astype(BF)


def pick(onehot, x, dims, flip=False):
    parts = split3(x)
    prods = [mm(p, onehot, dims) if flip else mm(onehot, p, dims) for p in parts]
    return prods[0] + prods[1] + prods[2]


def full_nt(a, b):
    a1, a2, a3 = split3(a)
    b1, b2, b3 = split3(b)
    return (
        mm(a1, b1, NT) + (mm(a1, b2, NT) + mm(a2, b1, NT))
        + (mm(a2, b2, NT) + mm(a1, b3, NT) + mm(a3, b1, NT))
    )


def horner(coefs, x):
    acc = coefs[-1] * x + coefs[-2]
    for c in coefs[-3::-1]:
        acc = acc * x + c
    return acc


def ntk_over_scale(c):
    inv_pi = 1.0 / math.pi
    ntk = c
    for layer in range(3):
        w = jnp.maximum(1.0 - c * c, 1e-30)
        root = w * lax.rsqrt(w)
        arg = jnp.abs(c) if layer == 0 else c
        angle = root * horner(ACOS_HIGH if layer == 2 else ACOS_FULL, arg)
        remain = jnp.where(c < 0.0, angle, 1.0 - angle) if layer == 0 else 1.0 - angle
        if layer == 2:
            return root * inv_pi + remain * (c + ntk)
        c = root * inv_pi + remain * c
        ntk = c + ntk * remain


def rows_hot(index, width):
    n = index.shape[1]
    col = jnp.broadcast_to(index.astype(F32), (128, n)).T
    lane = lax.broadcasted_iota(jnp.int32, (n, 128), 1).astype(F32)
    return jnp.concatenate(
        [(col == lane + float(128 * k)).astype(BF) for k in range(width // 128)], axis=1
    )


def packed(x):
    half = x.shape[0] // 2
    return jnp.concatenate([x[:half], x[half:]], axis=1)


def unpacked(x):
    wide = x.shape[-1] // 2
    return jnp.concatenate([x[..., :wide], x[..., wide:]], axis=-2)


def features_body(pool_f, pool_t, index, drawn):
    rows = index.shape[1]
    hot = rows_hot(index[...], pool_f.shape[0])
    drawn[0:rows, :] = pick(hot, pool_f[...], NN)
    drawn[rows:, :] = packed(pick(hot, pool_t[...], NT, flip=True).T)


def centers_body(centers, weights, pack):
    count = centers.shape[0]
    pack[0:count, :] = centers[...]
    pack[count:, :] = packed(weights[...].T)


def order_body(x, *refs):
    parts, out = refs[:-1], refs[-1]
    for o, part in enumerate(parts):
        out[x[0] ^ o] = part[...]


def quarters_body(member, eig, nys, *outs):
    count, q = eig.shape
    part = q // len(outs)
    row = jnp.broadcast_to(nys[...].astype(F32), (8, count))
    row = jnp.concatenate([row] * (part // count), axis=1)
    for o, out in enumerate(outs):
        mate = member[0] ^ o
        out[0:count, :] = eig[:, pl.ds(pl.multiple_of(mate * part, part), part)]
        out[count:, :] = row


def vectors_body(*refs, cdev):
    tables, send = refs[:-1], refs[-1]
    count, part = tables[0].shape[0] - 8, tables[0].shape[1]
    peers = send.shape[0]
    blocks, group, lanes = part // 128, CAP * len(tables), 128 // len(tables)
    earlier = lax.broadcasted_iota(jnp.int32, (count, count), 0) < lax.broadcasted_iota(
        jnp.int32, (count, count), 1
    )
    shared = []
    for t, table in enumerate(tables):
        nys = table[count : count + 1, 0:count].astype(jnp.int32)
        owner = nys // cdev
        offset = nys - owner * cdev
        row = jnp.broadcast_to(owner.astype(F32), (count, count))
        same = jnp.where(row.T == row, 1.0, 0.0)
        rank = jnp.sum(jnp.where(earlier, same, 0.0), axis=0, keepdims=True).astype(jnp.int32)
        place = owner * CAP + rank == lax.broadcasted_iota(jnp.int32, (peers * CAP, count), 0)
        offs = jnp.sum(jnp.where(place, offset.astype(F32), 0.0), axis=1, keepdims=True)
        shared.append(jnp.broadcast_to(offs, (peers * CAP, lanes)))
        vectors = pick(place.astype(BF), table[0:count, :], NN)
        for o in range(peers):
            own = slice(o * CAP, (o + 1) * CAP)
            for j in range(blocks):
                at = group * j + CAP * t
                send[o, at : at + CAP, :] = vectors[own, 128 * j : 128 * (j + 1)]
    shared = jnp.concatenate(shared, axis=1)
    for o in range(peers):
        send[o, group * blocks :, :] = shared[o * CAP : (o + 1) * CAP]


def kernel_body(*refs, nb, rows, sub, extra):
    own, mate = refs[0:2]
    packs = refs[2 : 2 + nb]
    khi, klo, keep, send = refs[2 + nb : 6 + nb]
    lhs, cen, wts, cos_a, cos_b, acc = refs[-6:]
    dim, count = own.shape[2], khi.shape[2]
    block = own.shape[0] * rows
    out = dim // 2
    for h, part in enumerate((own, mate)):
        f = part[:, 0:rows, :].reshape(block, dim)
        sa = jnp.sqrt(jnp.mean(f * f, axis=1, keepdims=True) + EPS)
        a1, a2, a3 = split3(f / sa)
        lhs[h] = jnp.concatenate([a1, a2, a1, a2, a1, a3], axis=1)
        if extra and h == 0:
            wide = jnp.broadcast_to(sa, (block, out)).reshape(own.shape[0], rows, out)
            half = rows // 2
            refs[6 + nb][...] = jnp.concatenate([wide[:, :half], wide[:, half:]], axis=2)
    for j, pack in enumerate(packs):
        b = pack[0:count, :]
        sb = jnp.sqrt(jnp.mean(b * b, axis=1, keepdims=True) + EPS)
        b1, b2, b3 = split3(b / sb * (1.0 / dim))
        cen[j] = jnp.concatenate([b1, b1, b2, b2, b3, b1], axis=1)
        w1, w2 = split2(unpacked(pack[count:, :]) * sb)
        wts[j] = jnp.concatenate([w1, w2], axis=1)
        if extra:
            nb_row = full_nt(jnp.ones((8, dim), F32), b * b) * (1.0 / dim) + EPS
            refs[7 + nb][...] = jnp.sqrt(nb_row)
    acc[...] = jnp.zeros(acc.shape, F32)

    def cosines(dst, j, h, n):
        at = slice(n * (count // 2), (n + 1) * (count // 2))
        dst[:, at] = mm(lhs[h], cen[j, at, :], NT)

    def elementwise(values, j, h, n):
        at = slice(h * block + n * sub, h * block + (n + 1) * sub)
        hi, lo = split2(ntk_over_scale(values[n * sub : (n + 1) * sub, :]))
        khi[j, at, :] = hi
        klo[j, at, :] = lo

    def predict(j, h):
        at = slice(h * block, (h + 1) * block)
        both = mm(khi[j, at, :], wts[j], NN) + mm(klo[j, at, :], wts[j], NN)
        acc[at, :] = acc[at, :] + both

    def step(j, h, now, later, after):
        elems = [functools.partial(elementwise, now, j, h, n) for n in range(block // sub)]
        others = [functools.partial(cosines, later, *after, n) for n in range(2)] if after else []
        if h == 1:
            others.append(functools.partial(predict, j, 0))
        every = len(elems) // 3
        for n, f in enumerate(elems):
            if n % every == 0 and others:
                others.pop(0)()
            f()

    for n in range(2):
        cosines(cos_a, 0, 0, n)
    if nb == 1:
        step(0, 0, cos_a, cos_b, (0, 1))
        step(0, 1, cos_b, cos_a, None)
        predict(0, 1)
    else:

        def pair(j, _):
            step(j, 0, cos_a, cos_b, (j, 1))
            step(j, 1, cos_b, cos_a, (jnp.minimum(j + 1, nb - 1), 0))
            predict(j, 1)
            return 0

        lax.fori_loop(0, nb, pair, 0)
    for h, dst in enumerate((keep, send)):
        total = acc[h * block : (h + 1) * block, :]
        total = (total[:, :out] + total[:, out:]).reshape(own.shape[0], 2, rows // 2, out)
        dst[...] = jnp.concatenate([total[:, 0], total[:, 1]], axis=2)


def residual_body(x, total, own, scale, resid, ready, value, *, rows, norm):
    value[...] = scale[...] * total[...] - own[:, rows:, :]
    resid[...] = unpacked(value[x[0]])
    ready[...] = value[...] * scale[...] * norm


def grads_body(own, mate, *refs):
    outs = refs[-4:]
    r = jnp.concatenate([unpacked(own[...]), unpacked(mate[...])], axis=0)
    out = r.shape[2]
    r1, r2 = split2(r.reshape(-1, out).T)
    rr = jnp.concatenate([r1, r2], axis=0)
    place = 0
    for khi, klo in zip(refs[0:-4:2], refs[1:-4:2]):
        for j in range(khi.shape[0]):
            both = mm(rr, khi[j], NN) + mm(rr, klo[j], NN)
            outs[place][...] = both[:out] + both[out:]
            place += 1


def block_of(points, j, tables):
    peers, group = points.shape[0], CAP * tables
    return points[:, group * j : group * (j + 1), :].reshape(peers * group, 128)


def points_hot(points, blocks, tables, width):
    peers, lanes = points.shape[0], 128 // tables
    offs = points[:, CAP * tables * blocks :, :]
    offs = jnp.concatenate(
        [
            jnp.broadcast_to(offs[:, :, lanes * t : lanes * t + 1], (peers, CAP, 128))
            for t in range(tables)
        ],
        axis=1,
    ).reshape(peers * CAP * tables, 128)
    lane = lax.broadcasted_iota(jnp.int32, offs.shape, 1).astype(F32)
    return jnp.concatenate(
        [(offs == lane + float(128 * k)).astype(BF) for k in range(width // 128)], axis=1
    )


def coeff_body(points, grads, coeff, *, tables):
    out, part = coeff.shape
    blocks = part // 128
    hot = points_hot(points, blocks, tables, grads.shape[1])
    g1, g2 = split2(pick(hot, grads[...], NT, flip=True))
    gg = jnp.concatenate([g1, g2], axis=0)
    for j in range(blocks):
        e1, e2 = split2(block_of(points, j, tables))
        both = mm(gg, e1, NN) + mm(gg, e2, NN)
        coeff[:, 128 * j : 128 * (j + 1)] = both[:out] + both[out:]


def corr_body(member, points, coeff, eig_scale, corr, *, tables):
    out, part = coeff.shape
    blocks = part // 128
    hot = points_hot(points, blocks, tables, corr.shape[1])
    total = jnp.zeros((2 * out, hot.shape[0]), F32)
    for j in range(blocks):
        at = slice(128 * j, 128 * (j + 1))
        e1, e2 = split2(block_of(points, j, tables))
        scale = eig_scale[:, pl.ds(pl.multiple_of(member[0] * part + 128 * j, 128), 128)]
        c1, c2 = split2(coeff[:, at] * scale)
        cc = jnp.concatenate([c1, c2], axis=0)
        total = total + mm(cc, e1, NT) + mm(cc, e2, NT)
    corr[...] = pick(hot, total[:out] + total[out:], NN, flip=True)


def shape(*dims, dtype=F32):
    return jax.ShapeDtypeStruct(dims, dtype)


def params(mib=16):
    return pltpu.CompilerParams(vmem_limit_bytes=mib << 20)


def call(body, outs, *args, mib=16, scalars=0, **kw):
    many = isinstance(outs, (list, tuple))
    smem = pl.BlockSpec(memory_space=pltpu.SMEM)
    return pl.pallas_call(
        body,
        out_shape=outs,
        in_specs=[smem] * scalars + [VMEM] * (len(args) - scalars),
        out_specs=[VMEM] * len(outs) if many else VMEM,
        compiler_params=params(mib),
        **kw,
    )(*args)


def exchange(v, axes):
    return functools.reduce(jnp.add, [v] + mates([v] * math.prod(SIZES[a] for a in axes), axes))


def mates(parts, axes):
    n = math.prod(SIZES[a] for a in axes)
    return [
        lax.ppermute(parts[o], axes, [(i, i ^ o) for i in range(n)]) for o in range(1, n)
    ]


def together(*arrays):
    return lax.optimization_barrier(arrays)


def per_device(
    pool_features, pool_targets, batch_index, centers, weights,
    eig_vectors, eig_scale, nys_owner, nys_offset,
):
    rows, dim = batch_index.shape[0], pool_features.shape[1]
    nx, ny, half = SIZES["x"], SIZES["y"], rows // 2
    cdev, out = weights.shape
    count, q = eig_vectors.shape
    tables = math.prod(SIZES[a] for a in PLANES)
    peers = math.prod(SIZES[a] for a in OWNERS)
    norm = 1.0 / math.sqrt(rows * math.prod(SIZES[a] for a in ALL))
    x = lax.axis_index("x").astype(jnp.int32)[None]
    member = lax.axis_index(PLANES).astype(jnp.int32)[None]
    straight = lax.axis_index("core") == lax.axis_index("zl")
    wide = 2 * out

    pack = call(centers_body, shape(cdev + cdev // 2, dim), centers, weights.T)
    moved = lax.ppermute(pack, ("core", "zl"), [(0, 1), (3, 2)])
    tile = jnp.where(straight, pack, moved)

    drawn = call(
        features_body, shape(rows + half, dim),
        pool_features, pool_targets.T, batch_index.reshape(1, rows),
    )
    tile, *gathered = together(tile, drawn, *mates([drawn] * nx, ("x",)))
    own = call(order_body, shape(nx, rows + half, dim), x, *gathered, scalars=1)
    others = mates([tile] * ny, ("y",))
    (mate,) = mates([own] * 2, ("core",))
    eig_vectors, own = together(eig_vectors, own)

    def kernel(packs, extra):
        nb = len(packs)
        outs = [shape(nb, 2 * nx * rows, cdev, dtype=BF)] * 2 + [shape(nx, half, wide)] * 2
        if extra:
            outs = outs + [shape(nx, half, wide), shape(8, cdev)]
        return call(
            functools.partial(kernel_body, nb=nb, rows=rows, sub=32, extra=extra),
            outs, own, mate, *packs,
            scratch_shapes=[
                pltpu.VMEM((2, nx * rows, 6 * dim), BF),
                pltpu.VMEM((nb, cdev, 6 * dim), BF),
                pltpu.VMEM((nb, cdev, wide), BF),
                pltpu.VMEM((nx * rows, cdev), F32),
                pltpu.VMEM((nx * rows, cdev), F32),
                pltpu.VMEM((2 * nx * rows, wide), F32),
            ],
            cost_estimate=pl.CostEstimate(
                flops=10_000_000_000 * nb, bytes_accessed=1 << 20, transcendentals=0
            ),
        )

    khi_a, klo_a, keep_a, send_a, scale, sb = kernel([tile], True)

    nys = (nys_owner.reshape(count) * cdev + nys_offset).reshape(1, count)
    parted = call(
        quarters_body, [shape(count + 8, q // tables)] * tables,
        member, eig_vectors, nys, scalars=1,
    )
    keep_a, *parted = together(keep_a, parted[0], *mates(parted, PLANES))
    points = call(
        functools.partial(vectors_body, cdev=cdev),
        shape(peers, CAP * (tables * (q // tables // 128) + 1), 128),
        *parted,
    )
    points = lax.all_to_all(points, OWNERS, split_axis=0, concat_axis=0, tiled=True)

    khi_b, klo_b, keep_b, send_b = kernel(others, False)

    (got,) = mates([send_a + send_b] * 2, ("core",))
    total = exchange(keep_a + keep_b + got, ("x",))
    resid, ready = call(
        functools.partial(residual_body, rows=rows, norm=norm),
        [shape(rows, out), shape(nx, half, wide)],
        x, total, own, scale,
        scalars=1, scratch_shapes=[pltpu.VMEM((nx, half, wide), F32)],
    )
    (ready_mate,) = mates([ready] * 2, ("core",))

    parts = call(
        grads_body, [shape(out, cdev)] * 4, ready, ready_mate, khi_a, klo_a, khi_b, klo_b
    )
    grads = functools.reduce(jnp.add, mates(parts, ("y",)), parts[0]) * sb[0:1]
    points, grads = together(points, grads)
    grads = exchange(grads, PLANES)
    coeff = call(
        functools.partial(coeff_body, tables=tables), shape(out, q // tables), points, grads
    )
    for axis in OWNERS[::-1]:
        coeff = exchange(coeff, (axis,))
    corr = call(
        functools.partial(corr_body, tables=tables),
        shape(out, cdev), member, points, coeff, eig_scale[None, :],
        scalars=1,
    )
    update = exchange(corr, PLANES) - grads
    (swapped,) = mates([update] * 2, ("core",))
    return resid, jnp.where(straight, update, swapped).T


def solution(mesh):
    fine = Mesh(mesh.devices.reshape(tuple(SIZES[a] for a in ALL)), ALL)
    placed = (
        P(ALL, None),
        P(ALL, None),
        P(ALL),
        P(CENTERS, None),
        P(CENTERS, None),
        P(ALL, None),
        P(),
        P(ALL, None),
        P(ALL),
    )
    return jax.shard_map(
        per_device,
        mesh=fine,
        in_specs=placed,
        out_specs=(P(ALL, None), P(CENTERS, None)),
        check_vma=False,
    )
```

```python
import functools
import math

import jax
import jax.numpy as jnp
from jax import lax
from jax.experimental import pallas as pl
from jax.experimental.pallas import tpu as pltpu
from jax.sharding import Mesh, PartitionSpec as P

EPS = 1e-06
CAP = 8
BF = jnp.bfloat16
F32 = jnp.float32
SIZES = {"zh": 2, "core": 2, "x": 4, "y": 4, "zl": 2}
ALL = ("zh", "core", "x", "y", "zl")
CENTERS = ("x", "y", "zl")
PLANES = ("zh", "zl")
OWNERS = ("x", "y", "core")
VMEM = pl.BlockSpec(memory_space=pltpu.VMEM)

ACOS_FULL = (
    0.4999999701976776, -0.31830424070358276, 0.24984024465084076, -0.210431307554245,
    0.17730562388896942, -0.13514360785484314, 0.0806083083152771, -0.031184406951069832,
    0.005619336850941181,
)
ACOS_HIGH = (
    0.4999392330646515, -0.3173876106739044, 0.24387668073177338, -0.18864932656288147,
    0.12859871983528137, -0.06701970100402832, 0.02248113788664341, -0.003529248759150505,
)

NN = (((1,), (0,)), ((), ()))
NT = (((1,), (1,)), ((), ()))


def mm(a, b, dims):
    return lax.dot_general(a, b, dims, preferred_element_type=F32)


def split2(x):
    hi = x.astype(BF)
    return hi, (x - hi.astype(F32)).astype(BF)


def split3(x):
    hi = x.astype(BF)
    rest = x - hi.astype(F32)
    mid = rest.astype(BF)
    return hi, mid, (rest - mid.astype(F32)).astype(BF)


def pick(onehot, x, dims, flip=False):
    parts = split3(x)
    prods = [mm(p, onehot, dims) if flip else mm(onehot, p, dims) for p in parts]
    return prods[0] + prods[1] + prods[2]


def full_nt(a, b):
    a1, a2, a3 = split3(a)
    b1, b2, b3 = split3(b)
    return (
        mm(a1, b1, NT) + (mm(a1, b2, NT) + mm(a2, b1, NT))
        + (mm(a2, b2, NT) + mm(a1, b3, NT) + mm(a3, b1, NT))
    )


def horner(coefs, x):
    acc = coefs[-1] * x + coefs[-2]
    for c in coefs[-3::-1]:
        acc = acc * x + c
    return acc


def ntk_over_scale(c):
    inv_pi = 1.0 / math.pi
    ntk = c
    for layer in range(3):
        w = jnp.maximum(1.0 - c * c, 1e-30)
        root = w * lax.rsqrt(w)
        arg = jnp.abs(c) if layer == 0 else c
        angle = root * horner(ACOS_HIGH if layer == 2 else ACOS_FULL, arg)
        remain = jnp.where(c < 0.0, angle, 1.0 - angle) if layer == 0 else 1.0 - angle
        if layer == 2:
            return root * inv_pi + remain * (c + ntk)
        c = root * inv_pi + remain * c
        ntk = c + ntk * remain


def rows_hot(index, width):
    n = index.shape[1]
    col = jnp.broadcast_to(index.astype(F32), (128, n)).T
    lane = lax.broadcasted_iota(jnp.int32, (n, 128), 1).astype(F32)
    return jnp.concatenate(
        [(col == lane + float(128 * k)).astype(BF) for k in range(width // 128)], axis=1
    )


def packed(x):
    half = x.shape[0] // 2
    return jnp.concatenate([x[:half], x[half:]], axis=1)


def unpacked(x):
    wide = x.shape[-1] // 2
    return jnp.concatenate([x[..., :wide], x[..., wide:]], axis=-2)


def front_body(index, pool_f, pool_t, centers, weights, drawn, pack, feats, targs, wts, sems):
    count = centers.shape[0]
    copies = [
        pltpu.make_async_copy(src, dst, sems.at[n])
        for n, (src, dst) in enumerate(
            ((pool_f, feats), (pool_t, targs), (weights, wts), (centers, pack.at[0:count, :]))
        )
    ]
    for copy in copies:
        copy.start()
    rows = index.shape[1]
    hot = rows_hot(index[...], feats.shape[0])
    copies[0].wait()
    drawn[0:rows, :] = pick(hot, feats[...], NN)
    copies[1].wait()
    drawn[rows:, :] = packed(pick(hot, targs[...], NT, flip=True).T)
    copies[2].wait()
    pack[count:, :] = packed(wts[...].T)
    copies[3].wait()


def order_body(x, *refs):
    parts, out = refs[:-1], refs[-1]
    for o, part in enumerate(parts):
        out[x[0] ^ o] = part[...]


def quarters_body(member, eig, nys, *outs):
    count, q = eig.shape
    part = q // len(outs)
    row = jnp.broadcast_to(nys[...].astype(F32), (8, count))
    row = jnp.concatenate([row] * (part // count), axis=1)
    for o, out in enumerate(outs):
        mate = member[0] ^ o
        out[0:count, :] = eig[:, pl.ds(pl.multiple_of(mate * part, part), part)]
        out[count:, :] = row


def vectors_body(*refs, cdev):
    tables, send = refs[:-1], refs[-1]
    count, part = tables[0].shape[0] - 8, tables[0].shape[1]
    peers = send.shape[0]
    blocks, group, lanes = part // 128, CAP * len(tables), 128 // len(tables)
    earlier = lax.broadcasted_iota(jnp.int32, (count, count), 0) < lax.broadcasted_iota(
        jnp.int32, (count, count), 1
    )
    shared = []
    for t, table in enumerate(tables):
        nys = table[count : count + 1, 0:count].astype(jnp.int32)
        owner = nys // cdev
        offset = nys - owner * cdev
        row = jnp.broadcast_to(owner.astype(F32), (count, count))
        same = jnp.where(row.T == row, 1.0, 0.0)
        rank = jnp.sum(jnp.where(earlier, same, 0.0), axis=0, keepdims=True).astype(jnp.int32)
        place = owner * CAP + rank == lax.broadcasted_iota(jnp.int32, (peers * CAP, count), 0)
        offs = jnp.sum(jnp.where(place, offset.astype(F32), 0.0), axis=1, keepdims=True)
        shared.append(jnp.broadcast_to(offs, (peers * CAP, lanes)))
        vectors = pick(place.astype(BF), table[0:count, :], NN)
        for o in range(peers):
            own = slice(o * CAP, (o + 1) * CAP)
            for j in range(blocks):
                at = group * j + CAP * t
                send[o, at : at + CAP, :] = vectors[own, 128 * j : 128 * (j + 1)]
    shared = jnp.concatenate(shared, axis=1)
    for o in range(peers):
        send[o, group * blocks :, :] = shared[o * CAP : (o + 1) * CAP]


def kernel_body(*refs, nb, rows, sub, extra):
    own, mate = refs[0:2]
    packs = refs[2 : 2 + nb]
    khi, klo, keep, send = refs[2 + nb : 6 + nb]
    lhs, cen, wts, cos_a, cos_b, acc = refs[-6:]
    dim, count = own.shape[2], khi.shape[2]
    block = own.shape[0] * rows
    out = dim // 2
    for h, part in enumerate((own, mate)):
        f = part[:, 0:rows, :].reshape(block, dim)
        sa = jnp.sqrt(jnp.mean(f * f, axis=1, keepdims=True) + EPS)
        a1, a2, a3 = split3(f / sa)
        lhs[h] = jnp.concatenate([a1, a2, a1, a2, a1, a3], axis=1)
        if extra and h == 0:
            wide = jnp.broadcast_to(sa, (block, out)).reshape(own.shape[0], rows, out)
            half = rows // 2
            refs[6 + nb][...] = jnp.concatenate([wide[:, :half], wide[:, half:]], axis=2)
    for j, pack in enumerate(packs):
        b = pack[0:count, :]
        sb = jnp.sqrt(jnp.mean(b * b, axis=1, keepdims=True) + EPS)
        b1, b2, b3 = split3(b / sb * (1.0 / dim))
        cen[j] = jnp.concatenate([b1, b1, b2, b2, b3, b1], axis=1)
        w1, w2 = split2(unpacked(pack[count:, :]) * sb)
        wts[j] = jnp.concatenate([w1, w2], axis=1)
        if extra:
            nb_row = full_nt(jnp.ones((8, dim), F32), b * b) * (1.0 / dim) + EPS
            refs[7 + nb][...] = jnp.sqrt(nb_row)
    acc[...] = jnp.zeros(acc.shape, F32)

    def cosines(dst, j, h, n):
        at = slice(n * (count // 2), (n + 1) * (count // 2))
        dst[:, at] = mm(lhs[h], cen[j, at, :], NT)

    def elementwise(values, j, h, n):
        at = slice(h * block + n * sub, h * block + (n + 1) * sub)
        hi, lo = split2(ntk_over_scale(values[n * sub : (n + 1) * sub, :]))
        khi[j, at, :] = hi
        klo[j, at, :] = lo

    def predict(j, h):
        at = slice(h * block, (h + 1) * block)
        both = mm(khi[j, at, :], wts[j], NN) + mm(klo[j, at, :], wts[j], NN)
        acc[at, :] = acc[at, :] + both

    def step(j, h, now, later, after):
        elems = [functools.partial(elementwise, now, j, h, n) for n in range(block // sub)]
        others = [functools.partial(cosines, later, *after, n) for n in range(2)] if after else []
        if h == 1:
            others.append(functools.partial(predict, j, 0))
        every = len(elems) // 3
        for n, f in enumerate(elems):
            if n % every == 0 and others:
                others.pop(0)()
            f()

    for n in range(2):
        cosines(cos_a, 0, 0, n)
    if nb == 1:
        step(0, 0, cos_a, cos_b, (0, 1))
        step(0, 1, cos_b, cos_a, None)
        predict(0, 1)
    else:

        def pair(j, _):
            step(j, 0, cos_a, cos_b, (j, 1))
            step(j, 1, cos_b, cos_a, (jnp.minimum(j + 1, nb - 1), 0))
            predict(j, 1)
            return 0

        lax.fori_loop(0, nb, pair, 0)
    for h, dst in enumerate((keep, send)):
        total = acc[h * block : (h + 1) * block, :]
        total = (total[:, :out] + total[:, out:]).reshape(own.shape[0], 2, rows // 2, out)
        dst[...] = jnp.concatenate([total[:, 0], total[:, 1]], axis=2)


def residual_body(x, total, own, scale, resid, ready, value, *, rows, norm):
    value[...] = scale[...] * total[...] - own[:, rows:, :]
    resid[...] = unpacked(value[x[0]])
    ready[...] = value[...] * scale[...] * norm


def grads_body(own, mate, *refs):
    outs = refs[-4:]
    r = jnp.concatenate([unpacked(own[...]), unpacked(mate[...])], axis=0)
    out = r.shape[2]
    r1, r2 = split2(r.reshape(-1, out).T)
    rr = jnp.concatenate([r1, r2], axis=0)
    place = 0
    for khi, klo in zip(refs[0:-4:2], refs[1:-4:2]):
        for j in range(khi.shape[0]):
            both = mm(rr, khi[j], NN) + mm(rr, klo[j], NN)
            outs[place][...] = both[:out] + both[out:]
            place += 1


def block_of(points, j, tables):
    peers, group = points.shape[0], CAP * tables
    return points[:, group * j : group * (j + 1), :].reshape(peers * group, 128)


def points_hot(points, blocks, tables, width):
    peers, lanes = points.shape[0], 128 // tables
    offs = points[:, CAP * tables * blocks :, :]
    offs = jnp.concatenate(
        [
            jnp.broadcast_to(offs[:, :, lanes * t : lanes * t + 1], (peers, CAP, 128))
            for t in range(tables)
        ],
        axis=1,
    ).reshape(peers * CAP * tables, 128)
    lane = lax.broadcasted_iota(jnp.int32, offs.shape, 1).astype(F32)
    return jnp.concatenate(
        [(offs == lane + float(128 * k)).astype(BF) for k in range(width // 128)], axis=1
    )


def coeff_body(points, grads, coeff, *, tables):
    out, part = coeff.shape
    blocks = part // 128
    hot = points_hot(points, blocks, tables, grads.shape[1])
    g1, g2 = split2(pick(hot, grads[...], NT, flip=True))
    gg = jnp.concatenate([g1, g2], axis=0)
    for j in range(blocks):
        e1, e2 = split2(block_of(points, j, tables))
        both = mm(gg, e1, NN) + mm(gg, e2, NN)
        coeff[:, 128 * j : 128 * (j + 1)] = both[:out] + both[out:]


def corr_body(member, points, coeff, eig_scale, corr, *, tables):
    out, part = coeff.shape
    blocks = part // 128
    hot = points_hot(points, blocks, tables, corr.shape[1])
    total = jnp.zeros((2 * out, hot.shape[0]), F32)
    for j in range(blocks):
        at = slice(128 * j, 128 * (j + 1))
        e1, e2 = split2(block_of(points, j, tables))
        scale = eig_scale[:, pl.ds(pl.multiple_of(member[0] * part + 128 * j, 128), 128)]
        c1, c2 = split2(coeff[:, at] * scale)
        cc = jnp.concatenate([c1, c2], axis=0)
        total = total + mm(cc, e1, NT) + mm(cc, e2, NT)
    corr[...] = pick(hot, total[:out] + total[out:], NN, flip=True)


def shape(*dims, dtype=F32):
    return jax.ShapeDtypeStruct(dims, dtype)


def params(mib=16):
    return pltpu.CompilerParams(vmem_limit_bytes=mib << 20)


def call(body, outs, *args, mib=16, scalars=0, **kw):
    many = isinstance(outs, (list, tuple))
    smem = pl.BlockSpec(memory_space=pltpu.SMEM)
    return pl.pallas_call(
        body,
        out_shape=outs,
        in_specs=[smem] * scalars + [VMEM] * (len(args) - scalars),
        out_specs=[VMEM] * len(outs) if many else VMEM,
        compiler_params=params(mib),
        **kw,
    )(*args)


def exchange(v, axes):
    return functools.reduce(jnp.add, [v] + mates([v] * math.prod(SIZES[a] for a in axes), axes))


def mates(parts, axes):
    n = math.prod(SIZES[a] for a in axes)
    return [
        lax.ppermute(parts[o], axes, [(i, i ^ o) for i in range(n)]) for o in range(1, n)
    ]


def tile_from(pack, o):
    ny = SIZES["y"]
    perm = [
        ((c * ny + y) * 2 + z, (z * ny + (y ^ o)) * 2 + c)
        for c in range(2) for y in range(ny) for z in range(2)
    ]
    return lax.ppermute(pack, ("core", "y", "zl"), perm)


def together(*arrays):
    return lax.optimization_barrier(arrays)


def per_device(
    pool_features, pool_targets, batch_index, centers, weights,
    eig_vectors, eig_scale, nys_owner, nys_offset,
):
    rows, dim = batch_index.shape[0], pool_features.shape[1]
    nx, ny, half = SIZES["x"], SIZES["y"], rows // 2
    cdev, out = weights.shape
    count, q = eig_vectors.shape
    tables = math.prod(SIZES[a] for a in PLANES)
    peers = math.prod(SIZES[a] for a in OWNERS)
    norm = 1.0 / math.sqrt(rows * math.prod(SIZES[a] for a in ALL))
    x = lax.axis_index("x").astype(jnp.int32)[None]
    member = lax.axis_index(PLANES).astype(jnp.int32)[None]
    straight = lax.axis_index("core") == lax.axis_index("zl")
    wide = 2 * out

    drawn, pack = pl.pallas_call(
        front_body,
        out_shape=[shape(rows + half, dim), shape(cdev + cdev // 2, dim)],
        in_specs=[VMEM] + [pl.BlockSpec(memory_space=pltpu.HBM)] * 4,
        out_specs=[VMEM] * 2,
        scratch_shapes=[
            pltpu.VMEM(pool_features.shape, F32),
            pltpu.VMEM(pool_targets.shape[::-1], F32),
            pltpu.VMEM((out, cdev), F32),
            pltpu.SemaphoreType.DMA((4,)),
        ],
        compiler_params=params(60),
    )(batch_index.reshape(1, rows), pool_features, pool_targets.T, centers, weights.T)

    gathered = mates([drawn] * nx, ("x",))
    tile = tile_from(pack, 0)
    tile, drawn, *gathered = together(tile, drawn, *gathered)
    own = call(order_body, shape(nx, rows + half, dim), x, drawn, *gathered, scalars=1)
    others = [tile_from(pack, o) for o in range(1, ny)]
    (mate,) = mates([own] * 2, ("core",))
    eig_vectors, own = together(eig_vectors, own)

    def kernel(packs, extra):
        nb = len(packs)
        outs = [shape(nb, 2 * nx * rows, cdev, dtype=BF)] * 2 + [shape(nx, half, wide)] * 2
        if extra:
            outs = outs + [shape(nx, half, wide), shape(8, cdev)]
        return call(
            functools.partial(kernel_body, nb=nb, rows=rows, sub=32, extra=extra),
            outs, own, mate, *packs,
            scratch_shapes=[
                pltpu.VMEM((2, nx * rows, 6 * dim), BF),
                pltpu.VMEM((nb, cdev, 6 * dim), BF),
                pltpu.VMEM((nb, cdev, wide), BF),
                pltpu.VMEM((nx * rows, cdev), F32),
                pltpu.VMEM((nx * rows, cdev), F32),
                pltpu.VMEM((2 * nx * rows, wide), F32),
            ],
            cost_estimate=pl.CostEstimate(
                flops=100_000_000 if extra else 10_000_000_000 * nb, bytes_accessed=1 << 16, transcendentals=0
            ),
        )

    khi_a, klo_a, keep_a, send_a, scale, sb = kernel([tile], True)

    nys = (nys_owner.reshape(count) * cdev + nys_offset).reshape(1, count)
    parted = call(
        quarters_body, [shape(count + 8, q // tables)] * tables,
        member, eig_vectors, nys, scalars=1,
    )
    keep_a, *parted = together(keep_a, parted[0], *mates(parted, PLANES))
    points = call(
        functools.partial(vectors_body, cdev=cdev),
        shape(peers, CAP * (tables * (q // tables // 128) + 1), 128),
        *parted,
    )
    points = lax.all_to_all(points, OWNERS, split_axis=0, concat_axis=0, tiled=True)

    khi_b, klo_b, keep_b, send_b = kernel(others, False)

    (got,) = mates([send_a + send_b] * 2, ("core",))
    total = exchange(keep_a + keep_b + got, ("x",))
    resid, ready = call(
        functools.partial(residual_body, rows=rows, norm=norm),
        [shape(rows, out), shape(nx, half, wide)],
        x, total, own, scale,
        scalars=1, scratch_shapes=[pltpu.VMEM((nx, half, wide), F32)],
    )
    (ready_mate,) = mates([ready] * 2, ("core",))

    parts = call(
        grads_body, [shape(out, cdev)] * 4, ready, ready_mate, khi_a, klo_a, khi_b, klo_b
    )
    grads = functools.reduce(jnp.add, mates(parts, ("y",)), parts[0]) * sb[0:1]
    points, grads = together(points, grads)
    grads = exchange(grads, PLANES)
    coeff = call(
        functools.partial(coeff_body, tables=tables), shape(out, q // tables), points, grads
    )
    for axis in OWNERS[::-1]:
        coeff = exchange(coeff, (axis,))
    corr = call(
        functools.partial(corr_body, tables=tables),
        shape(out, cdev), member, points, coeff, eig_scale[None, :],
        scalars=1,
    )
    update = exchange(corr, PLANES) - grads
    (swapped,) = mates([update] * 2, ("core",))
    return resid, jnp.where(straight, update, swapped).T


def solution(mesh):
    fine = Mesh(mesh.devices.reshape(tuple(SIZES[a] for a in ALL)), ALL)
    placed = (
        P(ALL, None),
        P(ALL, None),
        P(ALL),
        P(CENTERS, None),
        P(CENTERS, None),
        P(ALL, None),
        P(),
        P(ALL, None),
        P(ALL),
    )
    return jax.shard_map(
        per_device,
        mesh=fine,
        in_specs=placed,
        out_specs=(P(ALL, None), P(CENTERS, None)),
        check_vma=False,
    )
```

```python
import functools
import math

import jax
import jax.numpy as jnp
from jax import lax
from jax.experimental import pallas as pl
from jax.experimental.pallas import tpu as pltpu
from jax.sharding import Mesh, PartitionSpec as P

EPS = 1e-06
CAP = 8
BF = jnp.bfloat16
F32 = jnp.float32
SIZES = {"zh": 2, "core": 2, "x": 4, "y": 4, "zl": 2}
ALL = ("zh", "core", "x", "y", "zl")
CENTERS = ("x", "y", "zl")
PLANES = ("zh", "zl")
OWNERS = ("x", "y", "core")
VMEM = pl.BlockSpec(memory_space=pltpu.VMEM)

ACOS_FULL = (
    0.4999999701976776, -0.31830424070358276, 0.24984024465084076, -0.210431307554245,
    0.17730562388896942, -0.13514360785484314, 0.0806083083152771, -0.031184406951069832,
    0.005619336850941181,
)
ACOS_HIGH = (
    0.4999392330646515, -0.3173876106739044, 0.24387668073177338, -0.18864932656288147,
    0.12859871983528137, -0.06701970100402832, 0.02248113788664341, -0.003529248759150505,
)

NN = (((1,), (0,)), ((), ()))
NT = (((1,), (1,)), ((), ()))


def mm(a, b, dims):
    return lax.dot_general(a, b, dims, preferred_element_type=F32)


def split2(x):
    hi = x.astype(BF)
    return hi, (x - hi.astype(F32)).astype(BF)


def split3(x):
    hi = x.astype(BF)
    rest = x - hi.astype(F32)
    mid = rest.astype(BF)
    return hi, mid, (rest - mid.astype(F32)).astype(BF)


def pick(onehot, x, dims, flip=False):
    parts = split3(x)
    prods = [mm(p, onehot, dims) if flip else mm(onehot, p, dims) for p in parts]
    return prods[0] + prods[1] + prods[2]


def full_nt(a, b):
    a1, a2, a3 = split3(a)
    b1, b2, b3 = split3(b)
    return (
        mm(a1, b1, NT) + (mm(a1, b2, NT) + mm(a2, b1, NT))
        + (mm(a2, b2, NT) + mm(a1, b3, NT) + mm(a3, b1, NT))
    )


def horner(coefs, x):
    acc = coefs[-1] * x + coefs[-2]
    for c in coefs[-3::-1]:
        acc = acc * x + c
    return acc


def ntk_over_scale(c):
    inv_pi = 1.0 / math.pi
    ntk = c
    for layer in range(3):
        w = jnp.maximum(1.0 - c * c, 1e-30)
        root = w * lax.rsqrt(w)
        arg = jnp.abs(c) if layer == 0 else c
        angle = root * horner(ACOS_HIGH if layer == 2 else ACOS_FULL, arg)
        remain = jnp.where(c < 0.0, angle, 1.0 - angle) if layer == 0 else 1.0 - angle
        if layer == 2:
            return root * inv_pi + remain * (c + ntk)
        c = root * inv_pi + remain * c
        ntk = c + ntk * remain


def rows_hot(index, width):
    n = index.shape[1]
    col = jnp.broadcast_to(index.astype(F32), (128, n)).T
    lane = lax.broadcasted_iota(jnp.int32, (n, 128), 1).astype(F32)
    return jnp.concatenate(
        [(col == lane + float(128 * k)).astype(BF) for k in range(width // 128)], axis=1
    )


def packed(x):
    half = x.shape[0] // 2
    return jnp.concatenate([x[:half], x[half:]], axis=1)


def unpacked(x):
    wide = x.shape[-1] // 2
    return jnp.concatenate([x[..., :wide], x[..., wide:]], axis=-2)


def front_body(index, pool_f, pool_t, centers, weights, drawn, pack, feats, targs, wts, sems):
    count = centers.shape[0]
    copies = [
        pltpu.make_async_copy(src, dst, sems.at[n])
        for n, (src, dst) in enumerate(
            ((pool_f, feats), (pool_t, targs), (weights, wts), (centers, pack.at[0:count, :]))
        )
    ]
    for copy in copies:
        copy.start()
    rows = index.shape[1]
    hot = rows_hot(index[...], feats.shape[0])
    copies[0].wait()
    drawn[0:rows, :] = pick(hot, feats[...], NN)
    copies[1].wait()
    drawn[rows:, :] = packed(pick(hot, targs[...], NT, flip=True).T)
    copies[2].wait()
    pack[count:, :] = packed(wts[...].T)
    copies[3].wait()


def order_body(x, *refs):
    parts, out = refs[:-1], refs[-1]
    for o, part in enumerate(parts):
        out[x[0] ^ o] = part[...]


def quarters_body(member, eig, nys, *outs):
    count, q = eig.shape
    part = q // len(outs)
    row = jnp.broadcast_to(nys[...].astype(F32), (8, count))
    row = jnp.concatenate([row] * (part // count), axis=1)
    for o, out in enumerate(outs):
        mate = member[0] ^ o
        out[0:count, :] = eig[:, pl.ds(pl.multiple_of(mate * part, part), part)]
        out[count:, :] = row


def vectors_body(*refs, cdev):
    tables, send = refs[:-1], refs[-1]
    count, part = tables[0].shape[0] - 8, tables[0].shape[1]
    peers = send.shape[0]
    blocks, group, lanes = part // 128, CAP * len(tables), 128 // len(tables)
    earlier = lax.broadcasted_iota(jnp.int32, (count, count), 0) < lax.broadcasted_iota(
        jnp.int32, (count, count), 1
    )
    shared = []
    for t, table in enumerate(tables):
        nys = table[count : count + 1, 0:count].astype(jnp.int32)
        owner = nys // cdev
        offset = nys - owner * cdev
        row = jnp.broadcast_to(owner.astype(F32), (count, count))
        same = jnp.where(row.T == row, 1.0, 0.0)
        rank = jnp.sum(jnp.where(earlier, same, 0.0), axis=0, keepdims=True).astype(jnp.int32)
        place = owner * CAP + rank == lax.broadcasted_iota(jnp.int32, (peers * CAP, count), 0)
        offs = jnp.sum(jnp.where(place, offset.astype(F32), 0.0), axis=1, keepdims=True)
        shared.append(jnp.broadcast_to(offs, (peers * CAP, lanes)))
        vectors = pick(place.astype(BF), table[0:count, :], NN)
        for o in range(peers):
            own = slice(o * CAP, (o + 1) * CAP)
            for j in range(blocks):
                at = group * j + CAP * t
                send[o, at : at + CAP, :] = vectors[own, 128 * j : 128 * (j + 1)]
    shared = jnp.concatenate(shared, axis=1)
    for o in range(peers):
        send[o, group * blocks :, :] = shared[o * CAP : (o + 1) * CAP]


def kernel_body(*refs, nb, rows, sub, extra):
    own, mate = refs[0:2]
    packs = refs[2 : 2 + nb]
    khi, klo, keep, send = refs[2 + nb : 6 + nb]
    lhs, cen, wts, cos_a, cos_b, acc = refs[-6:]
    dim, count = own.shape[2], khi.shape[2]
    block = own.shape[0] * rows
    out = dim // 2
    for h, part in enumerate((own, mate)):
        f = part[:, 0:rows, :].reshape(block, dim)
        sa = jnp.sqrt(jnp.mean(f * f, axis=1, keepdims=True) + EPS)
        a1, a2, a3 = split3(f / sa)
        lhs[h] = jnp.concatenate([a1, a2, a1, a2, a1, a3], axis=1)
        if extra and h == 0:
            wide = jnp.broadcast_to(sa, (block, out)).reshape(own.shape[0], rows, out)
            half = rows // 2
            refs[6 + nb][...] = jnp.concatenate([wide[:, :half], wide[:, half:]], axis=2)
    for j, pack in enumerate(packs):
        b = pack[0:count, :]
        sb = jnp.sqrt(jnp.mean(b * b, axis=1, keepdims=True) + EPS)
        b1, b2, b3 = split3(b / sb * (1.0 / dim))
        cen[j] = jnp.concatenate([b1, b1, b2, b2, b3, b1], axis=1)
        w1, w2 = split2(unpacked(pack[count:, :]) * sb)
        wts[j] = jnp.concatenate([w1, w2], axis=1)
        if extra:
            nb_row = full_nt(jnp.ones((8, dim), F32), b * b) * (1.0 / dim) + EPS
            refs[7 + nb][...] = jnp.sqrt(nb_row)
    acc[...] = jnp.zeros(acc.shape, F32)

    def cosines(dst, j, h, n):
        at = slice(n * (count // 2), (n + 1) * (count // 2))
        dst[:, at] = mm(lhs[h], cen[j, at, :], NT)

    def elementwise(values, j, h, n):
        at = slice(h * block + n * sub, h * block + (n + 1) * sub)
        hi, lo = split2(ntk_over_scale(values[n * sub : (n + 1) * sub, :]))
        khi[j, at, :] = hi
        klo[j, at, :] = lo

    def predict(j, h):
        at = slice(h * block, (h + 1) * block)
        both = mm(khi[j, at, :], wts[j], NN) + mm(klo[j, at, :], wts[j], NN)
        acc[at, :] = acc[at, :] + both

    def step(j, h, now, later, after):
        elems = [functools.partial(elementwise, now, j, h, n) for n in range(block // sub)]
        others = [functools.partial(cosines, later, *after, n) for n in range(2)] if after else []
        if h == 1:
            others.append(functools.partial(predict, j, 0))
        every = len(elems) // 3
        for n, f in enumerate(elems):
            if n % every == 0 and others:
                others.pop(0)()
            f()

    for n in range(2):
        cosines(cos_a, 0, 0, n)
    if nb == 1:
        step(0, 0, cos_a, cos_b, (0, 1))
        step(0, 1, cos_b, cos_a, None)
        predict(0, 1)
    else:

        def pair(j, _):
            step(j, 0, cos_a, cos_b, (j, 1))
            step(j, 1, cos_b, cos_a, (jnp.minimum(j + 1, nb - 1), 0))
            predict(j, 1)
            return 0

        lax.fori_loop(0, nb, pair, 0)
    for h, dst in enumerate((keep, send)):
        total = acc[h * block : (h + 1) * block, :]
        total = (total[:, :out] + total[:, out:]).reshape(own.shape[0], 2, rows // 2, out)
        dst[...] = jnp.concatenate([total[:, 0], total[:, 1]], axis=2)


def residual_body(x, total, own, scale, resid, ready, value, *, rows, norm):
    value[...] = scale[...] * total[...] - own[:, rows:, :]
    resid[...] = unpacked(value[x[0]])
    ready[...] = value[...] * scale[...] * norm


def grads_body(own, mate, *refs):
    outs = refs[-4:]
    r = jnp.concatenate([unpacked(own[...]), unpacked(mate[...])], axis=0)
    out = r.shape[2]
    r1, r2 = split2(r.reshape(-1, out).T)
    rr = jnp.concatenate([r1, r2], axis=0)
    place = 0
    for khi, klo in zip(refs[0:-4:2], refs[1:-4:2]):
        for j in range(khi.shape[0]):
            both = mm(rr, khi[j], NN) + mm(rr, klo[j], NN)
            outs[place][...] = both[:out] + both[out:]
            place += 1


def block_of(points, j, tables):
    peers, group = points.shape[0], CAP * tables
    return points[:, group * j : group * (j + 1), :].reshape(peers * group, 128)


def points_hot(points, blocks, tables, width):
    peers, lanes = points.shape[0], 128 // tables
    offs = points[:, CAP * tables * blocks :, :]
    offs = jnp.concatenate(
        [
            jnp.broadcast_to(offs[:, :, lanes * t : lanes * t + 1], (peers, CAP, 128))
            for t in range(tables)
        ],
        axis=1,
    ).reshape(peers * CAP * tables, 128)
    lane = lax.broadcasted_iota(jnp.int32, offs.shape, 1).astype(F32)
    return jnp.concatenate(
        [(offs == lane + float(128 * k)).astype(BF) for k in range(width // 128)], axis=1
    )


def coeff_body(points, grads, coeff, *, tables):
    out, part = coeff.shape
    blocks = part // 128
    hot = points_hot(points, blocks, tables, grads.shape[1])
    g1, g2 = split2(pick(hot, grads[...], NT, flip=True))
    gg = jnp.concatenate([g1, g2], axis=0)
    for j in range(blocks):
        e1, e2 = split2(block_of(points, j, tables))
        both = mm(gg, e1, NN) + mm(gg, e2, NN)
        coeff[:, 128 * j : 128 * (j + 1)] = both[:out] + both[out:]


def corr_body(member, points, coeff, eig_scale, corr, *, tables):
    out, part = coeff.shape
    blocks = part // 128
    hot = points_hot(points, blocks, tables, corr.shape[1])
    total = jnp.zeros((2 * out, hot.shape[0]), F32)
    for j in range(blocks):
        at = slice(128 * j, 128 * (j + 1))
        e1, e2 = split2(block_of(points, j, tables))
        scale = eig_scale[:, pl.ds(pl.multiple_of(member[0] * part + 128 * j, 128), 128)]
        c1, c2 = split2(coeff[:, at] * scale)
        cc = jnp.concatenate([c1, c2], axis=0)
        total = total + mm(cc, e1, NT) + mm(cc, e2, NT)
    corr[...] = pick(hot, total[:out] + total[out:], NN, flip=True)


def shape(*dims, dtype=F32):
    return jax.ShapeDtypeStruct(dims, dtype)


def params(mib=16):
    return pltpu.CompilerParams(vmem_limit_bytes=mib << 20)


def call(body, outs, *args, mib=16, scalars=0, **kw):
    many = isinstance(outs, (list, tuple))
    smem = pl.BlockSpec(memory_space=pltpu.SMEM)
    return pl.pallas_call(
        body,
        out_shape=outs,
        in_specs=[smem] * scalars + [VMEM] * (len(args) - scalars),
        out_specs=[VMEM] * len(outs) if many else VMEM,
        compiler_params=params(mib),
        **kw,
    )(*args)


def exchange(v, axes):
    return functools.reduce(jnp.add, [v] + mates([v] * math.prod(SIZES[a] for a in axes), axes))


def mates(parts, axes):
    n = math.prod(SIZES[a] for a in axes)
    return [
        lax.ppermute(parts[o], axes, [(i, i ^ o) for i in range(n)]) for o in range(1, n)
    ]


def together(*arrays):
    return lax.optimization_barrier(arrays)


def per_device(
    pool_features, pool_targets, batch_index, centers, weights,
    eig_vectors, eig_scale, nys_owner, nys_offset,
):
    rows, dim = batch_index.shape[0], pool_features.shape[1]
    nx, ny, half = SIZES["x"], SIZES["y"], rows // 2
    cdev, out = weights.shape
    count, q = eig_vectors.shape
    tables = math.prod(SIZES[a] for a in PLANES)
    peers = math.prod(SIZES[a] for a in OWNERS)
    norm = 1.0 / math.sqrt(rows * math.prod(SIZES[a] for a in ALL))
    x = lax.axis_index("x").astype(jnp.int32)[None]
    member = lax.axis_index(PLANES).astype(jnp.int32)[None]
    straight = lax.axis_index("core") == lax.axis_index("zl")
    wide = 2 * out

    drawn, pack = pl.pallas_call(
        front_body,
        out_shape=[shape(rows + half, dim), shape(cdev + cdev // 2, dim)],
        in_specs=[VMEM] + [pl.BlockSpec(memory_space=pltpu.HBM)] * 4,
        out_specs=[VMEM] * 2,
        scratch_shapes=[
            pltpu.VMEM(pool_features.shape, F32),
            pltpu.VMEM(pool_targets.shape[::-1], F32),
            pltpu.VMEM((out, cdev), F32),
            pltpu.SemaphoreType.DMA((4,)),
        ],
        compiler_params=params(60),
    )(batch_index.reshape(1, rows), pool_features, pool_targets.T, centers, weights.T)

    gathered = mates([drawn] * nx, ("x",))
    tile = lax.ppermute(pack, ("core", "zl"), [(0, 0), (2, 1), (1, 2), (3, 3)])
    tile, drawn, *gathered = together(tile, drawn, *gathered)
    own = call(order_body, shape(nx, rows + half, dim), x, drawn, *gathered, scalars=1)
    others = mates([tile] * ny, ("y",))
    (mate,) = mates([own] * 2, ("core",))
    eig_vectors, own = together(eig_vectors, own)

    def kernel(packs, extra):
        nb = len(packs)
        outs = [shape(nb, 2 * nx * rows, cdev, dtype=BF)] * 2 + [shape(nx, half, wide)] * 2
        if extra:
            outs = outs + [shape(nx, half, wide), shape(8, cdev)]
        return call(
            functools.partial(kernel_body, nb=nb, rows=rows, sub=32, extra=extra),
            outs, own, mate, *packs,
            scratch_shapes=[
                pltpu.VMEM((2, nx * rows, 6 * dim), BF),
                pltpu.VMEM((nb, cdev, 6 * dim), BF),
                pltpu.VMEM((nb, cdev, wide), BF),
                pltpu.VMEM((nx * rows, cdev), F32),
                pltpu.VMEM((nx * rows, cdev), F32),
                pltpu.VMEM((2 * nx * rows, wide), F32),
            ],
            cost_estimate=pl.CostEstimate(
                flops=100_000_000 if extra else 10_000_000_000 * nb, bytes_accessed=1 << 16, transcendentals=0
            ),
        )

    khi_a, klo_a, keep_a, send_a, scale, sb = kernel([tile], True)

    nys = (nys_owner.reshape(count) * cdev + nys_offset).reshape(1, count)
    parted = call(
        quarters_body, [shape(count + 8, q // tables)] * tables,
        member, eig_vectors, nys, scalars=1,
    )
    keep_a, *parted = together(keep_a, parted[0], *mates(parted, PLANES))
    points = call(
        functools.partial(vectors_body, cdev=cdev),
        shape(peers, CAP * (tables * (q // tables // 128) + 1), 128),
        *parted,
    )
    points = lax.all_to_all(points, OWNERS, split_axis=0, concat_axis=0, tiled=True)

    khi_b, klo_b, keep_b, send_b = kernel(others, False)

    (got,) = mates([send_a + send_b] * 2, ("core",))
    total = exchange(keep_a + keep_b + got, ("x",))
    resid, ready = call(
        functools.partial(residual_body, rows=rows, norm=norm),
        [shape(rows, out), shape(nx, half, wide)],
        x, total, own, scale,
        scalars=1, scratch_shapes=[pltpu.VMEM((nx, half, wide), F32)],
    )
    (ready_mate,) = mates([ready] * 2, ("core",))

    parts = call(
        grads_body, [shape(out, cdev)] * 4, ready, ready_mate, khi_a, klo_a, khi_b, klo_b
    )
    grads = functools.reduce(jnp.add, mates(parts, ("y",)), parts[0]) * sb[0:1]
    points, grads = together(points, grads)
    grads = exchange(grads, PLANES)
    coeff = call(
        functools.partial(coeff_body, tables=tables), shape(out, q // tables), points, grads
    )
    for axis in OWNERS[::-1]:
        coeff = exchange(coeff, (axis,))
    corr = call(
        functools.partial(corr_body, tables=tables),
        shape(out, cdev), member, points, coeff, eig_scale[None, :],
        scalars=1,
    )
    update = exchange(corr, PLANES) - grads
    (swapped,) = mates([update] * 2, ("core",))
    return resid, jnp.where(straight, update, swapped).T


def solution(mesh):
    fine = Mesh(mesh.devices.reshape(tuple(SIZES[a] for a in ALL)), ALL)
    placed = (
        P(ALL, None),
        P(ALL, None),
        P(ALL),
        P(CENTERS, None),
        P(CENTERS, None),
        P(ALL, None),
        P(),
        P(ALL, None),
        P(ALL),
    )
    return jax.shard_map(
        per_device,
        mesh=fine,
        in_specs=placed,
        out_specs=(P(ALL, None), P(CENTERS, None)),
        check_vma=False,
    )
```

```python
import functools
import math

import jax
import jax.numpy as jnp
from jax import lax
from jax.experimental import pallas as pl
from jax.experimental.pallas import tpu as pltpu
from jax.sharding import Mesh, PartitionSpec as P

EPS = 1e-06
CAP = 8
BF = jnp.bfloat16
F32 = jnp.float32
SIZES = {"zh": 2, "core": 2, "x": 4, "y": 4, "zl": 2}
ALL = ("zh", "core", "x", "y", "zl")
CENTERS = ("x", "y", "zl")
PLANES = ("zh", "zl")
OWNERS = ("x", "y", "core")
VMEM = pl.BlockSpec(memory_space=pltpu.VMEM)

ACOS_FULL = (
    0.4999999701976776, -0.31830424070358276, 0.24984024465084076, -0.210431307554245,
    0.17730562388896942, -0.13514360785484314, 0.0806083083152771, -0.031184406951069832,
    0.005619336850941181,
)
ACOS_HIGH = (
    0.4999392330646515, -0.3173876106739044, 0.24387668073177338, -0.18864932656288147,
    0.12859871983528137, -0.06701970100402832, 0.02248113788664341, -0.003529248759150505,
)

NN = (((1,), (0,)), ((), ()))
NT = (((1,), (1,)), ((), ()))


def mm(a, b, dims):
    return lax.dot_general(a, b, dims, preferred_element_type=F32)


def split2(x):
    hi = x.astype(BF)
    return hi, (x - hi.astype(F32)).astype(BF)


def split3(x):
    hi = x.astype(BF)
    rest = x - hi.astype(F32)
    mid = rest.astype(BF)
    return hi, mid, (rest - mid.astype(F32)).astype(BF)


def pick(onehot, x, dims, flip=False):
    parts = split3(x)
    prods = [mm(p, onehot, dims) if flip else mm(onehot, p, dims) for p in parts]
    return prods[0] + prods[1] + prods[2]


def full_nt(a, b):
    a1, a2, a3 = split3(a)
    b1, b2, b3 = split3(b)
    return (
        mm(a1, b1, NT) + (mm(a1, b2, NT) + mm(a2, b1, NT))
        + (mm(a2, b2, NT) + mm(a1, b3, NT) + mm(a3, b1, NT))
    )


def horner(coefs, x):
    acc = coefs[-1] * x + coefs[-2]
    for c in coefs[-3::-1]:
        acc = acc * x + c
    return acc


def ntk_over_scale(c):
    inv_pi = 1.0 / math.pi
    ntk = c
    for layer in range(3):
        w = jnp.maximum(1.0 - c * c, 1e-30)
        root = w * lax.rsqrt(w)
        arg = jnp.abs(c) if layer == 0 else c
        angle = root * horner(ACOS_HIGH if layer == 2 else ACOS_FULL, arg)
        remain = jnp.where(c < 0.0, angle, 1.0 - angle) if layer == 0 else 1.0 - angle
        if layer == 2:
            return root * inv_pi + remain * (c + ntk)
        c = root * inv_pi + remain * c
        ntk = c + ntk * remain


def rows_hot(index, width):
    n = index.shape[1]
    col = jnp.broadcast_to(index.astype(F32), (128, n)).T
    lane = lax.broadcasted_iota(jnp.int32, (n, 128), 1).astype(F32)
    return jnp.concatenate(
        [(col == lane + float(128 * k)).astype(BF) for k in range(width // 128)], axis=1
    )


def packed(x):
    half = x.shape[0] // 2
    return jnp.concatenate([x[:half], x[half:]], axis=1)


def unpacked(x):
    wide = x.shape[-1] // 2
    return jnp.concatenate([x[..., :wide], x[..., wide:]], axis=-2)


def front_body(member, *refs, tables):
    index_h, pool_f, pool_t, weights_h, centers, eig_h, owner_h, offset_h = refs[0:8]
    drawn, pack = refs[8:10]
    parts = refs[10 : 10 + tables]
    index, feats, targs, wts, eig, owner, offset, sems = refs[10 + tables :]
    cdev = centers.shape[0]
    copies = [
        pltpu.make_async_copy(src, dst, sems.at[n])
        for n, (src, dst) in enumerate(
            (
                (index_h, index), (pool_f, feats), (pool_t, targs), (weights_h, wts),
                (centers, pack.at[0:cdev, :]), (eig_h, eig), (owner_h, owner), (offset_h, offset),
            )
        )
    ]
    for copy in copies:
        copy.start()
    rows = index.shape[1]
    copies[0].wait()
    hot = rows_hot(index[...], feats.shape[0])
    copies[1].wait()
    drawn[0:rows, :] = pick(hot, feats[...], NN)
    copies[2].wait()
    drawn[rows:, :] = packed(pick(hot, targs[...], NT, flip=True).T)
    copies[3].wait()
    pack[cdev:, :] = packed(wts[...].T)
    for copy in copies[4:]:
        copy.wait()
    count, q = eig.shape
    part = q // tables
    row = jnp.broadcast_to((owner[...] * cdev + offset[...]).astype(F32), (8, count))
    row = jnp.concatenate([row] * (part // count), axis=1)
    for o, out in enumerate(parts):
        mate = member[0] ^ o
        out[0:count, :] = eig[:, pl.ds(pl.multiple_of(mate * part, part), part)]
        out[count:, :] = row


def order_body(x, *refs):
    parts, out = refs[:-1], refs[-1]
    for o, part in enumerate(parts):
        out[x[0] ^ o] = part[...]


def vectors_body(*refs, cdev):
    tables, send = refs[:-1], refs[-1]
    count, part = tables[0].shape[0] - 8, tables[0].shape[1]
    peers = send.shape[0]
    blocks, group, lanes = part // 128, CAP * len(tables), 128 // len(tables)
    earlier = lax.broadcasted_iota(jnp.int32, (count, count), 0) < lax.broadcasted_iota(
        jnp.int32, (count, count), 1
    )
    shared = []
    for t, table in enumerate(tables):
        nys = table[count : count + 1, 0:count].astype(jnp.int32)
        owner = nys // cdev
        offset = nys - owner * cdev
        row = jnp.broadcast_to(owner.astype(F32), (count, count))
        same = jnp.where(row.T == row, 1.0, 0.0)
        rank = jnp.sum(jnp.where(earlier, same, 0.0), axis=0, keepdims=True).astype(jnp.int32)
        place = owner * CAP + rank == lax.broadcasted_iota(jnp.int32, (peers * CAP, count), 0)
        offs = jnp.sum(jnp.where(place, offset.astype(F32), 0.0), axis=1, keepdims=True)
        shared.append(jnp.broadcast_to(offs, (peers * CAP, lanes)))
        vectors = pick(place.astype(BF), table[0:count, :], NN)
        for o in range(peers):
            own = slice(o * CAP, (o + 1) * CAP)
            for j in range(blocks):
                at = group * j + CAP * t
                send[o, at : at + CAP, :] = vectors[own, 128 * j : 128 * (j + 1)]
    shared = jnp.concatenate(shared, axis=1)
    for o in range(peers):
        send[o, group * blocks :, :] = shared[o * CAP : (o + 1) * CAP]


def kernel_body(*refs, nb, rows, sub, extra):
    own, mate = refs[0:2]
    packs = refs[2 : 2 + nb]
    khi, klo, keep, send = refs[2 + nb : 6 + nb]
    lhs, cen, wts, cos_a, cos_b, acc = refs[-6:]
    dim, count = own.shape[2], khi.shape[2]
    block = own.shape[0] * rows
    out = dim // 2
    for h, part in enumerate((own, mate)):
        f = part[:, 0:rows, :].reshape(block, dim)
        sa = jnp.sqrt(jnp.mean(f * f, axis=1, keepdims=True) + EPS)
        a1, a2, a3 = split3(f / sa)
        lhs[h] = jnp.concatenate([a1, a2, a1, a2, a1, a3], axis=1)
        if extra and h == 0:
            wide = jnp.broadcast_to(sa, (block, out)).reshape(own.shape[0], rows, out)
            half = rows // 2
            refs[6 + nb][...] = jnp.concatenate([wide[:, :half], wide[:, half:]], axis=2)
    for j, pack in enumerate(packs):
        b = pack[0:count, :]
        sb = jnp.sqrt(jnp.mean(b * b, axis=1, keepdims=True) + EPS)
        b1, b2, b3 = split3(b / sb * (1.0 / dim))
        cen[j] = jnp.concatenate([b1, b1, b2, b2, b3, b1], axis=1)
        w1, w2 = split2(unpacked(pack[count:, :]) * sb)
        wts[j] = jnp.concatenate([w1, w2], axis=1)
        if extra:
            nb_row = full_nt(jnp.ones((8, dim), F32), b * b) * (1.0 / dim) + EPS
            refs[7 + nb][...] = jnp.sqrt(nb_row)
    acc[...] = jnp.zeros(acc.shape, F32)

    def cosines(dst, j, h, n):
        at = slice(n * (count // 2), (n + 1) * (count // 2))
        dst[:, at] = mm(lhs[h], cen[j, at, :], NT)

    def elementwise(values, j, h, n):
        at = slice(h * block + n * sub, h * block + (n + 1) * sub)
        hi, lo = split2(ntk_over_scale(values[n * sub : (n + 1) * sub, :]))
        khi[j, at, :] = hi
        klo[j, at, :] = lo

    def predict(j, h):
        at = slice(h * block, (h + 1) * block)
        both = mm(khi[j, at, :], wts[j], NN) + mm(klo[j, at, :], wts[j], NN)
        acc[at, :] = acc[at, :] + both

    def step(j, h, now, later, after):
        elems = [functools.partial(elementwise, now, j, h, n) for n in range(block // sub)]
        others = [functools.partial(cosines, later, *after, n) for n in range(2)] if after else []
        if h == 1:
            others.append(functools.partial(predict, j, 0))
        every = len(elems) // 3
        for n, f in enumerate(elems):
            if n % every == 0 and others:
                others.pop(0)()
            f()

    for n in range(2):
        cosines(cos_a, 0, 0, n)
    if nb == 1:
        step(0, 0, cos_a, cos_b, (0, 1))
        step(0, 1, cos_b, cos_a, None)
        predict(0, 1)
    else:

        def pair(j, _):
            step(j, 0, cos_a, cos_b, (j, 1))
            step(j, 1, cos_b, cos_a, (jnp.minimum(j + 1, nb - 1), 0))
            predict(j, 1)
            return 0

        lax.fori_loop(0, nb, pair, 0)
    for h, dst in enumerate((keep, send)):
        total = acc[h * block : (h + 1) * block, :]
        total = (total[:, :out] + total[:, out:]).reshape(own.shape[0], 2, rows // 2, out)
        dst[...] = jnp.concatenate([total[:, 0], total[:, 1]], axis=2)


def residual_body(x, total, own, scale, resid, ready, value, *, rows, norm):
    value[...] = scale[...] * total[...] - own[:, rows:, :]
    resid[...] = unpacked(value[x[0]])
    ready[...] = value[...] * scale[...] * norm


def grads_body(own, mate, *refs):
    outs = refs[-4:]
    r = jnp.concatenate([unpacked(own[...]), unpacked(mate[...])], axis=0)
    out = r.shape[2]
    r1, r2 = split2(r.reshape(-1, out).T)
    rr = jnp.concatenate([r1, r2], axis=0)
    place = 0
    for khi, klo in zip(refs[0:-4:2], refs[1:-4:2]):
        for j in range(khi.shape[0]):
            both = mm(rr, khi[j], NN) + mm(rr, klo[j], NN)
            outs[place][...] = both[:out] + both[out:]
            place += 1


def block_of(points, j, tables):
    peers, group = points.shape[0], CAP * tables
    return points[:, group * j : group * (j + 1), :].reshape(peers * group, 128)


def points_hot(points, blocks, tables, width):
    peers, lanes = points.shape[0], 128 // tables
    offs = points[:, CAP * tables * blocks :, :]
    offs = jnp.concatenate(
        [
            jnp.broadcast_to(offs[:, :, lanes * t : lanes * t + 1], (peers, CAP, 128))
            for t in range(tables)
        ],
        axis=1,
    ).reshape(peers * CAP * tables, 128)
    lane = lax.broadcasted_iota(jnp.int32, offs.shape, 1).astype(F32)
    return jnp.concatenate(
        [(offs == lane + float(128 * k)).astype(BF) for k in range(width // 128)], axis=1
    )


def coeff_body(points, grads, coeff, *, tables):
    out, part = coeff.shape
    blocks = part // 128
    hot = points_hot(points, blocks, tables, grads.shape[1])
    g1, g2 = split2(pick(hot, grads[...], NT, flip=True))
    gg = jnp.concatenate([g1, g2], axis=0)
    for j in range(blocks):
        e1, e2 = split2(block_of(points, j, tables))
        both = mm(gg, e1, NN) + mm(gg, e2, NN)
        coeff[:, 128 * j : 128 * (j + 1)] = both[:out] + both[out:]


def corr_body(member, points, coeff, eig_scale, corr, *, tables):
    out, part = coeff.shape
    blocks = part // 128
    hot = points_hot(points, blocks, tables, corr.shape[1])
    total = jnp.zeros((2 * out, hot.shape[0]), F32)
    for j in range(blocks):
        at = slice(128 * j, 128 * (j + 1))
        e1, e2 = split2(block_of(points, j, tables))
        scale = eig_scale[:, pl.ds(pl.multiple_of(member[0] * part + 128 * j, 128), 128)]
        c1, c2 = split2(coeff[:, at] * scale)
        cc = jnp.concatenate([c1, c2], axis=0)
        total = total + mm(cc, e1, NT) + mm(cc, e2, NT)
    corr[...] = pick(hot, total[:out] + total[out:], NN, flip=True)


def shape(*dims, dtype=F32):
    return jax.ShapeDtypeStruct(dims, dtype)


def params(mib=16):
    return pltpu.CompilerParams(vmem_limit_bytes=mib << 20)


def call(body, outs, *args, mib=16, scalars=0, **kw):
    many = isinstance(outs, (list, tuple))
    smem = pl.BlockSpec(memory_space=pltpu.SMEM)
    return pl.pallas_call(
        body,
        out_shape=outs,
        in_specs=[smem] * scalars + [VMEM] * (len(args) - scalars),
        out_specs=[VMEM] * len(outs) if many else VMEM,
        compiler_params=params(mib),
        **kw,
    )(*args)


def exchange(v, axes):
    return functools.reduce(jnp.add, [v] + mates([v] * math.prod(SIZES[a] for a in axes), axes))


def mates(parts, axes):
    return [mate_of(parts[o], axes, o) for o in range(1, len(parts))]


def mate_of(v, axes, o):
    n = math.prod(SIZES[a] for a in axes)
    return lax.ppermute(v, axes, [(i, i ^ o) for i in range(n)])


def together(*arrays):
    return lax.optimization_barrier(arrays)


def per_device(
    pool_features, pool_targets, batch_index, centers, weights,
    eig_vectors, eig_scale, nys_owner, nys_offset,
):
    rows, dim = batch_index.shape[0], pool_features.shape[1]
    nx, ny, half = SIZES["x"], SIZES["y"], rows // 2
    cdev, out = weights.shape
    count, q = eig_vectors.shape
    tables = math.prod(SIZES[a] for a in PLANES)
    peers = math.prod(SIZES[a] for a in OWNERS)
    norm = 1.0 / math.sqrt(rows * math.prod(SIZES[a] for a in ALL))
    x = lax.axis_index("x").astype(jnp.int32)[None]
    member = lax.axis_index(PLANES).astype(jnp.int32)[None]
    straight = lax.axis_index("core") == lax.axis_index("zl")
    wide = 2 * out

    hbm = pl.BlockSpec(memory_space=pltpu.HBM)
    drawn, pack, *parted = pl.pallas_call(
        functools.partial(front_body, tables=tables),
        out_shape=[shape(rows + half, dim), shape(cdev + cdev // 2, dim)]
        + [shape(count + 8, q // tables)] * tables,
        in_specs=[pl.BlockSpec(memory_space=pltpu.SMEM)] + [hbm] * 8,
        out_specs=[VMEM] * (2 + tables),
        scratch_shapes=[
            pltpu.VMEM((1, rows), jnp.int32),
            pltpu.VMEM(pool_features.shape, F32),
            pltpu.VMEM(pool_targets.shape[::-1], F32),
            pltpu.VMEM((out, cdev), F32),
            pltpu.VMEM(eig_vectors.shape, F32),
            pltpu.VMEM((1, count), jnp.int32),
            pltpu.VMEM((1, count), jnp.int32),
            pltpu.SemaphoreType.DMA((8,)),
        ],
        compiler_params=params(60),
    )(
        member, batch_index.reshape(1, rows), pool_features, pool_targets.T, weights.T, centers,
        eig_vectors, nys_owner.reshape(1, count), nys_offset.reshape(1, count),
    )

    gathered = mates([drawn] * nx, ("x",))
    tile = lax.ppermute(pack, ("core", "zl"), [(0, 0), (2, 1), (1, 2), (3, 3)])
    first = mate_of(parted[2], PLANES, 2)
    tile, first, drawn, *gathered = together(tile, first, drawn, *gathered)
    own = call(order_body, shape(nx, rows + half, dim), x, drawn, *gathered, scalars=1)
    others = mates([tile] * ny, ("y",))
    mate = mate_of(own, ("core",), 1)
    mate, second, third = together(mate, parted[1], parted[3])
    parted = [parted[0], first, mate_of(second, PLANES, 1), mate_of(third, PLANES, 3)]

    def kernel(packs, extra):
        nb = len(packs)
        outs = [shape(nb, 2 * nx * rows, cdev, dtype=BF)] * 2 + [shape(nx, half, wide)] * 2
        if extra:
            outs = outs + [shape(nx, half, wide), shape(8, cdev)]
        return call(
            functools.partial(kernel_body, nb=nb, rows=rows, sub=32, extra=extra),
            outs, own, mate, *packs,
            scratch_shapes=[
                pltpu.VMEM((2, nx * rows, 6 * dim), BF),
                pltpu.VMEM((nb, cdev, 6 * dim), BF),
                pltpu.VMEM((nb, cdev, wide), BF),
                pltpu.VMEM((nx * rows, cdev), F32),
                pltpu.VMEM((nx * rows, cdev), F32),
                pltpu.VMEM((2 * nx * rows, wide), F32),
            ],
            cost_estimate=pl.CostEstimate(
                flops=100_000_000 if extra else 10_000_000_000 * nb, bytes_accessed=1 << 16, transcendentals=0
            ),
        )

    khi_a, klo_a, keep_a, send_a, scale, sb = kernel([tile], True)

    keep_a, *parted = together(keep_a, *parted)
    points = call(
        functools.partial(vectors_body, cdev=cdev),
        shape(peers, CAP * (tables * (q // tables // 128) + 1), 128),
        *parted,
    )
    points = lax.all_to_all(points, OWNERS, split_axis=0, concat_axis=0, tiled=True)

    khi_b, klo_b, keep_b, send_b = kernel(others, False)

    (got,) = mates([send_a + send_b] * 2, ("core",))
    total = exchange(keep_a + keep_b + got, ("x",))
    resid, ready = call(
        functools.partial(residual_body, rows=rows, norm=norm),
        [shape(rows, out), shape(nx, half, wide)],
        x, total, own, scale,
        scalars=1, scratch_shapes=[pltpu.VMEM((nx, half, wide), F32)],
    )
    (ready_mate,) = mates([ready] * 2, ("core",))

    parts = call(
        grads_body, [shape(out, cdev)] * 4, ready, ready_mate, khi_a, klo_a, khi_b, klo_b
    )
    grads = functools.reduce(jnp.add, mates(parts, ("y",)), parts[0]) * sb[0:1]
    points, grads = together(points, grads)
    grads = exchange(grads, PLANES)
    coeff = call(
        functools.partial(coeff_body, tables=tables), shape(out, q // tables), points, grads
    )
    for axis in OWNERS[::-1]:
        coeff = exchange(coeff, (axis,))
    corr = call(
        functools.partial(corr_body, tables=tables),
        shape(out, cdev), member, points, coeff, eig_scale[None, :],
        scalars=1,
    )
    update = exchange(corr, PLANES) - grads
    (swapped,) = mates([update] * 2, ("core",))
    return resid, jnp.where(straight, update, swapped).T


def solution(mesh):
    fine = Mesh(mesh.devices.reshape(tuple(SIZES[a] for a in ALL)), ALL)
    placed = (
        P(ALL, None),
        P(ALL, None),
        P(ALL),
        P(CENTERS, None),
        P(CENTERS, None),
        P(ALL, None),
        P(),
        P(ALL, None),
        P(ALL),
    )
    return jax.shard_map(
        per_device,
        mesh=fine,
        in_specs=placed,
        out_specs=(P(ALL, None), P(CENTERS, None)),
        check_vma=False,
    )
```

```python
import functools
import math

import jax
import jax.numpy as jnp
from jax import lax
from jax.experimental import pallas as pl
from jax.experimental.pallas import tpu as pltpu
from jax.sharding import Mesh, PartitionSpec as P

EPS = 1e-06
CAP = 8
BF = jnp.bfloat16
F32 = jnp.float32
SIZES = {"zh": 2, "core": 2, "x": 4, "y": 4, "zl": 2}
ALL = ("zh", "core", "x", "y", "zl")
CENTERS = ("x", "y", "zl")
PLANES = ("zh", "zl")
OWNERS = ("x", "y", "core")
VMEM = pl.BlockSpec(memory_space=pltpu.VMEM)

ACOS_FULL = (
    0.4999999701976776, -0.31830424070358276, 0.24984024465084076, -0.210431307554245,
    0.17730562388896942, -0.13514360785484314, 0.0806083083152771, -0.031184406951069832,
    0.005619336850941181,
)
ACOS_HIGH = (
    0.4999392330646515, -0.3173876106739044, 0.24387668073177338, -0.18864932656288147,
    0.12859871983528137, -0.06701970100402832, 0.02248113788664341, -0.003529248759150505,
)

NN = (((1,), (0,)), ((), ()))
NT = (((1,), (1,)), ((), ()))


def mm(a, b, dims):
    return lax.dot_general(a, b, dims, preferred_element_type=F32)


def split2(x):
    hi = x.astype(BF)
    return hi, (x - hi.astype(F32)).astype(BF)


def split3(x):
    hi = x.astype(BF)
    rest = x - hi.astype(F32)
    mid = rest.astype(BF)
    return hi, mid, (rest - mid.astype(F32)).astype(BF)


def pick(onehot, x, dims, flip=False):
    parts = split3(x)
    prods = [mm(p, onehot, dims) if flip else mm(onehot, p, dims) for p in parts]
    return prods[0] + prods[1] + prods[2]


def full_nt(a, b):
    a1, a2, a3 = split3(a)
    b1, b2, b3 = split3(b)
    return (
        mm(a1, b1, NT) + (mm(a1, b2, NT) + mm(a2, b1, NT))
        + (mm(a2, b2, NT) + mm(a1, b3, NT) + mm(a3, b1, NT))
    )


def horner(coefs, x):
    acc = coefs[-1] * x + coefs[-2]
    for c in coefs[-3::-1]:
        acc = acc * x + c
    return acc


def ntk_over_scale(c):
    inv_pi = 1.0 / math.pi
    ntk = c
    for layer in range(3):
        w = jnp.maximum(1.0 - c * c, 1e-30)
        root = w * lax.rsqrt(w)
        arg = jnp.abs(c) if layer == 0 else c
        angle = root * horner(ACOS_HIGH if layer == 2 else ACOS_FULL, arg)
        remain = jnp.where(c < 0.0, angle, 1.0 - angle) if layer == 0 else 1.0 - angle
        if layer == 2:
            return root * inv_pi + remain * (c + ntk)
        c = root * inv_pi + remain * c
        ntk = c + ntk * remain


def rows_hot(index, width):
    n = index.shape[1]
    col = jnp.broadcast_to(index.astype(F32), (128, n)).T
    lane = lax.broadcasted_iota(jnp.int32, (n, 128), 1).astype(F32)
    return jnp.concatenate(
        [(col == lane + float(128 * k)).astype(BF) for k in range(width // 128)], axis=1
    )


def packed(x):
    half = x.shape[0] // 2
    return jnp.concatenate([x[:half], x[half:]], axis=1)


def unpacked(x):
    wide = x.shape[-1] // 2
    return jnp.concatenate([x[..., :wide], x[..., wide:]], axis=-2)


def front_body(index_h, pool_f, pool_t, weights_h, centers, drawn, pack, index, feats, targs, wts, sems):
    cdev = centers.shape[0]
    copies = [
        pltpu.make_async_copy(src, dst, sems.at[n])
        for n, (src, dst) in enumerate(
            (
                (index_h, index), (pool_f, feats), (pool_t, targs), (weights_h, wts),
                (centers, pack.at[0:cdev, :]),
            )
        )
    ]
    for copy in copies:
        copy.start()
    rows = index.shape[1]
    copies[0].wait()
    hot = rows_hot(index[...], feats.shape[0])
    copies[1].wait()
    drawn[0:rows, :] = pick(hot, feats[...], NN)
    copies[2].wait()
    drawn[rows:, :] = packed(pick(hot, targs[...], NT, flip=True).T)
    copies[3].wait()
    pack[cdev:, :] = packed(wts[...].T)
    copies[4].wait()


def order_body(x, *refs):
    parts, out = refs[:-1], refs[-1]
    for o, part in enumerate(parts):
        out[x[0] ^ o] = part[...]


def vectors_body(eig, owner_row, offset_row, send, *, planes):
    count, q = eig.shape
    peers = send.shape[0] // planes
    blocks = q // planes // 128
    owner = owner_row[...]
    earlier = lax.broadcasted_iota(jnp.int32, (count, count), 0) < lax.broadcasted_iota(
        jnp.int32, (count, count), 1
    )
    row = jnp.broadcast_to(owner.astype(F32), (count, count))
    same = jnp.where(row.T == row, 1.0, 0.0)
    rank = jnp.sum(jnp.where(earlier, same, 0.0), axis=0, keepdims=True).astype(jnp.int32)
    place = owner * CAP + rank == lax.broadcasted_iota(jnp.int32, (peers * CAP, count), 0)
    offs = jnp.sum(
        jnp.where(place, offset_row[...].astype(F32), 0.0), axis=1, keepdims=True
    )
    offs = jnp.broadcast_to(offs, (peers * CAP, 128))
    vectors = pick(place.astype(BF), eig[...], NN)
    for o in range(peers):
        own = slice(o * CAP, (o + 1) * CAP)
        for p in range(planes):
            for j in range(blocks):
                at = 128 * (p * blocks + j)
                send[o * planes + p, CAP * j : CAP * (j + 1), :] = vectors[own, at : at + 128]
            send[o * planes + p, CAP * blocks :, :] = offs[own]


def kernel_body(*refs, nb, rows, sub, extra):
    own, mate = refs[0:2]
    packs = refs[2 : 2 + nb]
    khi, klo, keep, send = refs[2 + nb : 6 + nb]
    lhs, cen, wts, cos_a, cos_b, acc = refs[-6:]
    dim, count = own.shape[2], khi.shape[2]
    block = own.shape[0] * rows
    out = dim // 2
    for h, part in enumerate((own, mate)):
        f = part[:, 0:rows, :].reshape(block, dim)
        sa = jnp.sqrt(jnp.mean(f * f, axis=1, keepdims=True) + EPS)
        a1, a2, a3 = split3(f / sa)
        lhs[h] = jnp.concatenate([a1, a2, a1, a2, a1, a3], axis=1)
        if extra and h == 0:
            wide = jnp.broadcast_to(sa, (block, out)).reshape(own.shape[0], rows, out)
            half = rows // 2
            refs[6 + nb][...] = jnp.concatenate([wide[:, :half], wide[:, half:]], axis=2)
    for j, pack in enumerate(packs):
        b = pack[0:count, :]
        sb = jnp.sqrt(jnp.mean(b * b, axis=1, keepdims=True) + EPS)
        b1, b2, b3 = split3(b / sb * (1.0 / dim))
        cen[j] = jnp.concatenate([b1, b1, b2, b2, b3, b1], axis=1)
        w1, w2 = split2(unpacked(pack[count:, :]) * sb)
        wts[j] = jnp.concatenate([w1, w2], axis=1)
        if extra:
            nb_row = full_nt(jnp.ones((8, dim), F32), b * b) * (1.0 / dim) + EPS
            refs[7 + nb][...] = jnp.sqrt(nb_row)
    acc[...] = jnp.zeros(acc.shape, F32)

    def cosines(dst, j, h, n):
        at = slice(n * (count // 2), (n + 1) * (count // 2))
        dst[:, at] = mm(lhs[h], cen[j, at, :], NT)

    def elementwise(values, j, h, n):
        at = slice(h * block + n * sub, h * block + (n + 1) * sub)
        hi, lo = split2(ntk_over_scale(values[n * sub : (n + 1) * sub, :]))
        khi[j, at, :] = hi
        klo[j, at, :] = lo

    def predict(j, h):
        at = slice(h * block, (h + 1) * block)
        both = mm(khi[j, at, :], wts[j], NN) + mm(klo[j, at, :], wts[j], NN)
        acc[at, :] = acc[at, :] + both

    def step(j, h, now, later, after):
        elems = [functools.partial(elementwise, now, j, h, n) for n in range(block // sub)]
        others = [functools.partial(cosines, later, *after, n) for n in range(2)] if after else []
        if h == 1:
            others.append(functools.partial(predict, j, 0))
        every = len(elems) // 3
        for n, f in enumerate(elems):
            if n % every == 0 and others:
                others.pop(0)()
            f()

    for n in range(2):
        cosines(cos_a, 0, 0, n)
    if nb == 1:
        step(0, 0, cos_a, cos_b, (0, 1))
        step(0, 1, cos_b, cos_a, None)
        predict(0, 1)
    else:

        def pair(j, _):
            step(j, 0, cos_a, cos_b, (j, 1))
            step(j, 1, cos_b, cos_a, (jnp.minimum(j + 1, nb - 1), 0))
            predict(j, 1)
            return 0

        lax.fori_loop(0, nb, pair, 0)
    for h, dst in enumerate((keep, send)):
        total = acc[h * block : (h + 1) * block, :]
        total = (total[:, :out] + total[:, out:]).reshape(own.shape[0], 2, rows // 2, out)
        dst[...] = jnp.concatenate([total[:, 0], total[:, 1]], axis=2)


def residual_body(x, total, own, scale, resid, ready, value, *, rows, norm):
    value[...] = scale[...] * total[...] - own[:, rows:, :]
    resid[...] = unpacked(value[x[0]])
    ready[...] = value[...] * scale[...] * norm


def grads_body(own, mate, *refs):
    outs = refs[-4:]
    r = jnp.concatenate([unpacked(own[...]), unpacked(mate[...])], axis=0)
    out = r.shape[2]
    r1, r2 = split2(r.reshape(-1, out).T)
    rr = jnp.concatenate([r1, r2], axis=0)
    place = 0
    for khi, klo in zip(refs[0:-4:2], refs[1:-4:2]):
        for j in range(khi.shape[0]):
            both = mm(rr, khi[j], NN) + mm(rr, klo[j], NN)
            outs[place][...] = both[:out] + both[out:]
            place += 1


def block_of(points, j):
    return points[:, CAP * j : CAP * (j + 1), :].reshape(-1, 128)


def points_hot(points, blocks, width):
    offs = block_of(points, blocks)
    lane = lax.broadcasted_iota(jnp.int32, offs.shape, 1).astype(F32)
    return jnp.concatenate(
        [(offs == lane + float(128 * k)).astype(BF) for k in range(width // 128)], axis=1
    )


def coeff_body(points, grads, coeff):
    out, part = coeff.shape
    blocks = part // 128
    hot = points_hot(points, blocks, grads.shape[1])
    g1, g2 = split2(pick(hot, grads[...], NT, flip=True))
    gg = jnp.concatenate([g1, g2], axis=0)
    for j in range(blocks):
        e1, e2 = split2(block_of(points, j))
        both = mm(gg, e1, NN) + mm(gg, e2, NN)
        coeff[:, 128 * j : 128 * (j + 1)] = both[:out] + both[out:]


def corr_body(member, points, coeff, eig_scale, corr):
    out, part = coeff.shape
    blocks = part // 128
    hot = points_hot(points, blocks, corr.shape[1])
    total = jnp.zeros((2 * out, hot.shape[0]), F32)
    for j in range(blocks):
        at = slice(128 * j, 128 * (j + 1))
        e1, e2 = split2(block_of(points, j))
        scale = eig_scale[:, pl.ds(pl.multiple_of(member[0] * part + 128 * j, 128), 128)]
        c1, c2 = split2(coeff[:, at] * scale)
        cc = jnp.concatenate([c1, c2], axis=0)
        total = total + mm(cc, e1, NT) + mm(cc, e2, NT)
    corr[...] = pick(hot, total[:out] + total[out:], NN, flip=True)


def shape(*dims, dtype=F32):
    return jax.ShapeDtypeStruct(dims, dtype)


def params(mib=16):
    return pltpu.CompilerParams(vmem_limit_bytes=mib << 20)


def call(body, outs, *args, mib=16, scalars=0, **kw):
    many = isinstance(outs, (list, tuple))
    smem = pl.BlockSpec(memory_space=pltpu.SMEM)
    return pl.pallas_call(
        body,
        out_shape=outs,
        in_specs=[smem] * scalars + [VMEM] * (len(args) - scalars),
        out_specs=[VMEM] * len(outs) if many else VMEM,
        compiler_params=params(mib),
        **kw,
    )(*args)


def exchange(v, axes):
    return functools.reduce(jnp.add, [v] + mates([v] * math.prod(SIZES[a] for a in axes), axes))


def mates(parts, axes):
    return [mate_of(parts[o], axes, o) for o in range(1, len(parts))]


def mate_of(v, axes, o):
    n = math.prod(SIZES[a] for a in axes)
    return lax.ppermute(v, axes, [(i, i ^ o) for i in range(n)])


def together(*arrays):
    return lax.optimization_barrier(arrays)


def per_device(
    pool_features, pool_targets, batch_index, centers, weights,
    eig_vectors, eig_scale, nys_owner, nys_offset,
):
    rows, dim = batch_index.shape[0], pool_features.shape[1]
    nx, ny, half = SIZES["x"], SIZES["y"], rows // 2
    cdev, out = weights.shape
    count, q = eig_vectors.shape
    planes = math.prod(SIZES[a] for a in PLANES)
    peers = math.prod(SIZES[a] for a in OWNERS)
    norm = 1.0 / math.sqrt(rows * math.prod(SIZES[a] for a in ALL))
    x = lax.axis_index("x").astype(jnp.int32)[None]
    member = lax.axis_index(PLANES).astype(jnp.int32)[None]
    straight = lax.axis_index("core") == lax.axis_index("zl")
    wide = 2 * out

    hbm = pl.BlockSpec(memory_space=pltpu.HBM)
    drawn, pack = pl.pallas_call(
        front_body,
        out_shape=[shape(rows + half, dim), shape(cdev + cdev // 2, dim)],
        in_specs=[hbm] * 5,
        out_specs=[VMEM] * 2,
        scratch_shapes=[
            pltpu.VMEM((1, rows), jnp.int32),
            pltpu.VMEM(pool_features.shape, F32),
            pltpu.VMEM(pool_targets.shape[::-1], F32),
            pltpu.VMEM((out, cdev), F32),
            pltpu.SemaphoreType.DMA((5,)),
        ],
        compiler_params=params(60),
    )(batch_index.reshape(1, rows), pool_features, pool_targets.T, weights.T, centers)

    gathered = mates([drawn] * nx, ("x",))
    tile = lax.ppermute(pack, ("core", "zl"), [(0, 0), (2, 1), (1, 2), (3, 3)])
    tile, drawn, *gathered = together(tile, drawn, *gathered)
    own = call(order_body, shape(nx, rows + half, dim), x, drawn, *gathered, scalars=1)
    others = mates([tile] * ny, ("y",))
    mate = mate_of(own, ("core",), 1)

    points = call(
        functools.partial(vectors_body, planes=planes),
        shape(peers * planes, CAP * (q // planes // 128 + 1), 128),
        eig_vectors, nys_owner.reshape(1, count), nys_offset.reshape(1, count),
    )
    points, mate = together(points, mate)
    points = lax.all_to_all(points, OWNERS + PLANES, split_axis=0, concat_axis=0, tiled=True)

    def kernel(packs, extra):
        nb = len(packs)
        outs = [shape(nb, 2 * nx * rows, cdev, dtype=BF)] * 2 + [shape(nx, half, wide)] * 2
        if extra:
            outs = outs + [shape(nx, half, wide), shape(8, cdev)]
        return call(
            functools.partial(kernel_body, nb=nb, rows=rows, sub=32, extra=extra),
            outs, own, mate, *packs,
            scratch_shapes=[
                pltpu.VMEM((2, nx * rows, 6 * dim), BF),
                pltpu.VMEM((nb, cdev, 6 * dim), BF),
                pltpu.VMEM((nb, cdev, wide), BF),
                pltpu.VMEM((nx * rows, cdev), F32),
                pltpu.VMEM((nx * rows, cdev), F32),
                pltpu.VMEM((2 * nx * rows, wide), F32),
            ],
            cost_estimate=pl.CostEstimate(
                flops=100_000_000 if extra else 10_000_000_000 * nb, bytes_accessed=1 << 16, transcendentals=0
            ),
        )

    khi_a, klo_a, keep_a, send_a, scale, sb = kernel([tile], True)

    khi_b, klo_b, keep_b, send_b = kernel(others, False)

    (got,) = mates([send_a + send_b] * 2, ("core",))
    total = exchange(keep_a + keep_b + got, ("x",))
    resid, ready = call(
        functools.partial(residual_body, rows=rows, norm=norm),
        [shape(rows, out), shape(nx, half, wide)],
        x, total, own, scale,
        scalars=1, scratch_shapes=[pltpu.VMEM((nx, half, wide), F32)],
    )
    (ready_mate,) = mates([ready] * 2, ("core",))

    parts = call(
        grads_body, [shape(out, cdev)] * 4, ready, ready_mate, khi_a, klo_a, khi_b, klo_b
    )
    grads = functools.reduce(jnp.add, mates(parts, ("y",)), parts[0]) * sb[0:1]
    points, grads = together(points, grads)
    grads = exchange(grads, PLANES)
    coeff = call(coeff_body, shape(out, q // planes), points, grads)
    for axis in OWNERS[::-1]:
        coeff = exchange(coeff, (axis,))
    corr = call(
        corr_body, shape(out, cdev), member, points, coeff, eig_scale[None, :],
        scalars=1,
    )
    update = exchange(corr, PLANES) - grads
    (swapped,) = mates([update] * 2, ("core",))
    return resid, jnp.where(straight, update, swapped).T


def solution(mesh):
    fine = Mesh(mesh.devices.reshape(tuple(SIZES[a] for a in ALL)), ALL)
    placed = (
        P(ALL, None),
        P(ALL, None),
        P(ALL),
        P(CENTERS, None),
        P(CENTERS, None),
        P(ALL, None),
        P(),
        P(ALL, None),
        P(ALL),
    )
    return jax.shard_map(
        per_device,
        mesh=fine,
        in_specs=placed,
        out_specs=(P(ALL, None), P(CENTERS, None)),
        check_vma=False,
    )
```

```python
import functools
import math

import jax
import jax.numpy as jnp
from jax import lax
from jax.experimental import pallas as pl
from jax.experimental.pallas import tpu as pltpu
from jax.sharding import Mesh, PartitionSpec as P

EPS = 1e-06
CAP = 8
BF = jnp.bfloat16
F32 = jnp.float32
SIZES = {"zh": 2, "core": 2, "x": 4, "y": 4, "zl": 2}
ALL = ("zh", "core", "x", "y", "zl")
CENTERS = ("x", "y", "zl")
PLANES = ("zh", "zl")
OWNERS = ("x", "y", "core")
VMEM = pl.BlockSpec(memory_space=pltpu.VMEM)

ACOS_FULL = (
    0.4999999701976776, -0.31830424070358276, 0.24984024465084076, -0.210431307554245,
    0.17730562388896942, -0.13514360785484314, 0.0806083083152771, -0.031184406951069832,
    0.005619336850941181,
)
ACOS_HIGH = (
    0.4999392330646515, -0.3173876106739044, 0.24387668073177338, -0.18864932656288147,
    0.12859871983528137, -0.06701970100402832, 0.02248113788664341, -0.003529248759150505,
)

NN = (((1,), (0,)), ((), ()))
NT = (((1,), (1,)), ((), ()))


def mm(a, b, dims):
    return lax.dot_general(a, b, dims, preferred_element_type=F32)


def split2(x):
    hi = x.astype(BF)
    return hi, (x - hi.astype(F32)).astype(BF)


def split3(x):
    hi = x.astype(BF)
    rest = x - hi.astype(F32)
    mid = rest.astype(BF)
    return hi, mid, (rest - mid.astype(F32)).astype(BF)


def pick(onehot, x, dims, flip=False):
    parts = split3(x)
    prods = [mm(p, onehot, dims) if flip else mm(onehot, p, dims) for p in parts]
    return prods[0] + prods[1] + prods[2]


def full_nt(a, b):
    a1, a2, a3 = split3(a)
    b1, b2, b3 = split3(b)
    return (
        mm(a1, b1, NT) + (mm(a1, b2, NT) + mm(a2, b1, NT))
        + (mm(a2, b2, NT) + mm(a1, b3, NT) + mm(a3, b1, NT))
    )


def horner(coefs, x):
    acc = coefs[-1] * x + coefs[-2]
    for c in coefs[-3::-1]:
        acc = acc * x + c
    return acc


def ntk_over_scale(c):
    inv_pi = 1.0 / math.pi
    ntk = c
    for layer in range(3):
        w = jnp.maximum(1.0 - c * c, 1e-30)
        root = w * lax.rsqrt(w)
        arg = jnp.abs(c) if layer == 0 else c
        angle = root * horner(ACOS_HIGH if layer == 2 else ACOS_FULL, arg)
        remain = jnp.where(c < 0.0, angle, 1.0 - angle) if layer == 0 else 1.0 - angle
        if layer == 2:
            return root * inv_pi + remain * (c + ntk)
        c = root * inv_pi + remain * c
        ntk = c + ntk * remain


def rows_hot(index, width):
    n = index.shape[1]
    col = jnp.broadcast_to(index.astype(F32), (128, n)).T
    lane = lax.broadcasted_iota(jnp.int32, (n, 128), 1).astype(F32)
    return jnp.concatenate(
        [(col == lane + float(128 * k)).astype(BF) for k in range(width // 128)], axis=1
    )


def packed(x):
    half = x.shape[0] // 2
    return jnp.concatenate([x[:half], x[half:]], axis=1)


def unpacked(x):
    wide = x.shape[-1] // 2
    return jnp.concatenate([x[..., :wide], x[..., wide:]], axis=-2)


def front_body(index_h, pool_f, pool_t, weights_h, centers, drawn, pack, index, feats, targs, wts, sems):
    cdev = centers.shape[0]
    copies = [
        pltpu.make_async_copy(src, dst, sems.at[n])
        for n, (src, dst) in enumerate(
            (
                (index_h, index), (pool_f, feats), (pool_t, targs), (weights_h, wts),
                (centers, pack.at[0:cdev, :]),
            )
        )
    ]
    for copy in copies:
        copy.start()
    rows = index.shape[1]
    copies[0].wait()
    hot = rows_hot(index[...], feats.shape[0])
    copies[1].wait()
    drawn[0:rows, :] = pick(hot, feats[...], NN)
    copies[2].wait()
    drawn[rows:, :] = packed(pick(hot, targs[...], NT, flip=True).T)
    copies[3].wait()
    pack[cdev:, :] = packed(wts[...].T)
    copies[4].wait()


def order_body(x, *refs):
    parts, out = refs[:-1], refs[-1]
    for o, part in enumerate(parts):
        out[x[0] ^ o] = part[...]


def vectors_body(eig, owner_row, offset_row, send, *, planes):
    count, q = eig.shape
    peers = send.shape[0] // planes
    blocks = q // planes // 128
    owner = owner_row[...]
    earlier = lax.broadcasted_iota(jnp.int32, (count, count), 0) < lax.broadcasted_iota(
        jnp.int32, (count, count), 1
    )
    row = jnp.broadcast_to(owner.astype(F32), (count, count))
    same = jnp.where(row.T == row, 1.0, 0.0)
    rank = jnp.sum(jnp.where(earlier, same, 0.0), axis=0, keepdims=True).astype(jnp.int32)
    place = owner * CAP + rank == lax.broadcasted_iota(jnp.int32, (peers * CAP, count), 0)
    offs = jnp.sum(
        jnp.where(place, offset_row[...].astype(F32), 0.0), axis=1, keepdims=True
    )
    offs = jnp.broadcast_to(offs, (peers * CAP, 128))
    vectors = pick(place.astype(BF), eig[...], NN)
    for o in range(peers):
        own = slice(o * CAP, (o + 1) * CAP)
        for p in range(planes):
            for j in range(blocks):
                at = 128 * (p * blocks + j)
                send[o * planes + p, CAP * j : CAP * (j + 1), :] = vectors[own, at : at + 128]
            send[o * planes + p, CAP * blocks :, :] = offs[own]


def kernel_body(*refs, nb, rows, sub, extra):
    own, mate = refs[0:2]
    packs = refs[2 : 2 + nb]
    khi, klo, keep, send = refs[2 + nb : 6 + nb]
    lhs, cen, wts, cos_a, cos_b, acc = refs[-6:]
    dim, count = own.shape[2], khi.shape[2]
    block = own.shape[0] * rows
    out = dim // 2
    for h, part in enumerate((own, mate)):
        f = part[:, 0:rows, :].reshape(block, dim)
        sa = jnp.sqrt(jnp.mean(f * f, axis=1, keepdims=True) + EPS)
        a1, a2, a3 = split3(f / sa)
        lhs[h] = jnp.concatenate([a1, a2, a1, a2, a1, a3], axis=1)
        if extra and h == 0:
            wide = jnp.broadcast_to(sa, (block, out)).reshape(own.shape[0], rows, out)
            half = rows // 2
            refs[6 + nb][...] = jnp.concatenate([wide[:, :half], wide[:, half:]], axis=2)
    for j, pack in enumerate(packs):
        b = pack[0:count, :]
        sb = jnp.sqrt(jnp.mean(b * b, axis=1, keepdims=True) + EPS)
        b1, b2, b3 = split3(b / sb * (1.0 / dim))
        cen[j] = jnp.concatenate([b1, b1, b2, b2, b3, b1], axis=1)
        w1, w2 = split2(unpacked(pack[count:, :]) * sb)
        wts[j] = jnp.concatenate([w1, w2], axis=1)
        if extra:
            nb_row = full_nt(jnp.ones((8, dim), F32), b * b) * (1.0 / dim) + EPS
            refs[7 + nb][...] = jnp.sqrt(nb_row)
    acc[...] = jnp.zeros(acc.shape, F32)

    def cosines(dst, j, h, n):
        at = slice(n * (count // 2), (n + 1) * (count // 2))
        dst[:, at] = mm(lhs[h], cen[j, at, :], NT)

    def elementwise(values, j, h, n):
        at = slice(h * block + n * sub, h * block + (n + 1) * sub)
        hi, lo = split2(ntk_over_scale(values[n * sub : (n + 1) * sub, :]))
        khi[j, at, :] = hi
        klo[j, at, :] = lo

    def predict(j, h):
        at = slice(h * block, (h + 1) * block)
        both = mm(khi[j, at, :], wts[j], NN) + mm(klo[j, at, :], wts[j], NN)
        acc[at, :] = acc[at, :] + both

    def step(j, h, now, later, after):
        elems = [functools.partial(elementwise, now, j, h, n) for n in range(block // sub)]
        others = [functools.partial(cosines, later, *after, n) for n in range(2)] if after else []
        if h == 1:
            others.append(functools.partial(predict, j, 0))
        every = len(elems) // 3
        for n, f in enumerate(elems):
            if n % every == 0 and others:
                others.pop(0)()
            f()

    for n in range(2):
        cosines(cos_a, 0, 0, n)
    if nb == 1:
        step(0, 0, cos_a, cos_b, (0, 1))
        step(0, 1, cos_b, cos_a, None)
        predict(0, 1)
    else:

        def pair(j, _):
            step(j, 0, cos_a, cos_b, (j, 1))
            step(j, 1, cos_b, cos_a, (jnp.minimum(j + 1, nb - 1), 0))
            predict(j, 1)
            return 0

        lax.fori_loop(0, nb, pair, 0)
    for h, dst in enumerate((keep, send)):
        total = acc[h * block : (h + 1) * block, :]
        total = (total[:, :out] + total[:, out:]).reshape(own.shape[0], 2, rows // 2, out)
        dst[...] = jnp.concatenate([total[:, 0], total[:, 1]], axis=2)


def residual_body(x, total, own, scale, resid, ready, value, *, rows, norm):
    value[...] = scale[...] * total[...] - own[:, rows:, :]
    resid[...] = unpacked(value[x[0]])
    ready[...] = value[...] * scale[...] * norm


def grads_body(own, mate, *refs):
    outs = refs[-4:]
    r = jnp.concatenate([unpacked(own[...]), unpacked(mate[...])], axis=0)
    out = r.shape[2]
    r1, r2 = split2(r.reshape(-1, out).T)
    rr = jnp.concatenate([r1, r2], axis=0)
    place = 0
    for khi, klo in zip(refs[0:-4:2], refs[1:-4:2]):
        for j in range(khi.shape[0]):
            both = mm(rr, khi[j], NN) + mm(rr, klo[j], NN)
            outs[place][...] = both[:out] + both[out:]
            place += 1


def block_of(points, j):
    return points[:, CAP * j : CAP * (j + 1), :].reshape(-1, 128)


def points_hot(points, blocks, width):
    offs = block_of(points, blocks)
    lane = lax.broadcasted_iota(jnp.int32, offs.shape, 1).astype(F32)
    return jnp.concatenate(
        [(offs == lane + float(128 * k)).astype(BF) for k in range(width // 128)], axis=1
    )


def coeff_body(points, grads, coeff):
    out, part = coeff.shape
    blocks = part // 128
    hot = points_hot(points, blocks, grads.shape[1])
    g1, g2 = split2(pick(hot, grads[...], NT, flip=True))
    gg = jnp.concatenate([g1, g2], axis=0)
    for j in range(blocks):
        e1, e2 = split2(block_of(points, j))
        both = mm(gg, e1, NN) + mm(gg, e2, NN)
        coeff[:, 128 * j : 128 * (j + 1)] = both[:out] + both[out:]


def corr_body(member, points, coeff, eig_scale, corr):
    out, part = coeff.shape
    blocks = part // 128
    hot = points_hot(points, blocks, corr.shape[1])
    total = jnp.zeros((2 * out, hot.shape[0]), F32)
    for j in range(blocks):
        at = slice(128 * j, 128 * (j + 1))
        e1, e2 = split2(block_of(points, j))
        scale = eig_scale[:, pl.ds(pl.multiple_of(member[0] * part + 128 * j, 128), 128)]
        c1, c2 = split2(coeff[:, at] * scale)
        cc = jnp.concatenate([c1, c2], axis=0)
        total = total + mm(cc, e1, NT) + mm(cc, e2, NT)
    corr[...] = pick(hot, total[:out] + total[out:], NN, flip=True)


def shape(*dims, dtype=F32):
    return jax.ShapeDtypeStruct(dims, dtype)


def params(mib=16):
    return pltpu.CompilerParams(vmem_limit_bytes=mib << 20)


def call(body, outs, *args, mib=16, scalars=0, **kw):
    many = isinstance(outs, (list, tuple))
    smem = pl.BlockSpec(memory_space=pltpu.SMEM)
    return pl.pallas_call(
        body,
        out_shape=outs,
        in_specs=[smem] * scalars + [VMEM] * (len(args) - scalars),
        out_specs=[VMEM] * len(outs) if many else VMEM,
        compiler_params=params(mib),
        **kw,
    )(*args)


def exchange(v, axes):
    return functools.reduce(jnp.add, [v] + mates([v] * math.prod(SIZES[a] for a in axes), axes))


def mates(parts, axes):
    return [mate_of(parts[o], axes, o) for o in range(1, len(parts))]


def mate_of(v, axes, o):
    n = math.prod(SIZES[a] for a in axes)
    return lax.ppermute(v, axes, [(i, i ^ o) for i in range(n)])


def together(*arrays):
    return lax.optimization_barrier(arrays)


def per_device(
    pool_features, pool_targets, batch_index, centers, weights,
    eig_vectors, eig_scale, nys_owner, nys_offset,
):
    rows, dim = batch_index.shape[0], pool_features.shape[1]
    nx, ny, half = SIZES["x"], SIZES["y"], rows // 2
    cdev, out = weights.shape
    count, q = eig_vectors.shape
    planes = math.prod(SIZES[a] for a in PLANES)
    peers = math.prod(SIZES[a] for a in OWNERS)
    norm = 1.0 / math.sqrt(rows * math.prod(SIZES[a] for a in ALL))
    x = lax.axis_index("x").astype(jnp.int32)[None]
    member = lax.axis_index(PLANES).astype(jnp.int32)[None]
    straight = lax.axis_index("core") == lax.axis_index("zl")
    wide = 2 * out

    hbm = pl.BlockSpec(memory_space=pltpu.HBM)
    drawn, pack = pl.pallas_call(
        front_body,
        out_shape=[shape(rows + half, dim), shape(cdev + cdev // 2, dim)],
        in_specs=[hbm] * 5,
        out_specs=[VMEM] * 2,
        scratch_shapes=[
            pltpu.VMEM((1, rows), jnp.int32),
            pltpu.VMEM(pool_features.shape, F32),
            pltpu.VMEM(pool_targets.shape[::-1], F32),
            pltpu.VMEM((out, cdev), F32),
            pltpu.SemaphoreType.DMA((5,)),
        ],
        compiler_params=params(60),
    )(batch_index.reshape(1, rows), pool_features, pool_targets.T, weights.T, centers)

    gathered = mates([drawn] * nx, ("x",))
    tile = lax.ppermute(pack, ("core", "zl"), [(0, 0), (2, 1), (1, 2), (3, 3)])
    tile, drawn, *gathered = together(tile, drawn, *gathered)
    own = call(order_body, shape(nx, rows + half, dim), x, drawn, *gathered, scalars=1)
    others = mates([tile] * ny, ("y",))
    mate = mate_of(own, ("core",), 1)

    def kernel(packs, extra):
        nb = len(packs)
        outs = [shape(nb, 2 * nx * rows, cdev, dtype=BF)] * 2 + [shape(nx, half, wide)] * 2
        if extra:
            outs = outs + [shape(nx, half, wide), shape(8, cdev)]
        return call(
            functools.partial(kernel_body, nb=nb, rows=rows, sub=32, extra=extra),
            outs, own, mate, *packs,
            scratch_shapes=[
                pltpu.VMEM((2, nx * rows, 6 * dim), BF),
                pltpu.VMEM((nb, cdev, 6 * dim), BF),
                pltpu.VMEM((nb, cdev, wide), BF),
                pltpu.VMEM((nx * rows, cdev), F32),
                pltpu.VMEM((nx * rows, cdev), F32),
                pltpu.VMEM((2 * nx * rows, wide), F32),
            ],
            cost_estimate=pl.CostEstimate(
                flops=100_000_000 if extra else 10_000_000_000 * nb, bytes_accessed=1 << 16, transcendentals=0
            ),
        )

    khi_a, klo_a, keep_a, send_a, scale, sb = kernel([tile], True)

    points = call(
        functools.partial(vectors_body, planes=planes),
        shape(peers * planes, CAP * (q // planes // 128 + 1), 128),
        eig_vectors, nys_owner.reshape(1, count), nys_offset.reshape(1, count),
    )
    points, keep_a = together(points, keep_a)
    points = lax.all_to_all(points, OWNERS + PLANES, split_axis=0, concat_axis=0, tiled=True)

    khi_b, klo_b, keep_b, send_b = kernel(others, False)

    (got,) = mates([send_a + send_b] * 2, ("core",))
    total = exchange(keep_a + keep_b + got, ("x",))
    resid, ready = call(
        functools.partial(residual_body, rows=rows, norm=norm),
        [shape(rows, out), shape(nx, half, wide)],
        x, total, own, scale,
        scalars=1, scratch_shapes=[pltpu.VMEM((nx, half, wide), F32)],
    )
    (ready_mate,) = mates([ready] * 2, ("core",))

    parts = call(
        grads_body, [shape(out, cdev)] * 4, ready, ready_mate, khi_a, klo_a, khi_b, klo_b
    )
    grads = functools.reduce(jnp.add, mates(parts, ("y",)), parts[0]) * sb[0:1]
    points, grads = together(points, grads)
    grads = exchange(grads, PLANES)
    coeff = call(coeff_body, shape(out, q // planes), points, grads)
    for axis in OWNERS[::-1]:
        coeff = exchange(coeff, (axis,))
    corr = call(
        corr_body, shape(out, cdev), member, points, coeff, eig_scale[None, :],
        scalars=1,
    )
    update = exchange(corr, PLANES) - grads
    (swapped,) = mates([update] * 2, ("core",))
    return resid, jnp.where(straight, update, swapped).T


def solution(mesh):
    fine = Mesh(mesh.devices.reshape(tuple(SIZES[a] for a in ALL)), ALL)
    placed = (
        P(ALL, None),
        P(ALL, None),
        P(ALL),
        P(CENTERS, None),
        P(CENTERS, None),
        P(ALL, None),
        P(),
        P(ALL, None),
        P(ALL),
    )
    return jax.shard_map(
        per_device,
        mesh=fine,
        in_specs=placed,
        out_specs=(P(ALL, None), P(CENTERS, None)),
        check_vma=False,
    )
```

```python
import functools
import math

import jax
import jax.numpy as jnp
from jax import lax
from jax.experimental import pallas as pl
from jax.experimental.pallas import tpu as pltpu
from jax.sharding import Mesh, PartitionSpec as P

EPS = 1e-06
CAP = 8
BF = jnp.bfloat16
F32 = jnp.float32
SIZES = {"zh": 2, "core": 2, "x": 4, "y": 4, "zl": 2}
ALL = ("zh", "core", "x", "y", "zl")
CENTERS = ("x", "y", "zl")
PLANES = ("zh", "zl")
OWNERS = ("x", "y", "core")
VMEM = pl.BlockSpec(memory_space=pltpu.VMEM)

ACOS_FULL = (
    0.4999999701976776, -0.31830424070358276, 0.24984024465084076, -0.210431307554245,
    0.17730562388896942, -0.13514360785484314, 0.0806083083152771, -0.031184406951069832,
    0.005619336850941181,
)
ACOS_HIGH = (
    0.4999392330646515, -0.3173876106739044, 0.24387668073177338, -0.18864932656288147,
    0.12859871983528137, -0.06701970100402832, 0.02248113788664341, -0.003529248759150505,
)

NN = (((1,), (0,)), ((), ()))
NT = (((1,), (1,)), ((), ()))


def mm(a, b, dims):
    return lax.dot_general(a, b, dims, preferred_element_type=F32)


def split2(x):
    hi = x.astype(BF)
    return hi, (x - hi.astype(F32)).astype(BF)


def split3(x):
    hi = x.astype(BF)
    rest = x - hi.astype(F32)
    mid = rest.astype(BF)
    return hi, mid, (rest - mid.astype(F32)).astype(BF)


def pick(onehot, x, dims, flip=False):
    parts = split3(x)
    prods = [mm(p, onehot, dims) if flip else mm(onehot, p, dims) for p in parts]
    return prods[0] + prods[1] + prods[2]


def full_nt(a, b):
    a1, a2, a3 = split3(a)
    b1, b2, b3 = split3(b)
    return (
        mm(a1, b1, NT) + (mm(a1, b2, NT) + mm(a2, b1, NT))
        + (mm(a2, b2, NT) + mm(a1, b3, NT) + mm(a3, b1, NT))
    )


def horner(coefs, x):
    acc = coefs[-1] * x + coefs[-2]
    for c in coefs[-3::-1]:
        acc = acc * x + c
    return acc


def ntk_over_scale(c):
    inv_pi = 1.0 / math.pi
    ntk = c
    for layer in range(3):
        w = jnp.maximum(1.0 - c * c, 1e-30)
        root = w * lax.rsqrt(w)
        arg = jnp.abs(c) if layer == 0 else c
        angle = root * horner(ACOS_HIGH if layer == 2 else ACOS_FULL, arg)
        remain = jnp.where(c < 0.0, angle, 1.0 - angle) if layer == 0 else 1.0 - angle
        if layer == 2:
            return root * inv_pi + remain * (c + ntk)
        c = root * inv_pi + remain * c
        ntk = c + ntk * remain


def rows_hot(index, width):
    n = index.shape[1]
    col = jnp.broadcast_to(index.astype(F32), (128, n)).T
    lane = lax.broadcasted_iota(jnp.int32, (n, 128), 1).astype(F32)
    return jnp.concatenate(
        [(col == lane + float(128 * k)).astype(BF) for k in range(width // 128)], axis=1
    )


def packed(x):
    half = x.shape[0] // 2
    return jnp.concatenate([x[:half], x[half:]], axis=1)


def unpacked(x):
    wide = x.shape[-1] // 2
    return jnp.concatenate([x[..., :wide], x[..., wide:]], axis=-2)


def front_body(member, *refs, tables):
    index_h, pool_f, pool_t, weights_h, centers, eig_h, owner_h, offset_h = refs[0:8]
    drawn, pack = refs[8:10]
    parts = refs[10 : 10 + tables]
    index, feats, targs, wts, eig, owner, offset, sems = refs[10 + tables :]
    cdev = centers.shape[0]
    copies = [
        pltpu.make_async_copy(src, dst, sems.at[n])
        for n, (src, dst) in enumerate(
            (
                (index_h, index), (pool_f, feats), (pool_t, targs), (weights_h, wts),
                (centers, pack.at[0:cdev, :]), (eig_h, eig), (owner_h, owner), (offset_h, offset),
            )
        )
    ]
    for copy in copies:
        copy.start()
    rows = index.shape[1]
    copies[0].wait()
    hot = rows_hot(index[...], feats.shape[0])
    copies[1].wait()
    drawn[0:rows, :] = pick(hot, feats[...], NN)
    copies[2].wait()
    drawn[rows:, :] = packed(pick(hot, targs[...], NT, flip=True).T)
    copies[3].wait()
    pack[cdev:, :] = packed(wts[...].T)
    for copy in copies[4:]:
        copy.wait()
    count, q = eig.shape
    part = q // tables
    row = jnp.broadcast_to((owner[...] * cdev + offset[...]).astype(F32), (8, count))
    row = jnp.concatenate([row] * (part // count), axis=1)
    for o, out in enumerate(parts):
        mate = member[0] ^ o
        out[0:count, :] = eig[:, pl.ds(pl.multiple_of(mate * part, part), part)]
        out[count:, :] = row


def order_body(x, *refs):
    parts, out = refs[:-1], refs[-1]
    for o, part in enumerate(parts):
        out[x[0] ^ o] = part[...]


def vectors_body(*refs, cdev):
    tables, send = refs[:-1], refs[-1]
    count, part = tables[0].shape[0] - 8, tables[0].shape[1]
    peers = send.shape[0]
    blocks, group, lanes = part // 128, CAP * len(tables), 128 // len(tables)
    earlier = lax.broadcasted_iota(jnp.int32, (count, count), 0) < lax.broadcasted_iota(
        jnp.int32, (count, count), 1
    )
    shared = []
    for t, table in enumerate(tables):
        nys = table[count : count + 1, 0:count].astype(jnp.int32)
        owner = nys // cdev
        offset = nys - owner * cdev
        row = jnp.broadcast_to(owner.astype(F32), (count, count))
        same = jnp.where(row.T == row, 1.0, 0.0)
        rank = jnp.sum(jnp.where(earlier, same, 0.0), axis=0, keepdims=True).astype(jnp.int32)
        place = owner * CAP + rank == lax.broadcasted_iota(jnp.int32, (peers * CAP, count), 0)
        offs = jnp.sum(jnp.where(place, offset.astype(F32), 0.0), axis=1, keepdims=True)
        shared.append(jnp.broadcast_to(offs, (peers * CAP, lanes)))
        vectors = pick(place.astype(BF), table[0:count, :], NN)
        for o in range(peers):
            own = slice(o * CAP, (o + 1) * CAP)
            for j in range(blocks):
                at = group * j + CAP * t
                send[o, at : at + CAP, :] = vectors[own, 128 * j : 128 * (j + 1)]
    shared = jnp.concatenate(shared, axis=1)
    for o in range(peers):
        send[o, group * blocks :, :] = shared[o * CAP : (o + 1) * CAP]


def kernel_body(*refs, nb, rows, sub, extra):
    own, mate = refs[0:2]
    packs = refs[2 : 2 + nb]
    khi, klo, keep, send = refs[2 + nb : 6 + nb]
    lhs, cen, wts, cos_a, cos_b, acc = refs[-6:]
    dim, count = own.shape[2], khi.shape[2]
    block = own.shape[0] * rows
    out = dim // 2
    for h, part in enumerate((own, mate)):
        f = part[:, 0:rows, :].reshape(block, dim)
        sa = jnp.sqrt(jnp.mean(f * f, axis=1, keepdims=True) + EPS)
        a1, a2, a3 = split3(f / sa)
        lhs[h] = jnp.concatenate([a1, a2, a1, a2, a1, a3], axis=1)
        if extra and h == 0:
            wide = jnp.broadcast_to(sa, (block, out)).reshape(own.shape[0], rows, out)
            half = rows // 2
            refs[6 + nb][...] = jnp.concatenate([wide[:, :half], wide[:, half:]], axis=2)
    for j, pack in enumerate(packs):
        b = pack[0:count, :]
        sb = jnp.sqrt(jnp.mean(b * b, axis=1, keepdims=True) + EPS)
        b1, b2, b3 = split3(b / sb * (1.0 / dim))
        cen[j] = jnp.concatenate([b1, b1, b2, b2, b3, b1], axis=1)
        w1, w2 = split2(unpacked(pack[count:, :]) * sb)
        wts[j] = jnp.concatenate([w1, w2], axis=1)
        if extra:
            nb_row = full_nt(jnp.ones((8, dim), F32), b * b) * (1.0 / dim) + EPS
            refs[7 + nb][...] = jnp.sqrt(nb_row)
    acc[...] = jnp.zeros(acc.shape, F32)

    def cosines(dst, j, h, n):
        at = slice(n * (count // 2), (n + 1) * (count // 2))
        dst[:, at] = mm(lhs[h], cen[j, at, :], NT)

    def elementwise(values, j, h, n):
        at = slice(h * block + n * sub, h * block + (n + 1) * sub)
        hi, lo = split2(ntk_over_scale(values[n * sub : (n + 1) * sub, :]))
        khi[j, at, :] = hi
        klo[j, at, :] = lo

    def predict(j, h):
        at = slice(h * block, (h + 1) * block)
        both = mm(khi[j, at, :], wts[j], NN) + mm(klo[j, at, :], wts[j], NN)
        acc[at, :] = acc[at, :] + both

    def step(j, h, now, later, after):
        elems = [functools.partial(elementwise, now, j, h, n) for n in range(block // sub)]
        others = [functools.partial(cosines, later, *after, n) for n in range(2)] if after else []
        if h == 1:
            others.append(functools.partial(predict, j, 0))
        every = len(elems) // 3
        for n, f in enumerate(elems):
            if n % every == 0 and others:
                others.pop(0)()
            f()

    for n in range(2):
        cosines(cos_a, 0, 0, n)
    if nb == 1:
        step(0, 0, cos_a, cos_b, (0, 1))
        step(0, 1, cos_b, cos_a, None)
        predict(0, 1)
    else:

        def pair(j, _):
            step(j, 0, cos_a, cos_b, (j, 1))
            step(j, 1, cos_b, cos_a, (jnp.minimum(j + 1, nb - 1), 0))
            predict(j, 1)
            return 0

        lax.fori_loop(0, nb, pair, 0)
    for h, dst in enumerate((keep, send)):
        total = acc[h * block : (h + 1) * block, :]
        total = (total[:, :out] + total[:, out:]).reshape(own.shape[0], 2, rows // 2, out)
        dst[...] = jnp.concatenate([total[:, 0], total[:, 1]], axis=2)


def residual_body(x, total, own, scale, resid, ready, value, *, rows, norm):
    value[...] = scale[...] * total[...] - own[:, rows:, :]
    resid[...] = unpacked(value[x[0]])
    ready[...] = value[...] * scale[...] * norm


def grads_body(own, mate, *refs):
    outs = refs[-4:]
    r = jnp.concatenate([unpacked(own[...]), unpacked(mate[...])], axis=0)
    out = r.shape[2]
    r1, r2 = split2(r.reshape(-1, out).T)
    rr = jnp.concatenate([r1, r2], axis=0)
    place = 0
    for khi, klo in zip(refs[0:-4:2], refs[1:-4:2]):
        for j in range(khi.shape[0]):
            both = mm(rr, khi[j], NN) + mm(rr, klo[j], NN)
            outs[place][...] = both[:out] + both[out:]
            place += 1


def block_of(points, j, tables):
    peers, group = points.shape[0], CAP * tables
    return points[:, group * j : group * (j + 1), :].reshape(peers * group, 128)


def points_hot(points, blocks, tables, width):
    peers, lanes = points.shape[0], 128 // tables
    offs = points[:, CAP * tables * blocks :, :]
    offs = jnp.concatenate(
        [
            jnp.broadcast_to(offs[:, :, lanes * t : lanes * t + 1], (peers, CAP, 128))
            for t in range(tables)
        ],
        axis=1,
    ).reshape(peers * CAP * tables, 128)
    lane = lax.broadcasted_iota(jnp.int32, offs.shape, 1).astype(F32)
    return jnp.concatenate(
        [(offs == lane + float(128 * k)).astype(BF) for k in range(width // 128)], axis=1
    )


def coeff_body(points, grads, coeff, *, tables):
    out, part = coeff.shape
    blocks = part // 128
    hot = points_hot(points, blocks, tables, grads.shape[1])
    g1, g2 = split2(pick(hot, grads[...], NT, flip=True))
    gg = jnp.concatenate([g1, g2], axis=0)
    for j in range(blocks):
        e1, e2 = split2(block_of(points, j, tables))
        both = mm(gg, e1, NN) + mm(gg, e2, NN)
        coeff[:, 128 * j : 128 * (j + 1)] = both[:out] + both[out:]


def corr_body(member, points, coeff, eig_scale, corr, *, tables):
    out, part = coeff.shape
    blocks = part // 128
    hot = points_hot(points, blocks, tables, corr.shape[1])
    total = jnp.zeros((2 * out, hot.shape[0]), F32)
    for j in range(blocks):
        at = slice(128 * j, 128 * (j + 1))
        e1, e2 = split2(block_of(points, j, tables))
        scale = eig_scale[:, pl.ds(pl.multiple_of(member[0] * part + 128 * j, 128), 128)]
        c1, c2 = split2(coeff[:, at] * scale)
        cc = jnp.concatenate([c1, c2], axis=0)
        total = total + mm(cc, e1, NT) + mm(cc, e2, NT)
    corr[...] = pick(hot, total[:out] + total[out:], NN, flip=True)


def shape(*dims, dtype=F32):
    return jax.ShapeDtypeStruct(dims, dtype)


def params(mib=16):
    return pltpu.CompilerParams(vmem_limit_bytes=mib << 20)


def call(body, outs, *args, mib=16, scalars=0, **kw):
    many = isinstance(outs, (list, tuple))
    smem = pl.BlockSpec(memory_space=pltpu.SMEM)
    return pl.pallas_call(
        body,
        out_shape=outs,
        in_specs=[smem] * scalars + [VMEM] * (len(args) - scalars),
        out_specs=[VMEM] * len(outs) if many else VMEM,
        compiler_params=params(mib),
        **kw,
    )(*args)


def exchange(v, axes):
    return functools.reduce(jnp.add, [v] + mates([v] * math.prod(SIZES[a] for a in axes), axes))


def mates(parts, axes):
    return [mate_of(parts[o], axes, o) for o in range(1, len(parts))]


def mate_of(v, axes, o):
    n = math.prod(SIZES[a] for a in axes)
    return lax.ppermute(v, axes, [(i, i ^ o) for i in range(n)])


def together(*arrays):
    return lax.optimization_barrier(arrays)


def per_device(
    pool_features, pool_targets, batch_index, centers, weights,
    eig_vectors, eig_scale, nys_owner, nys_offset,
):
    rows, dim = batch_index.shape[0], pool_features.shape[1]
    nx, ny, half = SIZES["x"], SIZES["y"], rows // 2
    cdev, out = weights.shape
    count, q = eig_vectors.shape
    tables = math.prod(SIZES[a] for a in PLANES)
    peers = math.prod(SIZES[a] for a in OWNERS)
    norm = 1.0 / math.sqrt(rows * math.prod(SIZES[a] for a in ALL))
    x = lax.axis_index("x").astype(jnp.int32)[None]
    member = lax.axis_index(PLANES).astype(jnp.int32)[None]
    straight = lax.axis_index("core") == lax.axis_index("zl")
    wide = 2 * out

    hbm = pl.BlockSpec(memory_space=pltpu.HBM)
    drawn, pack, *parted = pl.pallas_call(
        functools.partial(front_body, tables=tables),
        out_shape=[shape(rows + half, dim), shape(cdev + cdev // 2, dim)]
        + [shape(count + 8, q // tables)] * tables,
        in_specs=[pl.BlockSpec(memory_space=pltpu.SMEM)] + [hbm] * 8,
        out_specs=[VMEM] * (2 + tables),
        scratch_shapes=[
            pltpu.VMEM((1, rows), jnp.int32),
            pltpu.VMEM(pool_features.shape, F32),
            pltpu.VMEM(pool_targets.shape[::-1], F32),
            pltpu.VMEM((out, cdev), F32),
            pltpu.VMEM(eig_vectors.shape, F32),
            pltpu.VMEM((1, count), jnp.int32),
            pltpu.VMEM((1, count), jnp.int32),
            pltpu.SemaphoreType.DMA((8,)),
        ],
        compiler_params=params(16),
    )(
        member,
        *(
            pltpu.with_memory_space_constraint(v, pltpu.HBM)
            for v in (
                batch_index.reshape(1, rows), pool_features, pool_targets.T, weights.T, centers,
                eig_vectors, nys_owner.reshape(1, count), nys_offset.reshape(1, count),
            )
        ),
    )

    gathered = mates([drawn] * nx, ("x",))
    tile = lax.ppermute(pack, ("core", "zl"), [(0, 0), (2, 1), (1, 2), (3, 3)])
    first = mate_of(parted[2], PLANES, 2)
    tile, first, drawn, *gathered = together(tile, first, drawn, *gathered)
    own = call(order_body, shape(nx, rows + half, dim), x, drawn, *gathered, scalars=1)
    others = mates([tile] * ny, ("y",))
    mate = mate_of(own, ("core",), 1)
    mate, second, third = together(mate, parted[1], parted[3])
    parted = [parted[0], first, mate_of(second, PLANES, 1), mate_of(third, PLANES, 3)]

    def kernel(packs, extra):
        nb = len(packs)
        outs = [shape(nb, 2 * nx * rows, cdev, dtype=BF)] * 2 + [shape(nx, half, wide)] * 2
        if extra:
            outs = outs + [shape(nx, half, wide), shape(8, cdev)]
        return call(
            functools.partial(kernel_body, nb=nb, rows=rows, sub=32, extra=extra),
            outs, own, mate, *packs,
            scratch_shapes=[
                pltpu.VMEM((2, nx * rows, 6 * dim), BF),
                pltpu.VMEM((nb, cdev, 6 * dim), BF),
                pltpu.VMEM((nb, cdev, wide), BF),
                pltpu.VMEM((nx * rows, cdev), F32),
                pltpu.VMEM((nx * rows, cdev), F32),
                pltpu.VMEM((2 * nx * rows, wide), F32),
            ],
            cost_estimate=pl.CostEstimate(
                flops=100_000_000 if extra else 10_000_000_000 * nb, bytes_accessed=1 << 16, transcendentals=0
            ),
        )

    khi_a, klo_a, keep_a, send_a, scale, sb = kernel([tile], True)

    keep_a, *parted = together(keep_a, *parted)
    points = call(
        functools.partial(vectors_body, cdev=cdev),
        shape(peers, CAP * (tables * (q // tables // 128) + 1), 128),
        *parted,
    )
    points = lax.all_to_all(points, OWNERS, split_axis=0, concat_axis=0, tiled=True)

    khi_b, klo_b, keep_b, send_b = kernel(others, False)

    (got,) = mates([send_a + send_b] * 2, ("core",))
    total = exchange(keep_a + keep_b + got, ("x",))
    resid, ready = call(
        functools.partial(residual_body, rows=rows, norm=norm),
        [shape(rows, out), shape(nx, half, wide)],
        x, total, own, scale,
        scalars=1, scratch_shapes=[pltpu.VMEM((nx, half, wide), F32)],
    )
    (ready_mate,) = mates([ready] * 2, ("core",))

    parts = call(
        grads_body, [shape(out, cdev)] * 4, ready, ready_mate, khi_a, klo_a, khi_b, klo_b
    )
    grads = functools.reduce(jnp.add, mates(parts, ("y",)), parts[0]) * sb[0:1]
    points, grads = together(points, grads)
    grads = exchange(grads, PLANES)
    coeff = call(
        functools.partial(coeff_body, tables=tables), shape(out, q // tables), points, grads
    )
    for axis in OWNERS[::-1]:
        coeff = exchange(coeff, (axis,))
    corr = call(
        functools.partial(corr_body, tables=tables),
        shape(out, cdev), member, points, coeff, eig_scale[None, :],
        scalars=1,
    )
    update = exchange(corr, PLANES) - grads
    (swapped,) = mates([update] * 2, ("core",))
    return resid, jnp.where(straight, update, swapped).T


def solution(mesh):
    fine = Mesh(mesh.devices.reshape(tuple(SIZES[a] for a in ALL)), ALL)
    placed = (
        P(ALL, None),
        P(ALL, None),
        P(ALL),
        P(CENTERS, None),
        P(CENTERS, None),
        P(ALL, None),
        P(),
        P(ALL, None),
        P(ALL),
    )
    return jax.shard_map(
        per_device,
        mesh=fine,
        in_specs=placed,
        out_specs=(P(ALL, None), P(CENTERS, None)),
        check_vma=False,
    )
```

```python
import functools
import math

import jax
import jax.numpy as jnp
from jax import lax
from jax.experimental import pallas as pl
from jax.experimental.pallas import tpu as pltpu
from jax.sharding import Mesh, PartitionSpec as P

EPS = 1e-06
CAP = 8
BF = jnp.bfloat16
F32 = jnp.float32
SIZES = {"zh": 2, "core": 2, "x": 4, "y": 4, "zl": 2}
ALL = ("zh", "core", "x", "y", "zl")
CENTERS = ("x", "y", "zl")
PLANES = ("zh", "zl")
OWNERS = ("x", "y", "core")
VMEM = pl.BlockSpec(memory_space=pltpu.VMEM)

ACOS_FULL = (
    0.49999988079071045, -0.3182917535305023, 0.24954961240291595, -0.20787927508354187,
    0.1663874238729477, -0.10994759202003479, 0.04858129099011421, -0.01009112037718296,
)
ACOS_HIGH = (
    0.4998512864112854, -0.3162611424922943, 0.2378545105457306, -0.17122769355773926,
    0.09912680834533784, -0.03783833235502243, 0.006804656237363815,
)

NN = (((1,), (0,)), ((), ()))
NT = (((1,), (1,)), ((), ()))


def mm(a, b, dims):
    return lax.dot_general(a, b, dims, preferred_element_type=F32)


def split2(x):
    hi = x.astype(BF)
    return hi, (x - hi.astype(F32)).astype(BF)


def split3(x):
    hi = x.astype(BF)
    rest = x - hi.astype(F32)
    mid = rest.astype(BF)
    return hi, mid, (rest - mid.astype(F32)).astype(BF)


def pick(onehot, x, dims, flip=False):
    parts = split3(x)
    prods = [mm(p, onehot, dims) if flip else mm(onehot, p, dims) for p in parts]
    return prods[0] + prods[1] + prods[2]


def full_nt(a, b):
    a1, a2, a3 = split3(a)
    b1, b2, b3 = split3(b)
    return (
        mm(a1, b1, NT) + (mm(a1, b2, NT) + mm(a2, b1, NT))
        + (mm(a2, b2, NT) + mm(a1, b3, NT) + mm(a3, b1, NT))
    )


def horner(coefs, x):
    acc = coefs[-1] * x + coefs[-2]
    for c in coefs[-3::-1]:
        acc = acc * x + c
    return acc


def ntk_over_scale(c):
    inv_pi = 1.0 / math.pi
    ntk = c
    for layer in range(3):
        w = jnp.maximum(1.0 - c * c, 1e-30)
        root = w * lax.rsqrt(w)
        arg = jnp.abs(c) if layer == 0 else c
        angle = root * horner(ACOS_HIGH if layer == 2 else ACOS_FULL, arg)
        remain = jnp.where(c < 0.0, angle, 1.0 - angle) if layer == 0 else 1.0 - angle
        if layer == 2:
            return root * inv_pi + remain * (c + ntk)
        c = root * inv_pi + remain * c
        ntk = c + ntk * remain


def rows_hot(index, width):
    n = index.shape[1]
    col = jnp.broadcast_to(index.astype(F32), (128, n)).T
    lane = lax.broadcasted_iota(jnp.int32, (n, 128), 1).astype(F32)
    return jnp.concatenate(
        [(col == lane + float(128 * k)).astype(BF) for k in range(width // 128)], axis=1
    )


def packed(x):
    half = x.shape[0] // 2
    return jnp.concatenate([x[:half], x[half:]], axis=1)


def unpacked(x):
    wide = x.shape[-1] // 2
    return jnp.concatenate([x[..., :wide], x[..., wide:]], axis=-2)


def front_body(member, *refs, tables):
    index_h, pool_f, pool_t, weights_h, centers, eig_h, owner_h, offset_h = refs[0:8]
    drawn, pack = refs[8:10]
    parts = refs[10 : 10 + tables]
    index, feats, targs, wts, eig, owner, offset, sems = refs[10 + tables :]
    cdev = centers.shape[0]
    copies = [
        pltpu.make_async_copy(src, dst, sems.at[n])
        for n, (src, dst) in enumerate(
            (
                (index_h, index), (pool_f, feats), (pool_t, targs), (weights_h, wts),
                (centers, pack.at[0:cdev, :]), (eig_h, eig), (owner_h, owner), (offset_h, offset),
            )
        )
    ]
    for copy in copies:
        copy.start()
    rows = index.shape[1]
    copies[0].wait()
    hot = rows_hot(index[...], feats.shape[0])
    copies[1].wait()
    drawn[0:rows, :] = pick(hot, feats[...], NN)
    copies[2].wait()
    drawn[rows:, :] = packed(pick(hot, targs[...], NT, flip=True).T)
    copies[3].wait()
    pack[cdev:, :] = packed(wts[...].T)
    for copy in copies[4:]:
        copy.wait()
    count, q = eig.shape
    part = q // tables
    row = jnp.broadcast_to((owner[...] * cdev + offset[...]).astype(F32), (8, count))
    row = jnp.concatenate([row] * (part // count), axis=1)
    for o, out in enumerate(parts):
        mate = member[0] ^ o
        out[0:count, :] = eig[:, pl.ds(pl.multiple_of(mate * part, part), part)]
        out[count:, :] = row


def order_body(x, *refs):
    parts, out = refs[:-1], refs[-1]
    for o, part in enumerate(parts):
        out[x[0] ^ o] = part[...]


def vectors_body(*refs, cdev):
    tables, send = refs[:-1], refs[-1]
    count, part = tables[0].shape[0] - 8, tables[0].shape[1]
    peers = send.shape[0]
    blocks, group, lanes = part // 128, CAP * len(tables), 128 // len(tables)
    earlier = lax.broadcasted_iota(jnp.int32, (count, count), 0) < lax.broadcasted_iota(
        jnp.int32, (count, count), 1
    )
    shared = []
    for t, table in enumerate(tables):
        nys = table[count : count + 1, 0:count].astype(jnp.int32)
        owner = nys // cdev
        offset = nys - owner * cdev
        row = jnp.broadcast_to(owner.astype(F32), (count, count))
        same = jnp.where(row.T == row, 1.0, 0.0)
        rank = jnp.sum(jnp.where(earlier, same, 0.0), axis=0, keepdims=True).astype(jnp.int32)
        place = owner * CAP + rank == lax.broadcasted_iota(jnp.int32, (peers * CAP, count), 0)
        offs = jnp.sum(jnp.where(place, offset.astype(F32), 0.0), axis=1, keepdims=True)
        shared.append(jnp.broadcast_to(offs, (peers * CAP, lanes)))
        vectors = pick(place.astype(BF), table[0:count, :], NN)
        for o in range(peers):
            own = slice(o * CAP, (o + 1) * CAP)
            for j in range(blocks):
                at = group * j + CAP * t
                send[o, at : at + CAP, :] = vectors[own, 128 * j : 128 * (j + 1)]
    shared = jnp.concatenate(shared, axis=1)
    for o in range(peers):
        send[o, group * blocks :, :] = shared[o * CAP : (o + 1) * CAP]


def kernel_body(*refs, nb, rows, sub, extra):
    own, mate = refs[0:2]
    packs = refs[2 : 2 + nb]
    khi, klo, keep, send = refs[2 + nb : 6 + nb]
    lhs, cen, wts, cos_a, cos_b, acc = refs[-6:]
    dim, count = own.shape[2], khi.shape[2]
    block = own.shape[0] * rows
    out = dim // 2
    for h, part in enumerate((own, mate)):
        f = part[:, 0:rows, :].reshape(block, dim)
        sa = jnp.sqrt(jnp.mean(f * f, axis=1, keepdims=True) + EPS)
        a1, a2, a3 = split3(f / sa)
        lhs[h] = jnp.concatenate([a1, a2, a1, a2, a1, a3], axis=1)
        if extra and h == 0:
            wide = jnp.broadcast_to(sa, (block, out)).reshape(own.shape[0], rows, out)
            half = rows // 2
            refs[6 + nb][...] = jnp.concatenate([wide[:, :half], wide[:, half:]], axis=2)
    for j, pack in enumerate(packs):
        b = pack[0:count, :]
        sb = jnp.sqrt(jnp.mean(b * b, axis=1, keepdims=True) + EPS)
        b1, b2, b3 = split3(b / sb * (1.0 / dim))
        cen[j] = jnp.concatenate([b1, b1, b2, b2, b3, b1], axis=1)
        w1, w2 = split2(unpacked(pack[count:, :]) * sb)
        wts[j] = jnp.concatenate([w1, w2], axis=1)
        if extra:
            nb_row = full_nt(jnp.ones((8, dim), F32), b * b) * (1.0 / dim) + EPS
            refs[7 + nb][...] = jnp.sqrt(nb_row)
    acc[...] = jnp.zeros(acc.shape, F32)

    def cosines(dst, j, h, n):
        at = slice(n * (count // 2), (n + 1) * (count // 2))
        dst[:, at] = mm(lhs[h], cen[j, at, :], NT)

    def elementwise(values, j, h, n):
        at = slice(h * block + n * sub, h * block + (n + 1) * sub)
        hi, lo = split2(ntk_over_scale(values[n * sub : (n + 1) * sub, :]))
        khi[j, at, :] = hi
        klo[j, at, :] = lo

    def predict(j, h):
        at = slice(h * block, (h + 1) * block)
        both = mm(khi[j, at, :], wts[j], NN) + mm(klo[j, at, :], wts[j], NN)
        acc[at, :] = acc[at, :] + both

    def step(j, h, now, later, after):
        elems = [functools.partial(elementwise, now, j, h, n) for n in range(block // sub)]
        others = [functools.partial(cosines, later, *after, n) for n in range(2)] if after else []
        if h == 1:
            others.append(functools.partial(predict, j, 0))
        every = len(elems) // 3
        for n, f in enumerate(elems):
            if n % every == 0 and others:
                others.pop(0)()
            f()

    for n in range(2):
        cosines(cos_a, 0, 0, n)
    if nb == 1:
        step(0, 0, cos_a, cos_b, (0, 1))
        step(0, 1, cos_b, cos_a, None)
        predict(0, 1)
    else:

        def pair(j, _):
            step(j, 0, cos_a, cos_b, (j, 1))
            step(j, 1, cos_b, cos_a, (jnp.minimum(j + 1, nb - 1), 0))
            predict(j, 1)
            return 0

        lax.fori_loop(0, nb, pair, 0)
    for h, dst in enumerate((keep, send)):
        total = acc[h * block : (h + 1) * block, :]
        total = (total[:, :out] + total[:, out:]).reshape(own.shape[0], 2, rows // 2, out)
        dst[...] = jnp.concatenate([total[:, 0], total[:, 1]], axis=2)


def residual_body(x, total, own, scale, resid, ready, value, *, rows, norm):
    value[...] = scale[...] * total[...] - own[:, rows:, :]
    resid[...] = unpacked(value[x[0]])
    ready[...] = value[...] * scale[...] * norm


def grads_body(own, mate, *refs):
    outs = refs[-4:]
    r = jnp.concatenate([unpacked(own[...]), unpacked(mate[...])], axis=0)
    out = r.shape[2]
    r1, r2 = split2(r.reshape(-1, out).T)
    rr = jnp.concatenate([r1, r2], axis=0)
    place = 0
    for khi, klo in zip(refs[0:-4:2], refs[1:-4:2]):
        for j in range(khi.shape[0]):
            both = mm(rr, khi[j], NN) + mm(rr, klo[j], NN)
            outs[place][...] = both[:out] + both[out:]
            place += 1


def block_of(points, j, tables):
    peers, group = points.shape[0], CAP * tables
    return points[:, group * j : group * (j + 1), :].reshape(peers * group, 128)


def points_hot(points, blocks, tables, width):
    peers, lanes = points.shape[0], 128 // tables
    offs = points[:, CAP * tables * blocks :, :]
    offs = jnp.concatenate(
        [
            jnp.broadcast_to(offs[:, :, lanes * t : lanes * t + 1], (peers, CAP, 128))
            for t in range(tables)
        ],
        axis=1,
    ).reshape(peers * CAP * tables, 128)
    lane = lax.broadcasted_iota(jnp.int32, offs.shape, 1).astype(F32)
    return jnp.concatenate(
        [(offs == lane + float(128 * k)).astype(BF) for k in range(width // 128)], axis=1
    )


def coeff_body(points, grads, coeff, *, tables):
    out, part = coeff.shape
    blocks = part // 128
    hot = points_hot(points, blocks, tables, grads.shape[1])
    g1, g2 = split2(pick(hot, grads[...], NT, flip=True))
    gg = jnp.concatenate([g1, g2], axis=0)
    for j in range(blocks):
        e1, e2 = split2(block_of(points, j, tables))
        both = mm(gg, e1, NN) + mm(gg, e2, NN)
        coeff[:, 128 * j : 128 * (j + 1)] = both[:out] + both[out:]


def corr_body(member, points, coeff, eig_scale, corr, *, tables):
    out, part = coeff.shape
    blocks = part // 128
    hot = points_hot(points, blocks, tables, corr.shape[1])
    total = jnp.zeros((2 * out, hot.shape[0]), F32)
    for j in range(blocks):
        at = slice(128 * j, 128 * (j + 1))
        e1, e2 = split2(block_of(points, j, tables))
        scale = eig_scale[:, pl.ds(pl.multiple_of(member[0] * part + 128 * j, 128), 128)]
        c1, c2 = split2(coeff[:, at] * scale)
        cc = jnp.concatenate([c1, c2], axis=0)
        total = total + mm(cc, e1, NT) + mm(cc, e2, NT)
    corr[...] = pick(hot, total[:out] + total[out:], NN, flip=True)


def shape(*dims, dtype=F32):
    return jax.ShapeDtypeStruct(dims, dtype)


def params(mib=16):
    return pltpu.CompilerParams(vmem_limit_bytes=mib << 20)


def call(body, outs, *args, mib=16, scalars=0, **kw):
    many = isinstance(outs, (list, tuple))
    smem = pl.BlockSpec(memory_space=pltpu.SMEM)
    return pl.pallas_call(
        body,
        out_shape=outs,
        in_specs=[smem] * scalars + [VMEM] * (len(args) - scalars),
        out_specs=[VMEM] * len(outs) if many else VMEM,
        compiler_params=params(mib),
        **kw,
    )(*args)


def exchange(v, axes):
    return add_up([v] * math.prod(SIZES[a] for a in axes), axes)


def mates(parts, axes):
    return [mate_of(parts[o], axes, o) for o in range(1, len(parts))]


def add_up(parts, axes):
    order = sorted(range(1, len(parts)), key=lambda o: o != 2)
    return functools.reduce(jnp.add, [mate_of(parts[o], axes, o) for o in order], parts[0])


def mate_of(v, axes, o):
    n = math.prod(SIZES[a] for a in axes)
    return lax.ppermute(v, axes, [(i, i ^ o) for i in range(n)])


def together(*arrays):
    return lax.optimization_barrier(arrays)


def per_device(
    pool_features, pool_targets, batch_index, centers, weights,
    eig_vectors, eig_scale, nys_owner, nys_offset,
):
    rows, dim = batch_index.shape[0], pool_features.shape[1]
    nx, ny, half = SIZES["x"], SIZES["y"], rows // 2
    cdev, out = weights.shape
    count, q = eig_vectors.shape
    tables = math.prod(SIZES[a] for a in PLANES)
    peers = math.prod(SIZES[a] for a in OWNERS)
    norm = 1.0 / math.sqrt(rows * math.prod(SIZES[a] for a in ALL))
    x = lax.axis_index("x").astype(jnp.int32)[None]
    member = lax.axis_index(PLANES).astype(jnp.int32)[None]
    straight = lax.axis_index("core") == lax.axis_index("zl")
    wide = 2 * out

    hbm = pl.BlockSpec(memory_space=pltpu.HBM)
    drawn, pack, *parted = pl.pallas_call(
        functools.partial(front_body, tables=tables),
        out_shape=[shape(rows + half, dim), shape(cdev + cdev // 2, dim)]
        + [shape(count + 8, q // tables)] * tables,
        in_specs=[pl.BlockSpec(memory_space=pltpu.SMEM)] + [hbm] * 8,
        out_specs=[VMEM] * (2 + tables),
        scratch_shapes=[
            pltpu.VMEM((1, rows), jnp.int32),
            pltpu.VMEM(pool_features.shape, F32),
            pltpu.VMEM(pool_targets.shape[::-1], F32),
            pltpu.VMEM((out, cdev), F32),
            pltpu.VMEM(eig_vectors.shape, F32),
            pltpu.VMEM((1, count), jnp.int32),
            pltpu.VMEM((1, count), jnp.int32),
            pltpu.SemaphoreType.DMA((8,)),
        ],
        compiler_params=params(16),
    )(
        member,
        *(
            pltpu.with_memory_space_constraint(v, pltpu.HBM)
            for v in (
                batch_index.reshape(1, rows), pool_features, pool_targets.T, weights.T, centers,
                eig_vectors, nys_owner.reshape(1, count), nys_offset.reshape(1, count),
            )
        ),
    )

    gathered = mates([drawn] * nx, ("x",))
    tile = lax.ppermute(pack, ("core", "zl"), [(0, 0), (2, 1), (1, 2), (3, 3)])
    first = mate_of(parted[2], PLANES, 2)
    tile, first, drawn, *gathered = together(tile, first, drawn, *gathered)
    own = call(order_body, shape(nx, rows + half, dim), x, drawn, *gathered, scalars=1)
    others = mates([tile] * ny, ("y",))
    mate = mate_of(own, ("core",), 1)
    mate, second, third = together(mate, parted[1], parted[3])
    parted = [parted[0], first, mate_of(second, PLANES, 1), mate_of(third, PLANES, 3)]

    def kernel(packs, extra):
        nb = len(packs)
        outs = [shape(nb, 2 * nx * rows, cdev, dtype=BF)] * 2 + [shape(nx, half, wide)] * 2
        if extra:
            outs = outs + [shape(nx, half, wide), shape(8, cdev)]
        return call(
            functools.partial(kernel_body, nb=nb, rows=rows, sub=32, extra=extra),
            outs, own, mate, *packs,
            scratch_shapes=[
                pltpu.VMEM((2, nx * rows, 6 * dim), BF),
                pltpu.VMEM((nb, cdev, 6 * dim), BF),
                pltpu.VMEM((nb, cdev, wide), BF),
                pltpu.VMEM((nx * rows, cdev), F32),
                pltpu.VMEM((nx * rows, cdev), F32),
                pltpu.VMEM((2 * nx * rows, wide), F32),
            ],
            cost_estimate=pl.CostEstimate(
                flops=100_000_000 if extra else 10_000_000_000 * nb, bytes_accessed=1 << 16, transcendentals=0
            ),
        )

    khi_a, klo_a, keep_a, send_a, scale, sb = kernel([tile], True)

    keep_a, *parted = together(keep_a, *parted)
    points = call(
        functools.partial(vectors_body, cdev=cdev),
        shape(peers, CAP * (tables * (q // tables // 128) + 1), 128),
        *parted,
    )
    points = lax.all_to_all(points, OWNERS, split_axis=0, concat_axis=0, tiled=True)

    khi_b, klo_b, keep_b, send_b = kernel(others, False)

    (got,) = mates([send_a + send_b] * 2, ("core",))
    total = exchange(keep_a + keep_b + got, ("x",))
    resid, ready = call(
        functools.partial(residual_body, rows=rows, norm=norm),
        [shape(rows, out), shape(nx, half, wide)],
        x, total, own, scale,
        scalars=1, scratch_shapes=[pltpu.VMEM((nx, half, wide), F32)],
    )
    (ready_mate,) = mates([ready] * 2, ("core",))

    parts = call(
        grads_body, [shape(out, cdev)] * 4, ready, ready_mate, khi_a, klo_a, khi_b, klo_b
    )
    grads = add_up(parts, ("y",)) * sb[0:1]
    points, grads = together(points, grads)
    grads = exchange(grads, PLANES)
    coeff = call(
        functools.partial(coeff_body, tables=tables), shape(out, q // tables), points, grads
    )
    for axis in OWNERS[::-1]:
        coeff = exchange(coeff, (axis,))
    corr = call(
        functools.partial(corr_body, tables=tables),
        shape(out, cdev), member, points, coeff, eig_scale[None, :],
        scalars=1,
    )
    update = exchange(corr, PLANES) - grads
    (swapped,) = mates([update] * 2, ("core",))
    return resid, jnp.where(straight, update, swapped).T


def solution(mesh):
    fine = Mesh(mesh.devices.reshape(tuple(SIZES[a] for a in ALL)), ALL)
    placed = (
        P(ALL, None),
        P(ALL, None),
        P(ALL),
        P(CENTERS, None),
        P(CENTERS, None),
        P(ALL, None),
        P(),
        P(ALL, None),
        P(ALL),
    )
    return jax.shard_map(
        per_device,
        mesh=fine,
        in_specs=placed,
        out_specs=(P(ALL, None), P(CENTERS, None)),
        check_vma=False,
    )
```

```python
import functools
import math

import jax
import jax.numpy as jnp
from jax import lax
from jax.experimental import pallas as pl
from jax.experimental.pallas import tpu as pltpu
from jax.sharding import Mesh, PartitionSpec as P

EPS = 1e-06
CAP = 8
BF = jnp.bfloat16
F32 = jnp.float32
SIZES = {"zh": 2, "core": 2, "x": 4, "y": 4, "zl": 2}
ALL = ("zh", "core", "x", "y", "zl")
CENTERS = ("x", "y", "zl")
PLANES = ("zh", "zl")
TILES = (0, 1, 3, 2)
OWNERS = ("x", "y", "core")
VMEM = pl.BlockSpec(memory_space=pltpu.VMEM)

ACOS_FULL = (
    0.49999988079071045, -0.3182917535305023, 0.24954961240291595, -0.20787927508354187,
    0.1663874238729477, -0.10994759202003479, 0.04858129099011421, -0.01009112037718296,
)
ACOS_HIGH = (
    0.4998512864112854, -0.3162611424922943, 0.2378545105457306, -0.17122769355773926,
    0.09912680834533784, -0.03783833235502243, 0.006804656237363815,
)

NN = (((1,), (0,)), ((), ()))
NT = (((1,), (1,)), ((), ()))


def mm(a, b, dims):
    return lax.dot_general(a, b, dims, preferred_element_type=F32)


def split2(x):
    hi = x.astype(BF)
    return hi, (x - hi.astype(F32)).astype(BF)


def split3(x):
    hi = x.astype(BF)
    rest = x - hi.astype(F32)
    mid = rest.astype(BF)
    return hi, mid, (rest - mid.astype(F32)).astype(BF)


def pick(onehot, x, dims, flip=False):
    parts = split3(x)
    prods = [mm(p, onehot, dims) if flip else mm(onehot, p, dims) for p in parts]
    return prods[0] + prods[1] + prods[2]


def full_nt(a, b):
    a1, a2, a3 = split3(a)
    b1, b2, b3 = split3(b)
    return (
        mm(a1, b1, NT) + (mm(a1, b2, NT) + mm(a2, b1, NT))
        + (mm(a2, b2, NT) + mm(a1, b3, NT) + mm(a3, b1, NT))
    )


def horner(coefs, x):
    acc = coefs[-1] * x + coefs[-2]
    for c in coefs[-3::-1]:
        acc = acc * x + c
    return acc


def ntk_over_scale(c):
    inv_pi = 1.0 / math.pi
    ntk = c
    for layer in range(3):
        w = jnp.maximum(1.0 - c * c, 1e-30)
        root = w * lax.rsqrt(w)
        arg = jnp.abs(c) if layer == 0 else c
        angle = root * horner(ACOS_HIGH if layer == 2 else ACOS_FULL, arg)
        remain = jnp.where(c < 0.0, angle, 1.0 - angle) if layer == 0 else 1.0 - angle
        if layer == 2:
            return root * inv_pi + remain * (c + ntk)
        c = root * inv_pi + remain * c
        ntk = c + ntk * remain


def rows_hot(index, width):
    n = index.shape[1]
    col = jnp.broadcast_to(index.astype(F32), (128, n)).T
    lane = lax.broadcasted_iota(jnp.int32, (n, 128), 1).astype(F32)
    return jnp.concatenate(
        [(col == lane + float(128 * k)).astype(BF) for k in range(width // 128)], axis=1
    )


def packed(x):
    half = x.shape[0] // 2
    return jnp.concatenate([x[:half], x[half:]], axis=1)


def unpacked(x):
    wide = x.shape[-1] // 2
    return jnp.concatenate([x[..., :wide], x[..., wide:]], axis=-2)


def front_body(member, *refs, tables):
    index_h, pool_f, pool_t, weights_h, centers, eig_h, owner_h, offset_h = refs[0:8]
    drawn, pack = refs[8:10]
    parts = refs[10 : 10 + tables]
    index, feats, targs, wts, eig, owner, offset, sems = refs[10 + tables :]
    cdev = centers.shape[0]
    copies = [
        pltpu.make_async_copy(src, dst, sems.at[n])
        for n, (src, dst) in enumerate(
            (
                (index_h, index), (pool_f, feats), (pool_t, targs), (weights_h, wts),
                (centers, pack.at[0:cdev, :]), (eig_h, eig), (owner_h, owner), (offset_h, offset),
            )
        )
    ]
    for copy in copies:
        copy.start()
    rows = index.shape[1]
    copies[0].wait()
    hot = rows_hot(index[...], feats.shape[0])
    copies[1].wait()
    drawn[0:rows, :] = pick(hot, feats[...], NN)
    copies[2].wait()
    drawn[rows:, :] = packed(pick(hot, targs[...], NT, flip=True).T)
    copies[3].wait()
    pack[cdev:, :] = packed(wts[...].T)
    for copy in copies[4:]:
        copy.wait()
    count, q = eig.shape
    part = q // tables
    row = jnp.broadcast_to((owner[...] * cdev + offset[...]).astype(F32), (8, count))
    row = jnp.concatenate([row] * (part // count), axis=1)
    for o, out in enumerate(parts):
        mate = member[0] ^ o
        out[0:count, :] = eig[:, pl.ds(pl.multiple_of(mate * part, part), part)]
        out[count:, :] = row


def order_body(x, *refs, offsets):
    parts, out = refs[:-1], refs[-1]
    for o, part in zip(offsets, parts):
        out[x[0] ^ o] = part[...]


def vectors_body(*refs, cdev):
    tables, send = refs[:-1], refs[-1]
    count, part = tables[0].shape[0] - 8, tables[0].shape[1]
    peers = send.shape[0]
    blocks, group, lanes = part // 128, CAP * len(tables), 128 // len(tables)
    earlier = lax.broadcasted_iota(jnp.int32, (count, count), 0) < lax.broadcasted_iota(
        jnp.int32, (count, count), 1
    )
    shared = []
    for t, table in enumerate(tables):
        nys = table[count : count + 1, 0:count].astype(jnp.int32)
        owner = nys // cdev
        offset = nys - owner * cdev
        row = jnp.broadcast_to(owner.astype(F32), (count, count))
        same = jnp.where(row.T == row, 1.0, 0.0)
        rank = jnp.sum(jnp.where(earlier, same, 0.0), axis=0, keepdims=True).astype(jnp.int32)
        place = owner * CAP + rank == lax.broadcasted_iota(jnp.int32, (peers * CAP, count), 0)
        offs = jnp.sum(jnp.where(place, offset.astype(F32), 0.0), axis=1, keepdims=True)
        shared.append(jnp.broadcast_to(offs, (peers * CAP, lanes)))
        vectors = pick(place.astype(BF), table[0:count, :], NN)
        for o in range(peers):
            own = slice(o * CAP, (o + 1) * CAP)
            for j in range(blocks):
                at = group * j + CAP * t
                send[o, at : at + CAP, :] = vectors[own, 128 * j : 128 * (j + 1)]
    shared = jnp.concatenate(shared, axis=1)
    for o in range(peers):
        send[o, group * blocks :, :] = shared[o * CAP : (o + 1) * CAP]


def kernel_body(*refs, nb, rows, sub, extra):
    own, mate = refs[0:2]
    packs = refs[2 : 2 + nb]
    khi, klo, keep, send = refs[2 + nb : 6 + nb]
    lhs, cen, wts, cos_a, cos_b, acc = refs[-6:]
    dim, count = own.shape[2], khi.shape[2]
    block = own.shape[0] * rows
    out = dim // 2
    for h, part in enumerate((own, mate)):
        f = part[:, 0:rows, :].reshape(block, dim)
        sa = jnp.sqrt(jnp.mean(f * f, axis=1, keepdims=True) + EPS)
        a1, a2, a3 = split3(f / sa)
        lhs[h] = jnp.concatenate([a1, a2, a1, a2, a1, a3], axis=1)
        if extra and h == 0:
            wide = jnp.broadcast_to(sa, (block, out)).reshape(own.shape[0], rows, out)
            half = rows // 2
            refs[6 + nb][...] = jnp.concatenate([wide[:, :half], wide[:, half:]], axis=2)
    for j, pack in enumerate(packs):
        b = pack[0:count, :]
        sb = jnp.sqrt(jnp.mean(b * b, axis=1, keepdims=True) + EPS)
        b1, b2, b3 = split3(b / sb * (1.0 / dim))
        cen[j] = jnp.concatenate([b1, b1, b2, b2, b3, b1], axis=1)
        w1, w2 = split2(unpacked(pack[count:, :]) * sb)
        wts[j] = jnp.concatenate([w1, w2], axis=1)
        if extra:
            nb_row = full_nt(jnp.ones((8, dim), F32), b * b) * (1.0 / dim) + EPS
            refs[7 + nb][...] = jnp.sqrt(nb_row)
    acc[...] = jnp.zeros(acc.shape, F32)

    def cosines(dst, j, h, n):
        at = slice(n * (count // 2), (n + 1) * (count // 2))
        dst[:, at] = mm(lhs[h], cen[j, at, :], NT)

    def elementwise(values, j, h, n):
        at = slice(h * block + n * sub, h * block + (n + 1) * sub)
        hi, lo = split2(ntk_over_scale(values[n * sub : (n + 1) * sub, :]))
        khi[j, at, :] = hi
        klo[j, at, :] = lo

    def predict(j, h):
        at = slice(h * block, (h + 1) * block)
        both = mm(khi[j, at, :], wts[j], NN) + mm(klo[j, at, :], wts[j], NN)
        acc[at, :] = acc[at, :] + both

    def step(j, h, now, later, after):
        elems = [functools.partial(elementwise, now, j, h, n) for n in range(block // sub)]
        others = [functools.partial(cosines, later, *after, n) for n in range(2)] if after else []
        if h == 1:
            others.append(functools.partial(predict, j, 0))
        every = len(elems) // 3
        for n, f in enumerate(elems):
            if n % every == 0 and others:
                others.pop(0)()
            f()

    for n in range(2):
        cosines(cos_a, 0, 0, n)
    if nb == 1:
        step(0, 0, cos_a, cos_b, (0, 1))
        step(0, 1, cos_b, cos_a, None)
        predict(0, 1)
    else:

        def pair(j, _):
            step(j, 0, cos_a, cos_b, (j, 1))
            step(j, 1, cos_b, cos_a, (jnp.minimum(j + 1, nb - 1), 0))
            predict(j, 1)
            return 0

        lax.fori_loop(0, nb, pair, 0)
    for h, dst in enumerate((keep, send)):
        total = acc[h * block : (h + 1) * block, :]
        total = (total[:, :out] + total[:, out:]).reshape(own.shape[0], 2, rows // 2, out)
        dst[...] = jnp.concatenate([total[:, 0], total[:, 1]], axis=2)


def residual_body(x, total, own, scale, resid, ready, value, *, rows, norm):
    value[...] = scale[...] * total[...] - own[:, rows:, :]
    resid[...] = unpacked(value[x[0]])
    ready[...] = value[...] * scale[...] * norm


def grads_body(own, mate, *refs):
    outs = refs[-4:]
    r = jnp.concatenate([unpacked(own[...]), unpacked(mate[...])], axis=0)
    out = r.shape[2]
    r1, r2 = split2(r.reshape(-1, out).T)
    rr = jnp.concatenate([r1, r2], axis=0)
    place = 0
    for khi, klo in zip(refs[0:-4:2], refs[1:-4:2]):
        for j in range(khi.shape[0]):
            both = mm(rr, khi[j], NN) + mm(rr, klo[j], NN)
            outs[place][...] = both[:out] + both[out:]
            place += 1


def block_of(points, j, tables):
    peers, group = points.shape[0], CAP * tables
    return points[:, group * j : group * (j + 1), :].reshape(peers * group, 128)


def points_hot(points, blocks, tables, width):
    peers, lanes = points.shape[0], 128 // tables
    offs = points[:, CAP * tables * blocks :, :]
    offs = jnp.concatenate(
        [
            jnp.broadcast_to(offs[:, :, lanes * t : lanes * t + 1], (peers, CAP, 128))
            for t in range(tables)
        ],
        axis=1,
    ).reshape(peers * CAP * tables, 128)
    lane = lax.broadcasted_iota(jnp.int32, offs.shape, 1).astype(F32)
    return jnp.concatenate(
        [(offs == lane + float(128 * k)).astype(BF) for k in range(width // 128)], axis=1
    )


def coeff_body(points, grads, coeff, *, tables):
    out, part = coeff.shape
    blocks = part // 128
    hot = points_hot(points, blocks, tables, grads.shape[1])
    g1, g2 = split2(pick(hot, grads[...], NT, flip=True))
    gg = jnp.concatenate([g1, g2], axis=0)
    for j in range(blocks):
        e1, e2 = split2(block_of(points, j, tables))
        both = mm(gg, e1, NN) + mm(gg, e2, NN)
        coeff[:, 128 * j : 128 * (j + 1)] = both[:out] + both[out:]


def corr_body(member, points, coeff, eig_scale, corr, *, tables):
    out, part = coeff.shape
    blocks = part // 128
    hot = points_hot(points, blocks, tables, corr.shape[1])
    total = jnp.zeros((2 * out, hot.shape[0]), F32)
    for j in range(blocks):
        at = slice(128 * j, 128 * (j + 1))
        e1, e2 = split2(block_of(points, j, tables))
        scale = eig_scale[:, pl.ds(pl.multiple_of(member[0] * part + 128 * j, 128), 128)]
        c1, c2 = split2(coeff[:, at] * scale)
        cc = jnp.concatenate([c1, c2], axis=0)
        total = total + mm(cc, e1, NT) + mm(cc, e2, NT)
    corr[...] = pick(hot, total[:out] + total[out:], NN, flip=True)


def shape(*dims, dtype=F32):
    return jax.ShapeDtypeStruct(dims, dtype)


def params(mib=16):
    return pltpu.CompilerParams(vmem_limit_bytes=mib << 20)


def call(body, outs, *args, mib=16, scalars=0, **kw):
    many = isinstance(outs, (list, tuple))
    smem = pl.BlockSpec(memory_space=pltpu.SMEM)
    return pl.pallas_call(
        body,
        out_shape=outs,
        in_specs=[smem] * scalars + [VMEM] * (len(args) - scalars),
        out_specs=[VMEM] * len(outs) if many else VMEM,
        compiler_params=params(mib),
        **kw,
    )(*args)


def exchange(v, axes):
    return add_up([v] * math.prod(SIZES[a] for a in axes), axes)


def mates(parts, axes):
    return [mate_of(parts[o], axes, o) for o in range(1, len(parts))]


def add_up(parts, axes):
    order = sorted(range(1, len(parts)), key=lambda o: o != 2)
    return functools.reduce(jnp.add, [mate_of(parts[o], axes, o) for o in order], parts[0])


def mate_of(v, axes, o):
    n = math.prod(SIZES[a] for a in axes)
    return lax.ppermute(v, axes, [(i, i ^ o) for i in range(n)])


def together(*arrays):
    return lax.optimization_barrier(arrays)


def per_device(
    pool_features, pool_targets, batch_index, centers, weights,
    eig_vectors, eig_scale, nys_owner, nys_offset,
):
    rows, dim = batch_index.shape[0], pool_features.shape[1]
    nx, ny, half = SIZES["x"], SIZES["y"], rows // 2
    cdev, out = weights.shape
    count, q = eig_vectors.shape
    tables = math.prod(SIZES[a] for a in PLANES)
    peers = math.prod(SIZES[a] for a in OWNERS)
    norm = 1.0 / math.sqrt(rows * math.prod(SIZES[a] for a in ALL))
    x = lax.axis_index("x").astype(jnp.int32)[None]
    member = lax.axis_index(PLANES).astype(jnp.int32)[None]
    straight = lax.axis_index("core") == lax.axis_index("zl")
    wide = 2 * out

    hbm = pl.BlockSpec(memory_space=pltpu.HBM)
    drawn, pack, *parted = pl.pallas_call(
        functools.partial(front_body, tables=tables),
        out_shape=[shape(rows + half, dim), shape(cdev + cdev // 2, dim)]
        + [shape(count + 8, q // tables)] * tables,
        in_specs=[pl.BlockSpec(memory_space=pltpu.SMEM)] + [hbm] * 8,
        out_specs=[VMEM] * (2 + tables),
        scratch_shapes=[
            pltpu.VMEM((1, rows), jnp.int32),
            pltpu.VMEM(pool_features.shape, F32),
            pltpu.VMEM(pool_targets.shape[::-1], F32),
            pltpu.VMEM((out, cdev), F32),
            pltpu.VMEM(eig_vectors.shape, F32),
            pltpu.VMEM((1, count), jnp.int32),
            pltpu.VMEM((1, count), jnp.int32),
            pltpu.SemaphoreType.DMA((8,)),
        ],
        compiler_params=params(16),
    )(
        member,
        *(
            pltpu.with_memory_space_constraint(v, pltpu.HBM)
            for v in (
                batch_index.reshape(1, rows), pool_features, pool_targets.T, weights.T, centers,
                eig_vectors, nys_owner.reshape(1, count), nys_offset.reshape(1, count),
            )
        ),
    )

    hops = (2, 1, 3)
    gathered = [mate_of(drawn, ("x",), o) for o in hops]
    tile = lax.ppermute(pack, ("core", "zl"), [(0, 0), (2, 1), (1, 2), (3, 3)])
    first = mate_of(parted[2], PLANES, 2)
    tile, first, drawn, *gathered = together(tile, first, drawn, *gathered)
    own = call(
        functools.partial(order_body, offsets=(0,) + hops),
        shape(nx, rows + half, dim), x, drawn, *gathered,
        scalars=1,
    )
    others = [mate_of(tile, ("y",), o) for o in TILES[1:]]
    mate = mate_of(own, ("core",), 1)
    mate, second, third = together(mate, parted[1], parted[3])
    parted = [parted[0], first, mate_of(second, PLANES, 1), mate_of(third, PLANES, 3)]

    def kernel(packs, extra):
        nb = len(packs)
        outs = [shape(nb, 2 * nx * rows, cdev, dtype=BF)] * 2 + [shape(nx, half, wide)] * 2
        if extra:
            outs = outs + [shape(nx, half, wide), shape(8, cdev)]
        return call(
            functools.partial(kernel_body, nb=nb, rows=rows, sub=32, extra=extra),
            outs, own, mate, *packs,
            scratch_shapes=[
                pltpu.VMEM((2, nx * rows, 6 * dim), BF),
                pltpu.VMEM((nb, cdev, 6 * dim), BF),
                pltpu.VMEM((nb, cdev, wide), BF),
                pltpu.VMEM((nx * rows, cdev), F32),
                pltpu.VMEM((nx * rows, cdev), F32),
                pltpu.VMEM((2 * nx * rows, wide), F32),
            ],
            cost_estimate=pl.CostEstimate(
                flops=100_000_000 if extra else 10_000_000_000 * nb, bytes_accessed=1 << 16, transcendentals=0
            ),
        )

    khi_a, klo_a, keep_a, send_a, scale, sb = kernel([tile], True)

    keep_a, *parted = together(keep_a, *parted)
    points = call(
        functools.partial(vectors_body, cdev=cdev),
        shape(peers, CAP * (tables * (q // tables // 128) + 1), 128),
        *parted,
    )
    points = lax.all_to_all(points, OWNERS, split_axis=0, concat_axis=0, tiled=True)

    khi_b, klo_b, keep_b, send_b = kernel(others, False)

    (got,) = mates([send_a + send_b] * 2, ("core",))
    total = exchange(keep_a + keep_b + got, ("x",))
    resid, ready = call(
        functools.partial(residual_body, rows=rows, norm=norm),
        [shape(rows, out), shape(nx, half, wide)],
        x, total, own, scale,
        scalars=1, scratch_shapes=[pltpu.VMEM((nx, half, wide), F32)],
    )
    (ready_mate,) = mates([ready] * 2, ("core",))

    parts = call(
        grads_body, [shape(out, cdev)] * 4, ready, ready_mate, khi_a, klo_a, khi_b, klo_b
    )
    parts = [parts[TILES.index(o)] for o in range(ny)]
    grads = add_up(parts, ("y",)) * sb[0:1]
    points, grads = together(points, grads)
    grads = exchange(grads, PLANES)
    coeff = call(
        functools.partial(coeff_body, tables=tables), shape(out, q // tables), points, grads
    )
    for axis in OWNERS[::-1]:
        coeff = exchange(coeff, (axis,))
    corr = call(
        functools.partial(corr_body, tables=tables),
        shape(out, cdev), member, points, coeff, eig_scale[None, :],
        scalars=1,
    )
    update = exchange(corr, PLANES) - grads
    (swapped,) = mates([update] * 2, ("core",))
    return resid, jnp.where(straight, update, swapped).T


def solution(mesh):
    fine = Mesh(mesh.devices.reshape(tuple(SIZES[a] for a in ALL)), ALL)
    placed = (
        P(ALL, None),
        P(ALL, None),
        P(ALL),
        P(CENTERS, None),
        P(CENTERS, None),
        P(ALL, None),
        P(),
        P(ALL, None),
        P(ALL),
    )
    return jax.shard_map(
        per_device,
        mesh=fine,
        in_specs=placed,
        out_specs=(P(ALL, None), P(CENTERS, None)),
        check_vma=False,
    )
```

```python
import functools
import math

import jax
import jax.numpy as jnp
from jax import lax
from jax.experimental import pallas as pl
from jax.experimental.pallas import tpu as pltpu
from jax.sharding import Mesh, PartitionSpec as P

EPS = 1e-06
CAP = 8
BF = jnp.bfloat16
F32 = jnp.float32
SIZES = {"zh": 2, "core": 2, "x": 4, "y": 4, "zl": 2}
ALL = ("zh", "core", "x", "y", "zl")
CENTERS = ("x", "y", "zl")
PLANES = ("zh", "zl")
TILES = (0, 1, 3, 2)
OWNERS = ("x", "y", "core")
VMEM = pl.BlockSpec(memory_space=pltpu.VMEM)

ACOS_FULL = (
    0.49999988079071045, -0.3182917535305023, 0.24954961240291595, -0.20787927508354187,
    0.1663874238729477, -0.10994759202003479, 0.04858129099011421, -0.01009112037718296,
)
ACOS_HIGH = (
    0.4998512864112854, -0.3162611424922943, 0.2378545105457306, -0.17122769355773926,
    0.09912680834533784, -0.03783833235502243, 0.006804656237363815,
)

NN = (((1,), (0,)), ((), ()))
NT = (((1,), (1,)), ((), ()))


def mm(a, b, dims):
    return lax.dot_general(a, b, dims, preferred_element_type=F32)


def split2(x):
    hi = x.astype(BF)
    return hi, (x - hi.astype(F32)).astype(BF)


def split3(x):
    hi = x.astype(BF)
    rest = x - hi.astype(F32)
    mid = rest.astype(BF)
    return hi, mid, (rest - mid.astype(F32)).astype(BF)


def pick(onehot, x, dims, flip=False):
    parts = split3(x)
    prods = [mm(p, onehot, dims) if flip else mm(onehot, p, dims) for p in parts]
    return prods[0] + prods[1] + prods[2]


def full_nt(a, b):
    a1, a2, a3 = split3(a)
    b1, b2, b3 = split3(b)
    return (
        mm(a1, b1, NT) + (mm(a1, b2, NT) + mm(a2, b1, NT))
        + (mm(a2, b2, NT) + mm(a1, b3, NT) + mm(a3, b1, NT))
    )


def horner(coefs, x):
    acc = coefs[-1] * x + coefs[-2]
    for c in coefs[-3::-1]:
        acc = acc * x + c
    return acc


def ntk_over_scale(c):
    inv_pi = 1.0 / math.pi
    ntk = c
    for layer in range(3):
        w = jnp.maximum(1.0 - c * c, 1e-30)
        root = w * lax.rsqrt(w)
        arg = jnp.abs(c) if layer == 0 else c
        angle = root * horner(ACOS_HIGH if layer == 2 else ACOS_FULL, arg)
        remain = jnp.where(c < 0.0, angle, 1.0 - angle) if layer == 0 else 1.0 - angle
        if layer == 2:
            return root * inv_pi + remain * (c + ntk)
        c = root * inv_pi + remain * c
        ntk = c + ntk * remain


def rows_hot(index, width):
    n = index.shape[1]
    col = jnp.broadcast_to(index.astype(F32), (128, n)).T
    lane = lax.broadcasted_iota(jnp.int32, (n, 128), 1).astype(F32)
    return jnp.concatenate(
        [(col == lane + float(128 * k)).astype(BF) for k in range(width // 128)], axis=1
    )


def packed(x):
    half = x.shape[0] // 2
    return jnp.concatenate([x[:half], x[half:]], axis=1)


def unpacked(x):
    wide = x.shape[-1] // 2
    return jnp.concatenate([x[..., :wide], x[..., wide:]], axis=-2)


def front_body(member, *refs, tables):
    index_h, pool_f, pool_t, weights_h, centers, eig_h, owner_h, offset_h = refs[0:8]
    drawn, pack = refs[8:10]
    parts = refs[10 : 10 + tables]
    index, feats, targs, wts, eig, owner, offset, sems = refs[10 + tables :]
    cdev = centers.shape[0]
    copies = [
        pltpu.make_async_copy(src, dst, sems.at[n])
        for n, (src, dst) in enumerate(
            (
                (index_h, index), (pool_f, feats), (pool_t, targs), (weights_h, wts),
                (centers, pack.at[0:cdev, :]), (eig_h, eig), (owner_h, owner), (offset_h, offset),
            )
        )
    ]
    for copy in copies:
        copy.start()
    rows = index.shape[1]
    copies[0].wait()
    hot = rows_hot(index[...], feats.shape[0])
    copies[1].wait()
    drawn[0:rows, :] = pick(hot, feats[...], NN)
    copies[2].wait()
    drawn[rows:, :] = packed(pick(hot, targs[...], NT, flip=True).T)
    copies[3].wait()
    pack[cdev:, :] = packed(wts[...].T)
    for copy in copies[4:]:
        copy.wait()
    count, q = eig.shape
    part = q // tables
    row = jnp.broadcast_to((owner[...] * cdev + offset[...]).astype(F32), (8, count))
    row = jnp.concatenate([row] * (part // count), axis=1)
    for o, out in enumerate(parts):
        mate = member[0] ^ o
        out[0:count, :] = eig[:, pl.ds(pl.multiple_of(mate * part, part), part)]
        out[count:, :] = row


def order_body(x, *refs, offsets):
    parts, out = refs[:-1], refs[-1]
    for o, part in zip(offsets, parts):
        out[x[0] ^ o] = part[...]


def vectors_body(*refs, cdev):
    tables, send = refs[:-1], refs[-1]
    count, part = tables[0].shape[0] - 8, tables[0].shape[1]
    peers = send.shape[0]
    blocks, group, lanes = part // 128, CAP * len(tables), 128 // len(tables)
    earlier = lax.broadcasted_iota(jnp.int32, (count, count), 0) < lax.broadcasted_iota(
        jnp.int32, (count, count), 1
    )
    shared = []
    for t, table in enumerate(tables):
        nys = table[count : count + 1, 0:count].astype(jnp.int32)
        owner = nys // cdev
        offset = nys - owner * cdev
        row = jnp.broadcast_to(owner.astype(F32), (count, count))
        same = jnp.where(row.T == row, 1.0, 0.0)
        rank = jnp.sum(jnp.where(earlier, same, 0.0), axis=0, keepdims=True).astype(jnp.int32)
        place = owner * CAP + rank == lax.broadcasted_iota(jnp.int32, (peers * CAP, count), 0)
        offs = jnp.sum(jnp.where(place, offset.astype(F32), 0.0), axis=1, keepdims=True)
        shared.append(jnp.broadcast_to(offs, (peers * CAP, lanes)))
        vectors = pick(place.astype(BF), table[0:count, :], NN)
        for o in range(peers):
            own = slice(o * CAP, (o + 1) * CAP)
            for j in range(blocks):
                at = group * j + CAP * t
                send[o, at : at + CAP, :] = vectors[own, 128 * j : 128 * (j + 1)]
    shared = jnp.concatenate(shared, axis=1)
    for o in range(peers):
        send[o, group * blocks :, :] = shared[o * CAP : (o + 1) * CAP]


def kernel_body(*refs, nb, rows, sub, extra):
    own, mate = refs[0:2]
    packs = refs[2 : 2 + nb]
    khi, klo, keep, send = refs[2 + nb : 6 + nb]
    lhs, cen, wts, cos_a, cos_b, acc = refs[-6:]
    dim, count = own.shape[2], khi.shape[2]
    block = own.shape[0] * rows
    out = dim // 2
    for h, part in enumerate((own, mate)):
        f = part[:, 0:rows, :].reshape(block, dim)
        sa = jnp.sqrt(jnp.mean(f * f, axis=1, keepdims=True) + EPS)
        a1, a2, a3 = split3(f / sa)
        lhs[h] = jnp.concatenate([a1, a2, a1, a2, a1, a3], axis=1)
        if extra and h == 0:
            wide = jnp.broadcast_to(sa, (block, out)).reshape(own.shape[0], rows, out)
            half = rows // 2
            refs[6 + nb][...] = jnp.concatenate([wide[:, :half], wide[:, half:]], axis=2)
    for j, pack in enumerate(packs):
        b = pack[0:count, :]
        sb = jnp.sqrt(jnp.mean(b * b, axis=1, keepdims=True) + EPS)
        b1, b2, b3 = split3(b / sb * (1.0 / dim))
        cen[j] = jnp.concatenate([b1, b1, b2, b2, b3, b1], axis=1)
        w1, w2 = split2(unpacked(pack[count:, :]) * sb)
        wts[j] = jnp.concatenate([w1, w2], axis=1)
        if extra:
            nb_row = full_nt(jnp.ones((8, dim), F32), b * b) * (1.0 / dim) + EPS
            refs[7 + nb][...] = jnp.sqrt(nb_row)
    acc[...] = jnp.zeros(acc.shape, F32)

    def cosines(dst, j, h, n):
        at = slice(n * (count // 2), (n + 1) * (count // 2))
        dst[:, at] = mm(lhs[h], cen[j, at, :], NT)

    def elementwise(values, j, h, n):
        at = slice(h * block + n * sub, h * block + (n + 1) * sub)
        hi, lo = split2(ntk_over_scale(values[n * sub : (n + 1) * sub, :]))
        khi[j, at, :] = hi
        klo[j, at, :] = lo

    def predict(j, h):
        at = slice(h * block, (h + 1) * block)
        both = mm(khi[j, at, :], wts[j], NN) + mm(klo[j, at, :], wts[j], NN)
        acc[at, :] = acc[at, :] + both

    def step(j, h, now, later, after):
        elems = [functools.partial(elementwise, now, j, h, n) for n in range(block // sub)]
        others = [functools.partial(cosines, later, *after, n) for n in range(2)] if after else []
        if h == 1:
            others.append(functools.partial(predict, j, 0))
        every = len(elems) // 3
        for n, f in enumerate(elems):
            if n % every == 0 and others:
                others.pop(0)()
            f()

    for n in range(2):
        cosines(cos_a, 0, 0, n)
    if nb == 1:
        step(0, 0, cos_a, cos_b, (0, 1))
        step(0, 1, cos_b, cos_a, None)
        predict(0, 1)
    else:

        def pair(j, _):
            step(j, 0, cos_a, cos_b, (j, 1))
            step(j, 1, cos_b, cos_a, (jnp.minimum(j + 1, nb - 1), 0))
            predict(j, 1)
            return 0

        lax.fori_loop(0, nb, pair, 0)
    for h, dst in enumerate((keep, send)):
        total = acc[h * block : (h + 1) * block, :]
        total = (total[:, :out] + total[:, out:]).reshape(own.shape[0], 2, rows // 2, out)
        dst[...] = jnp.concatenate([total[:, 0], total[:, 1]], axis=2)


def residual_body(x, total, own, scale, resid, ready, value, *, rows, norm):
    value[...] = scale[...] * total[...] - own[:, rows:, :]
    resid[...] = unpacked(value[x[0]])
    ready[...] = value[...] * scale[...] * norm


def grads_body(own, mate, *refs):
    outs = refs[-4:]
    r = jnp.concatenate([unpacked(own[...]), unpacked(mate[...])], axis=0)
    out = r.shape[2]
    r1, r2 = split2(r.reshape(-1, out).T)
    rr = jnp.concatenate([r1, r2], axis=0)
    place = 0
    for khi, klo in zip(refs[0:-4:2], refs[1:-4:2]):
        for j in range(khi.shape[0]):
            both = mm(rr, khi[j], NN) + mm(rr, klo[j], NN)
            outs[place][...] = both[:out] + both[out:]
            place += 1


def block_of(points, j, tables):
    peers, group = points.shape[0], CAP * tables
    return points[:, group * j : group * (j + 1), :].reshape(peers * group, 128)


def gather_body(points, summed, *, tables):
    cdev, part = summed.shape[0], summed.shape[1] // 2
    blocks = part // 128
    peers, lanes = points.shape[0], 128 // tables
    offs = points[:, CAP * tables * blocks :, :]
    offs = jnp.concatenate(
        [
            jnp.broadcast_to(offs[:, :, lanes * t : lanes * t + 1], (peers, CAP, 128))
            for t in range(tables)
        ],
        axis=1,
    ).reshape(peers * CAP * tables, 128).T
    center = lax.broadcasted_iota(jnp.int32, offs.shape, 0).astype(F32)
    hot = jnp.concatenate(
        [(offs == center + float(128 * k)).astype(BF) for k in range(cdev // 128)], axis=0
    )
    for j in range(blocks):
        hi, lo = split2(pick(hot, block_of(points, j, tables), NN))
        summed[:, 128 * j : 128 * (j + 1)] = hi
        summed[:, part + 128 * j : part + 128 * (j + 1)] = lo


def coeff_body(summed, grads, coeff):
    out, part = coeff.shape
    g1, g2 = split2(grads[...])
    both = mm(jnp.concatenate([g1, g2], axis=0), summed[...], NN)
    both = both[:out] + both[out:]
    coeff[...] = both[:, :part] + both[:, part:]


def corr_body(member, summed, coeff, eig_scale, corr):
    out, part = coeff.shape
    scale = eig_scale[:, pl.ds(pl.multiple_of(member[0] * part, part), part)]
    c1, c2 = split2(coeff[...] * scale)
    cc = jnp.concatenate([c1, c2], axis=0)
    both = mm(cc, summed[:, :part], NT) + mm(cc, summed[:, part:], NT)
    corr[...] = both[:out] + both[out:]


def shape(*dims, dtype=F32):
    return jax.ShapeDtypeStruct(dims, dtype)


def params(mib=16):
    return pltpu.CompilerParams(vmem_limit_bytes=mib << 20)


def call(body, outs, *args, mib=16, scalars=0, **kw):
    many = isinstance(outs, (list, tuple))
    smem = pl.BlockSpec(memory_space=pltpu.SMEM)
    return pl.pallas_call(
        body,
        out_shape=outs,
        in_specs=[smem] * scalars + [VMEM] * (len(args) - scalars),
        out_specs=[VMEM] * len(outs) if many else VMEM,
        compiler_params=params(mib),
        **kw,
    )(*args)


def exchange(v, axes):
    return add_up([v] * math.prod(SIZES[a] for a in axes), axes)


def mates(parts, axes):
    return [mate_of(parts[o], axes, o) for o in range(1, len(parts))]


def add_up(parts, axes):
    order = sorted(range(1, len(parts)), key=lambda o: o != 2)
    return functools.reduce(jnp.add, [mate_of(parts[o], axes, o) for o in order], parts[0])


def mate_of(v, axes, o):
    n = math.prod(SIZES[a] for a in axes)
    return lax.ppermute(v, axes, [(i, i ^ o) for i in range(n)])


def together(*arrays):
    return lax.optimization_barrier(arrays)


def per_device(
    pool_features, pool_targets, batch_index, centers, weights,
    eig_vectors, eig_scale, nys_owner, nys_offset,
):
    rows, dim = batch_index.shape[0], pool_features.shape[1]
    nx, ny, half = SIZES["x"], SIZES["y"], rows // 2
    cdev, out = weights.shape
    count, q = eig_vectors.shape
    tables = math.prod(SIZES[a] for a in PLANES)
    peers = math.prod(SIZES[a] for a in OWNERS)
    norm = 1.0 / math.sqrt(rows * math.prod(SIZES[a] for a in ALL))
    x = lax.axis_index("x").astype(jnp.int32)[None]
    member = lax.axis_index(PLANES).astype(jnp.int32)[None]
    straight = lax.axis_index("core") == lax.axis_index("zl")
    wide = 2 * out

    hbm = pl.BlockSpec(memory_space=pltpu.HBM)
    drawn, pack, *parted = pl.pallas_call(
        functools.partial(front_body, tables=tables),
        out_shape=[shape(rows + half, dim), shape(cdev + cdev // 2, dim)]
        + [shape(count + 8, q // tables)] * tables,
        in_specs=[pl.BlockSpec(memory_space=pltpu.SMEM)] + [hbm] * 8,
        out_specs=[VMEM] * (2 + tables),
        scratch_shapes=[
            pltpu.VMEM((1, rows), jnp.int32),
            pltpu.VMEM(pool_features.shape, F32),
            pltpu.VMEM(pool_targets.shape[::-1], F32),
            pltpu.VMEM((out, cdev), F32),
            pltpu.VMEM(eig_vectors.shape, F32),
            pltpu.VMEM((1, count), jnp.int32),
            pltpu.VMEM((1, count), jnp.int32),
            pltpu.SemaphoreType.DMA((8,)),
        ],
        compiler_params=params(16),
    )(
        member,
        *(
            pltpu.with_memory_space_constraint(v, pltpu.HBM)
            for v in (
                batch_index.reshape(1, rows), pool_features, pool_targets.T, weights.T, centers,
                eig_vectors, nys_owner.reshape(1, count), nys_offset.reshape(1, count),
            )
        ),
    )

    hops = (2, 1, 3)
    gathered = [mate_of(drawn, ("x",), o) for o in hops]
    tile = lax.ppermute(pack, ("core", "zl"), [(0, 0), (2, 1), (1, 2), (3, 3)])
    first = mate_of(parted[2], PLANES, 2)
    tile, first, drawn, *gathered = together(tile, first, drawn, *gathered)
    own = call(
        functools.partial(order_body, offsets=(0,) + hops),
        shape(nx, rows + half, dim), x, drawn, *gathered,
        scalars=1,
    )
    others = [mate_of(tile, ("y",), o) for o in TILES[1:]]
    mate = mate_of(own, ("core",), 1)
    mate, second, third = together(mate, parted[1], parted[3])
    parted = [parted[0], first, mate_of(second, PLANES, 1), mate_of(third, PLANES, 3)]

    def kernel(packs, extra):
        nb = len(packs)
        outs = [shape(nb, 2 * nx * rows, cdev, dtype=BF)] * 2 + [shape(nx, half, wide)] * 2
        if extra:
            outs = outs + [shape(nx, half, wide), shape(8, cdev)]
        return call(
            functools.partial(kernel_body, nb=nb, rows=rows, sub=32, extra=extra),
            outs, own, mate, *packs,
            scratch_shapes=[
                pltpu.VMEM((2, nx * rows, 6 * dim), BF),
                pltpu.VMEM((nb, cdev, 6 * dim), BF),
                pltpu.VMEM((nb, cdev, wide), BF),
                pltpu.VMEM((nx * rows, cdev), F32),
                pltpu.VMEM((nx * rows, cdev), F32),
                pltpu.VMEM((2 * nx * rows, wide), F32),
            ],
            cost_estimate=pl.CostEstimate(
                flops=100_000_000 if extra else 10_000_000_000 * nb, bytes_accessed=1 << 16, transcendentals=0
            ),
        )

    khi_a, klo_a, keep_a, send_a, scale, sb = kernel([tile], True)

    keep_a, *parted = together(keep_a, *parted)
    points = call(
        functools.partial(vectors_body, cdev=cdev),
        shape(peers, CAP * (tables * (q // tables // 128) + 1), 128),
        *parted,
    )
    points = lax.all_to_all(points, OWNERS, split_axis=0, concat_axis=0, tiled=True)

    khi_b, klo_b, keep_b, send_b = kernel(others, False)

    (got,) = mates([send_a + send_b] * 2, ("core",))
    total = exchange(keep_a + keep_b + got, ("x",))
    resid, ready = call(
        functools.partial(residual_body, rows=rows, norm=norm),
        [shape(rows, out), shape(nx, half, wide)],
        x, total, own, scale,
        scalars=1, scratch_shapes=[pltpu.VMEM((nx, half, wide), F32)],
    )
    (ready_mate,) = mates([ready] * 2, ("core",))

    parts = call(
        grads_body, [shape(out, cdev)] * 4, ready, ready_mate, khi_a, klo_a, khi_b, klo_b
    )
    parts = [parts[TILES.index(o)] for o in range(ny)]
    grads = add_up(parts, ("y",)) * sb[0:1]
    points, grads = together(points, grads)
    summed = call(
        functools.partial(gather_body, tables=tables),
        shape(cdev, 2 * q // tables, dtype=BF), points,
        cost_estimate=pl.CostEstimate(
            flops=800_000_000, bytes_accessed=1 << 21, transcendentals=0
        ),
    )
    grads = exchange(grads, PLANES)
    coeff = call(coeff_body, shape(out, q // tables), summed, grads)
    for axis in OWNERS[::-1]:
        coeff = exchange(coeff, (axis,))
    corr = call(
        corr_body, shape(out, cdev), member, summed, coeff, eig_scale[None, :], scalars=1
    )
    update = exchange(corr, PLANES) - grads
    (swapped,) = mates([update] * 2, ("core",))
    return resid, jnp.where(straight, update, swapped).T


def solution(mesh):
    fine = Mesh(mesh.devices.reshape(tuple(SIZES[a] for a in ALL)), ALL)
    placed = (
        P(ALL, None),
        P(ALL, None),
        P(ALL),
        P(CENTERS, None),
        P(CENTERS, None),
        P(ALL, None),
        P(),
        P(ALL, None),
        P(ALL),
    )
    return jax.shard_map(
        per_device,
        mesh=fine,
        in_specs=placed,
        out_specs=(P(ALL, None), P(CENTERS, None)),
        check_vma=False,
    )
```

```python
import functools
import math

import jax
import jax.numpy as jnp
from jax import lax
from jax.experimental import pallas as pl
from jax.experimental.pallas import tpu as pltpu
from jax.sharding import Mesh, PartitionSpec as P

EPS = 1e-06
CAP = 8
BF = jnp.bfloat16
F32 = jnp.float32
SIZES = {"zh": 2, "core": 2, "x": 4, "y": 4, "zl": 2}
ALL = ("zh", "core", "x", "y", "zl")
CENTERS = ("x", "y", "zl")
PLANES = ("zh", "zl")
TILES = (0, 1, 3, 2)
OWNERS = ("x", "y", "core")
VMEM = pl.BlockSpec(memory_space=pltpu.VMEM)

ACOS_FULL = (
    0.49999988079071045, -0.3182917535305023, 0.24954961240291595, -0.20787927508354187,
    0.1663874238729477, -0.10994759202003479, 0.04858129099011421, -0.01009112037718296,
)
ACOS_HIGH = (
    0.4998512864112854, -0.3162611424922943, 0.2378545105457306, -0.17122769355773926,
    0.09912680834533784, -0.03783833235502243, 0.006804656237363815,
)

NN = (((1,), (0,)), ((), ()))
NT = (((1,), (1,)), ((), ()))


def mm(a, b, dims):
    return lax.dot_general(a, b, dims, preferred_element_type=F32)


def split2(x):
    hi = x.astype(BF)
    return hi, (x - hi.astype(F32)).astype(BF)


def split3(x):
    hi = x.astype(BF)
    rest = x - hi.astype(F32)
    mid = rest.astype(BF)
    return hi, mid, (rest - mid.astype(F32)).astype(BF)


def pick(onehot, x, dims, flip=False):
    parts = split3(x)
    prods = [mm(p, onehot, dims) if flip else mm(onehot, p, dims) for p in parts]
    return prods[0] + prods[1] + prods[2]


def full_nt(a, b):
    a1, a2, a3 = split3(a)
    b1, b2, b3 = split3(b)
    return (
        mm(a1, b1, NT) + (mm(a1, b2, NT) + mm(a2, b1, NT))
        + (mm(a2, b2, NT) + mm(a1, b3, NT) + mm(a3, b1, NT))
    )


def horner(coefs, x):
    acc = coefs[-1] * x + coefs[-2]
    for c in coefs[-3::-1]:
        acc = acc * x + c
    return acc


def ntk_over_scale(c):
    inv_pi = 1.0 / math.pi
    ntk = c
    for layer in range(3):
        w = jnp.maximum(1.0 - c * c, 1e-30)
        root = w * lax.rsqrt(w)
        arg = jnp.abs(c) if layer == 0 else c
        angle = root * horner(ACOS_HIGH if layer == 2 else ACOS_FULL, arg)
        remain = jnp.where(c < 0.0, angle, 1.0 - angle) if layer == 0 else 1.0 - angle
        if layer == 2:
            return root * inv_pi + remain * (c + ntk)
        c = root * inv_pi + remain * c
        ntk = c + ntk * remain


def rows_hot(index, width):
    n = index.shape[1]
    col = jnp.broadcast_to(index.astype(F32), (128, n)).T
    lane = lax.broadcasted_iota(jnp.int32, (n, 128), 1).astype(F32)
    return jnp.concatenate(
        [(col == lane + float(128 * k)).astype(BF) for k in range(width // 128)], axis=1
    )


def packed(x):
    half = x.shape[0] // 2
    return jnp.concatenate([x[:half], x[half:]], axis=1)


def unpacked(x):
    wide = x.shape[-1] // 2
    return jnp.concatenate([x[..., :wide], x[..., wide:]], axis=-2)


def front_body(member, *refs, tables):
    index_h, pool_f, pool_t, weights_h, centers, eig_h, owner_h, offset_h = refs[0:8]
    drawn, pack = refs[8:10]
    parts = refs[10 : 10 + tables]
    index, feats, targs, wts, eig, owner, offset, sems = refs[10 + tables :]
    cdev = centers.shape[0]
    copies = [
        pltpu.make_async_copy(src, dst, sems.at[n])
        for n, (src, dst) in enumerate(
            (
                (index_h, index), (pool_f, feats), (pool_t, targs), (weights_h, wts),
                (centers, pack.at[0:cdev, :]), (eig_h, eig), (owner_h, owner), (offset_h, offset),
            )
        )
    ]
    for copy in copies:
        copy.start()
    rows = index.shape[1]
    copies[0].wait()
    hot = rows_hot(index[...], feats.shape[0])
    copies[1].wait()
    drawn[0:rows, :] = pick(hot, feats[...], NN)
    copies[2].wait()
    drawn[rows:, :] = packed(pick(hot, targs[...], NT, flip=True).T)
    copies[3].wait()
    pack[cdev:, :] = packed(wts[...].T)
    for copy in copies[4:]:
        copy.wait()
    count, q = eig.shape
    part = q // tables
    row = jnp.broadcast_to((owner[...] * cdev + offset[...]).astype(F32), (8, count))
    row = jnp.concatenate([row] * (part // count), axis=1)
    for o, out in enumerate(parts):
        mate = member[0] ^ o
        out[0:count, :] = eig[:, pl.ds(pl.multiple_of(mate * part, part), part)]
        out[count:, :] = row


def order_body(x, *refs, offsets):
    parts, out = refs[:-1], refs[-1]
    for o, part in zip(offsets, parts):
        out[x[0] ^ o] = part[...]


def vectors_body(*refs, cdev):
    tables, send = refs[:-1], refs[-1]
    count, part = tables[0].shape[0] - 8, tables[0].shape[1]
    peers = send.shape[0]
    blocks, group, lanes = part // 128, CAP * len(tables), 128 // len(tables)
    earlier = lax.broadcasted_iota(jnp.int32, (count, count), 0) < lax.broadcasted_iota(
        jnp.int32, (count, count), 1
    )
    shared = []
    for t, table in enumerate(tables):
        nys = table[count : count + 1, 0:count].astype(jnp.int32)
        owner = nys // cdev
        offset = nys - owner * cdev
        row = jnp.broadcast_to(owner.astype(F32), (count, count))
        same = jnp.where(row.T == row, 1.0, 0.0)
        rank = jnp.sum(jnp.where(earlier, same, 0.0), axis=0, keepdims=True).astype(jnp.int32)
        place = owner * CAP + rank == lax.broadcasted_iota(jnp.int32, (peers * CAP, count), 0)
        offs = jnp.sum(jnp.where(place, offset.astype(F32), 0.0), axis=1, keepdims=True)
        shared.append(jnp.broadcast_to(offs, (peers * CAP, lanes)))
        vectors = pick(place.astype(BF), table[0:count, :], NN)
        for o in range(peers):
            own = slice(o * CAP, (o + 1) * CAP)
            for j in range(blocks):
                at = group * j + CAP * t
                send[o, at : at + CAP, :] = vectors[own, 128 * j : 128 * (j + 1)]
    shared = jnp.concatenate(shared, axis=1)
    for o in range(peers):
        send[o, group * blocks :, :] = shared[o * CAP : (o + 1) * CAP]


def kernel_body(*refs, nb, rows, sub, extra):
    own, mate = refs[0:2]
    packs = refs[2 : 2 + nb]
    khi, klo, keep, send = refs[2 + nb : 6 + nb]
    lhs, cen, wts, cos_a, cos_b, acc = refs[-6:]
    dim, count = own.shape[2], khi.shape[2]
    block = own.shape[0] * rows
    out = dim // 2
    for h, part in enumerate((own, mate)):
        f = part[:, 0:rows, :].reshape(block, dim)
        sa = jnp.sqrt(jnp.mean(f * f, axis=1, keepdims=True) + EPS)
        a1, a2, a3 = split3(f / sa)
        lhs[h] = jnp.concatenate([a1, a2, a1, a2, a1, a3], axis=1)
        if extra and h == 0:
            wide = jnp.broadcast_to(sa, (block, out)).reshape(own.shape[0], rows, out)
            half = rows // 2
            refs[6 + nb][...] = jnp.concatenate([wide[:, :half], wide[:, half:]], axis=2)
    for j, pack in enumerate(packs):
        b = pack[0:count, :]
        sb = jnp.sqrt(jnp.mean(b * b, axis=1, keepdims=True) + EPS)
        b1, b2, b3 = split3(b / sb * (1.0 / dim))
        cen[j] = jnp.concatenate([b1, b1, b2, b2, b3, b1], axis=1)
        w1, w2 = split2(unpacked(pack[count:, :]) * sb)
        wts[j] = jnp.concatenate([w1, w2], axis=1)
        if extra:
            nb_row = full_nt(jnp.ones((8, dim), F32), b * b) * (1.0 / dim) + EPS
            refs[7 + nb][...] = jnp.sqrt(nb_row)
    acc[...] = jnp.zeros(acc.shape, F32)

    def cosines(dst, j, h, n):
        at = slice(n * (count // 2), (n + 1) * (count // 2))
        dst[:, at] = mm(lhs[h], cen[j, at, :], NT)

    def elementwise(values, j, h, n):
        at = slice(h * block + n * sub, h * block + (n + 1) * sub)
        hi, lo = split2(ntk_over_scale(values[n * sub : (n + 1) * sub, :]))
        khi[j, at, :] = hi
        klo[j, at, :] = lo

    def predict(j, h):
        at = slice(h * block, (h + 1) * block)
        both = mm(khi[j, at, :], wts[j], NN) + mm(klo[j, at, :], wts[j], NN)
        acc[at, :] = acc[at, :] + both

    def step(j, h, now, later, after):
        elems = [functools.partial(elementwise, now, j, h, n) for n in range(block // sub)]
        others = [functools.partial(cosines, later, *after, n) for n in range(2)] if after else []
        if h == 1:
            others.append(functools.partial(predict, j, 0))
        every = len(elems) // 3
        for n, f in enumerate(elems):
            if n % every == 0 and others:
                others.pop(0)()
            f()

    for n in range(2):
        cosines(cos_a, 0, 0, n)
    if nb == 1:
        step(0, 0, cos_a, cos_b, (0, 1))
        step(0, 1, cos_b, cos_a, None)
        predict(0, 1)
    else:

        def pair(j, _):
            step(j, 0, cos_a, cos_b, (j, 1))
            step(j, 1, cos_b, cos_a, (jnp.minimum(j + 1, nb - 1), 0))
            predict(j, 1)
            return 0

        lax.fori_loop(0, nb, pair, 0)
    for h, dst in enumerate((keep, send)):
        total = acc[h * block : (h + 1) * block, :]
        total = (total[:, :out] + total[:, out:]).reshape(own.shape[0], 2, rows // 2, out)
        dst[...] = jnp.concatenate([total[:, 0], total[:, 1]], axis=2)


def residual_body(x, total, own, scale, resid, ready, value, *, rows, norm):
    value[...] = scale[...] * total[...] - own[:, rows:, :]
    resid[...] = unpacked(value[x[0]])
    ready[...] = value[...] * scale[...] * norm


def grads_body(own, mate, *refs):
    outs = refs[-4:]
    r = jnp.concatenate([unpacked(own[...]), unpacked(mate[...])], axis=0)
    out = r.shape[2]
    r1, r2 = split2(r.reshape(-1, out).T)
    rr = jnp.concatenate([r1, r2], axis=0)
    place = 0
    for khi, klo in zip(refs[0:-4:2], refs[1:-4:2]):
        for j in range(khi.shape[0]):
            both = mm(rr, khi[j], NN) + mm(rr, klo[j], NN)
            outs[place][...] = both[:out] + both[out:]
            place += 1


def block_of(points, j, tables):
    peers, group = points.shape[0], CAP * tables
    return points[:, group * j : group * (j + 1), :].reshape(peers * group, 128)


def gather_body(points, summed, *, tables):
    cdev, part = summed.shape[0], summed.shape[1] // 2
    blocks = part // 128
    peers, lanes = points.shape[0], 128 // tables
    offs = points[:, CAP * tables * blocks :, :]
    offs = jnp.concatenate(
        [
            jnp.broadcast_to(offs[:, :, lanes * t : lanes * t + 1], (peers, CAP, 128))
            for t in range(tables)
        ],
        axis=1,
    ).reshape(peers * CAP * tables, 128).T
    center = lax.broadcasted_iota(jnp.int32, offs.shape, 0).astype(F32)
    hot = jnp.concatenate(
        [(offs == center + float(128 * k)).astype(BF) for k in range(cdev // 128)], axis=0
    )
    for j in range(blocks):
        hi, lo = split2(pick(hot, block_of(points, j, tables), NN))
        summed[:, 128 * j : 128 * (j + 1)] = hi
        summed[:, part + 128 * j : part + 128 * (j + 1)] = lo


def coeff_body(summed, grads, coeff):
    out, part = coeff.shape
    g1, g2 = split2(grads[...])
    both = mm(jnp.concatenate([g1, g2], axis=0), summed[...], NN)
    both = both[:out] + both[out:]
    coeff[...] = both[:, :part] + both[:, part:]


def corr_body(member, summed, coeff, eig_scale, grads, corr):
    out, part = coeff.shape
    scale = eig_scale[:, pl.ds(pl.multiple_of(member[0] * part, part), part)]
    c1, c2 = split2(coeff[...] * scale)
    cc = jnp.concatenate([c1, c2], axis=0)
    both = mm(cc, summed[:, :part], NT) + mm(cc, summed[:, part:], NT)
    corr[...] = both[:out] + both[out:] - grads[...] * 0.25


def shape(*dims, dtype=F32):
    return jax.ShapeDtypeStruct(dims, dtype)


def params(mib=16):
    return pltpu.CompilerParams(vmem_limit_bytes=mib << 20)


def call(body, outs, *args, mib=16, scalars=0, **kw):
    many = isinstance(outs, (list, tuple))
    smem = pl.BlockSpec(memory_space=pltpu.SMEM)
    return pl.pallas_call(
        body,
        out_shape=outs,
        in_specs=[smem] * scalars + [VMEM] * (len(args) - scalars),
        out_specs=[VMEM] * len(outs) if many else VMEM,
        compiler_params=params(mib),
        **kw,
    )(*args)


def exchange(v, axes):
    return add_up([v] * math.prod(SIZES[a] for a in axes), axes)


def mates(parts, axes):
    return [mate_of(parts[o], axes, o) for o in range(1, len(parts))]


def add_up(parts, axes):
    order = sorted(range(1, len(parts)), key=lambda o: o != 2)
    return functools.reduce(jnp.add, [mate_of(parts[o], axes, o) for o in order], parts[0])


def mate_of(v, axes, o):
    n = math.prod(SIZES[a] for a in axes)
    return lax.ppermute(v, axes, [(i, i ^ o) for i in range(n)])


def together(*arrays):
    return lax.optimization_barrier(arrays)


def per_device(
    pool_features, pool_targets, batch_index, centers, weights,
    eig_vectors, eig_scale, nys_owner, nys_offset,
):
    rows, dim = batch_index.shape[0], pool_features.shape[1]
    nx, ny, half = SIZES["x"], SIZES["y"], rows // 2
    cdev, out = weights.shape
    count, q = eig_vectors.shape
    tables = math.prod(SIZES[a] for a in PLANES)
    peers = math.prod(SIZES[a] for a in OWNERS)
    norm = 1.0 / math.sqrt(rows * math.prod(SIZES[a] for a in ALL))
    x = lax.axis_index("x").astype(jnp.int32)[None]
    member = lax.axis_index(PLANES).astype(jnp.int32)[None]
    wide = 2 * out

    hbm = pl.BlockSpec(memory_space=pltpu.HBM)
    drawn, pack, *parted = pl.pallas_call(
        functools.partial(front_body, tables=tables),
        out_shape=[shape(rows + half, dim), shape(cdev + cdev // 2, dim)]
        + [shape(count + 8, q // tables)] * tables,
        in_specs=[pl.BlockSpec(memory_space=pltpu.SMEM)] + [hbm] * 8,
        out_specs=[VMEM] * (2 + tables),
        scratch_shapes=[
            pltpu.VMEM((1, rows), jnp.int32),
            pltpu.VMEM(pool_features.shape, F32),
            pltpu.VMEM(pool_targets.shape[::-1], F32),
            pltpu.VMEM((out, cdev), F32),
            pltpu.VMEM(eig_vectors.shape, F32),
            pltpu.VMEM((1, count), jnp.int32),
            pltpu.VMEM((1, count), jnp.int32),
            pltpu.SemaphoreType.DMA((8,)),
        ],
        compiler_params=params(16),
    )(
        member,
        *(
            pltpu.with_memory_space_constraint(v, pltpu.HBM)
            for v in (
                batch_index.reshape(1, rows), pool_features, pool_targets.T, weights.T, centers,
                eig_vectors, nys_owner.reshape(1, count), nys_offset.reshape(1, count),
            )
        ),
    )

    hops = (2, 1, 3)
    gathered = [mate_of(drawn, ("x",), o) for o in hops]
    tile = lax.ppermute(pack, ("core", "zl"), [(0, 0), (2, 1), (1, 2), (3, 3)])
    first = mate_of(parted[2], PLANES, 2)
    tile, first, drawn, *gathered = together(tile, first, drawn, *gathered)
    own = call(
        functools.partial(order_body, offsets=(0,) + hops),
        shape(nx, rows + half, dim), x, drawn, *gathered,
        scalars=1,
    )
    others = [mate_of(tile, ("y",), o) for o in TILES[1:]]
    mate = mate_of(own, ("core",), 1)
    mate, second, third = together(mate, parted[1], parted[3])
    parted = [parted[0], first, mate_of(second, PLANES, 1), mate_of(third, PLANES, 3)]

    def kernel(packs, extra):
        nb = len(packs)
        outs = [shape(nb, 2 * nx * rows, cdev, dtype=BF)] * 2 + [shape(nx, half, wide)] * 2
        if extra:
            outs = outs + [shape(nx, half, wide), shape(8, cdev)]
        return call(
            functools.partial(kernel_body, nb=nb, rows=rows, sub=32, extra=extra),
            outs, own, mate, *packs,
            scratch_shapes=[
                pltpu.VMEM((2, nx * rows, 6 * dim), BF),
                pltpu.VMEM((nb, cdev, 6 * dim), BF),
                pltpu.VMEM((nb, cdev, wide), BF),
                pltpu.VMEM((nx * rows, cdev), F32),
                pltpu.VMEM((nx * rows, cdev), F32),
                pltpu.VMEM((2 * nx * rows, wide), F32),
            ],
            cost_estimate=pl.CostEstimate(
                flops=100_000_000 if extra else 10_000_000_000 * nb, bytes_accessed=1 << 16, transcendentals=0
            ),
        )

    khi_a, klo_a, keep_a, send_a, scale, sb = kernel([tile], True)

    keep_a, *parted = together(keep_a, *parted)
    points = call(
        functools.partial(vectors_body, cdev=cdev),
        shape(peers, CAP * (tables * (q // tables // 128) + 1), 128),
        *parted,
    )
    points = lax.all_to_all(points, OWNERS, split_axis=0, concat_axis=0, tiled=True)

    khi_b, klo_b, keep_b, send_b = kernel(others, False)

    (got,) = mates([send_a + send_b] * 2, ("core",))
    total = exchange(keep_a + keep_b + got, ("x",))
    resid, ready = call(
        functools.partial(residual_body, rows=rows, norm=norm),
        [shape(rows, out), shape(nx, half, wide)],
        x, total, own, scale,
        scalars=1, scratch_shapes=[pltpu.VMEM((nx, half, wide), F32)],
    )
    (ready_mate,) = mates([ready] * 2, ("core",))

    parts = call(
        grads_body, [shape(out, cdev)] * 4, ready, ready_mate, khi_a, klo_a, khi_b, klo_b
    )
    parts = [parts[TILES.index(o)] for o in range(ny)]
    grads = add_up(parts, ("y",)) * sb[0:1]
    points, grads = together(points, grads)
    summed = call(
        functools.partial(gather_body, tables=tables),
        shape(cdev, 2 * q // tables, dtype=BF), points,
        cost_estimate=pl.CostEstimate(
            flops=800_000_000, bytes_accessed=1 << 21, transcendentals=0
        ),
    )
    grads = exchange(grads, PLANES)
    coeff = call(coeff_body, shape(out, q // tables), summed, grads)
    for axis in OWNERS[::-1]:
        coeff = exchange(coeff, (axis,))
    corr = call(
        corr_body, shape(out, cdev), member, summed, coeff, eig_scale[None, :], grads, scalars=1
    )
    received = []
    for r in (2, 3, 1, 0):
        perm = [
            ((z // 2) * 4 + k * 2 + z % 2, ((z ^ r) // 2) * 4 + ((z ^ r) % 2) * 2 + k)
            for k in range(2) for z in range(4)
        ]
        received.append(lax.ppermute(corr, ("zh", "core", "zl"), perm))
    return resid, functools.reduce(jnp.add, received).T


def solution(mesh):
    fine = Mesh(mesh.devices.reshape(tuple(SIZES[a] for a in ALL)), ALL)
    placed = (
        P(ALL, None),
        P(ALL, None),
        P(ALL),
        P(CENTERS, None),
        P(CENTERS, None),
        P(ALL, None),
        P(),
        P(ALL, None),
        P(ALL),
    )
    return jax.shard_map(
        per_device,
        mesh=fine,
        in_specs=placed,
        out_specs=(P(ALL, None), P(CENTERS, None)),
        check_vma=False,
    )
```

```python
import functools
import math

import jax
import jax.numpy as jnp
from jax import lax
from jax.experimental import pallas as pl
from jax.experimental.pallas import tpu as pltpu
from jax.sharding import Mesh, PartitionSpec as P

EPS = 1e-06
CAP = 8
BF = jnp.bfloat16
F32 = jnp.float32
SIZES = {"zh": 2, "core": 2, "x": 4, "y": 4, "zl": 2}
ALL = ("zh", "core", "x", "y", "zl")
CENTERS = ("x", "y", "zl")
PLANES = ("zh", "zl")
TILES = (0, 1, 3, 2)
OWNERS = ("x", "y", "core")
VMEM = pl.BlockSpec(memory_space=pltpu.VMEM)

ACOS_FULL = (
    0.49999988079071045, -0.3182917535305023, 0.24954961240291595, -0.20787927508354187,
    0.1663874238729477, -0.10994759202003479, 0.04858129099011421, -0.01009112037718296,
)
ACOS_HIGH = (
    0.4998512864112854, -0.3162611424922943, 0.2378545105457306, -0.17122769355773926,
    0.09912680834533784, -0.03783833235502243, 0.006804656237363815,
)

NN = (((1,), (0,)), ((), ()))
NT = (((1,), (1,)), ((), ()))


def mm(a, b, dims):
    return lax.dot_general(a, b, dims, preferred_element_type=F32)


def split2(x):
    hi = x.astype(BF)
    return hi, (x - hi.astype(F32)).astype(BF)


def split3(x):
    hi = x.astype(BF)
    rest = x - hi.astype(F32)
    mid = rest.astype(BF)
    return hi, mid, (rest - mid.astype(F32)).astype(BF)


def pick(onehot, x, dims, flip=False):
    parts = split3(x)
    prods = [mm(p, onehot, dims) if flip else mm(onehot, p, dims) for p in parts]
    return prods[0] + prods[1] + prods[2]


def full_nt(a, b):
    a1, a2, a3 = split3(a)
    b1, b2, b3 = split3(b)
    return (
        mm(a1, b1, NT) + (mm(a1, b2, NT) + mm(a2, b1, NT))
        + (mm(a2, b2, NT) + mm(a1, b3, NT) + mm(a3, b1, NT))
    )


def horner(coefs, x):
    acc = coefs[-1] * x + coefs[-2]
    for c in coefs[-3::-1]:
        acc = acc * x + c
    return acc


def ntk_over_scale(c):
    inv_pi = 1.0 / math.pi
    ntk = c
    for layer in range(3):
        w = jnp.maximum(1.0 - c * c, 1e-30)
        root = w * lax.rsqrt(w)
        arg = jnp.abs(c) if layer == 0 else c
        angle = root * horner(ACOS_HIGH if layer == 2 else ACOS_FULL, arg)
        remain = jnp.where(c < 0.0, angle, 1.0 - angle) if layer == 0 else 1.0 - angle
        if layer == 2:
            return root * inv_pi + remain * (c + ntk)
        c = root * inv_pi + remain * c
        ntk = c + ntk * remain


def rows_hot(index, width):
    n = index.shape[1]
    col = jnp.broadcast_to(index.astype(F32), (128, n)).T
    lane = lax.broadcasted_iota(jnp.int32, (n, 128), 1).astype(F32)
    return jnp.concatenate(
        [(col == lane + float(128 * k)).astype(BF) for k in range(width // 128)], axis=1
    )


def packed(x):
    half = x.shape[0] // 2
    return jnp.concatenate([x[:half], x[half:]], axis=1)


def unpacked(x):
    wide = x.shape[-1] // 2
    return jnp.concatenate([x[..., :wide], x[..., wide:]], axis=-2)


def front_body(member, *refs, tables):
    index_h, pool_f, pool_t, weights_h, centers, eig_h, owner_h, offset_h = refs[0:8]
    drawn, pack = refs[8:10]
    parts = refs[10 : 10 + tables]
    index, feats, targs, wts, eig, owner, offset, sems = refs[10 + tables :]
    cdev = centers.shape[0]
    copies = [
        pltpu.make_async_copy(src, dst, sems.at[n])
        for n, (src, dst) in enumerate(
            (
                (index_h, index), (pool_f, feats), (pool_t, targs), (weights_h, wts),
                (centers, pack.at[0:cdev, :]), (eig_h, eig), (owner_h, owner), (offset_h, offset),
            )
        )
    ]
    for copy in copies:
        copy.start()
    rows = index.shape[1]
    copies[0].wait()
    hot = rows_hot(index[...], feats.shape[0])
    copies[1].wait()
    drawn[0:rows, :] = pick(hot, feats[...], NN)
    copies[2].wait()
    drawn[rows:, :] = packed(pick(hot, targs[...], NT, flip=True).T)
    copies[3].wait()
    pack[cdev:, :] = packed(wts[...].T)
    for copy in copies[4:]:
        copy.wait()
    count, q = eig.shape
    part = q // tables
    row = jnp.broadcast_to((owner[...] * cdev + offset[...]).astype(F32), (8, count))
    row = jnp.concatenate([row] * (part // count), axis=1)
    for o, out in enumerate(parts):
        mate = member[0] ^ o
        out[0:count, :] = eig[:, pl.ds(pl.multiple_of(mate * part, part), part)]
        out[count:, :] = row


def order_body(x, *refs, offsets):
    parts, out = refs[:-1], refs[-1]
    for o, part in zip(offsets, parts):
        out[x[0] ^ o] = part[...]


def vectors_body(*refs, cdev):
    tables, send = refs[:-1], refs[-1]
    count, part = tables[0].shape[0] - 8, tables[0].shape[1]
    peers = send.shape[0]
    blocks, group, lanes = part // 128, CAP * len(tables), 128 // len(tables)
    earlier = lax.broadcasted_iota(jnp.int32, (count, count), 0) < lax.broadcasted_iota(
        jnp.int32, (count, count), 1
    )
    shared = []
    for t, table in enumerate(tables):
        nys = table[count : count + 1, 0:count].astype(jnp.int32)
        owner = nys // cdev
        offset = nys - owner * cdev
        row = jnp.broadcast_to(owner.astype(F32), (count, count))
        same = jnp.where(row.T == row, 1.0, 0.0)
        rank = jnp.sum(jnp.where(earlier, same, 0.0), axis=0, keepdims=True).astype(jnp.int32)
        place = owner * CAP + rank == lax.broadcasted_iota(jnp.int32, (peers * CAP, count), 0)
        offs = jnp.sum(jnp.where(place, offset.astype(F32), 0.0), axis=1, keepdims=True)
        shared.append(jnp.broadcast_to(offs, (peers * CAP, lanes)))
        vectors = pick(place.astype(BF), table[0:count, :], NN)
        for o in range(peers):
            own = slice(o * CAP, (o + 1) * CAP)
            for j in range(blocks):
                at = group * j + CAP * t
                send[o, at : at + CAP, :] = vectors[own, 128 * j : 128 * (j + 1)]
    shared = jnp.concatenate(shared, axis=1)
    for o in range(peers):
        send[o, group * blocks :, :] = shared[o * CAP : (o + 1) * CAP]


def kernel_body(*refs, nb, rows, sub, extra):
    own, mate = refs[0:2]
    packs = refs[2 : 2 + nb]
    khi, klo, keep, send = refs[2 + nb : 6 + nb]
    lhs, cen, wts, cos_a, cos_b, acc = refs[-6:]
    dim, count = own.shape[2], khi.shape[2]
    block = own.shape[0] * rows
    out = dim // 2
    for h, part in enumerate((own, mate)):
        f = part[:, 0:rows, :].reshape(block, dim)
        sa = jnp.sqrt(jnp.mean(f * f, axis=1, keepdims=True) + EPS)
        a1, a2, a3 = split3(f / sa)
        lhs[h] = jnp.concatenate([a1, a2, a1, a2, a1, a3], axis=1)
        if extra and h == 0:
            wide = jnp.broadcast_to(sa, (block, out)).reshape(own.shape[0], rows, out)
            half = rows // 2
            refs[6 + nb][...] = jnp.concatenate([wide[:, :half], wide[:, half:]], axis=2)
    for j, pack in enumerate(packs):
        b = pack[0:count, :]
        sb = jnp.sqrt(jnp.mean(b * b, axis=1, keepdims=True) + EPS)
        b1, b2, b3 = split3(b / sb * (1.0 / dim))
        cen[j] = jnp.concatenate([b1, b1, b2, b2, b3, b1], axis=1)
        w1, w2 = split2(unpacked(pack[count:, :]) * sb)
        wts[j] = jnp.concatenate([w1, w2], axis=1)
        if extra:
            nb_row = full_nt(jnp.ones((8, dim), F32), b * b) * (1.0 / dim) + EPS
            refs[7 + nb][...] = jnp.sqrt(nb_row)
    acc[...] = jnp.zeros(acc.shape, F32)

    def cosines(dst, j, h, n):
        at = slice(n * (count // 2), (n + 1) * (count // 2))
        dst[:, at] = mm(lhs[h], cen[j, at, :], NT)

    def elementwise(values, j, h, n):
        at = slice(h * block + n * sub, h * block + (n + 1) * sub)
        hi, lo = split2(ntk_over_scale(values[n * sub : (n + 1) * sub, :]))
        khi[j, at, :] = hi
        klo[j, at, :] = lo

    def predict(j, h):
        at = slice(h * block, (h + 1) * block)
        both = mm(khi[j, at, :], wts[j], NN) + mm(klo[j, at, :], wts[j], NN)
        acc[at, :] = acc[at, :] + both

    def step(j, h, now, later, after):
        elems = [functools.partial(elementwise, now, j, h, n) for n in range(block // sub)]
        others = [functools.partial(cosines, later, *after, n) for n in range(2)] if after else []
        if h == 1:
            others.append(functools.partial(predict, j, 0))
        every = len(elems) // 3
        for n, f in enumerate(elems):
            if n % every == 0 and others:
                others.pop(0)()
            f()

    for n in range(2):
        cosines(cos_a, 0, 0, n)
    if nb == 1:
        step(0, 0, cos_a, cos_b, (0, 1))
        step(0, 1, cos_b, cos_a, None)
        predict(0, 1)
    else:

        def pair(j, _):
            step(j, 0, cos_a, cos_b, (j, 1))
            step(j, 1, cos_b, cos_a, (jnp.minimum(j + 1, nb - 1), 0))
            predict(j, 1)
            return 0

        lax.fori_loop(0, nb, pair, 0)
    for h, dst in enumerate((keep, send)):
        total = acc[h * block : (h + 1) * block, :]
        total = (total[:, :out] + total[:, out:]).reshape(own.shape[0], 2, rows // 2, out)
        dst[...] = jnp.concatenate([total[:, 0], total[:, 1]], axis=2)


def residual_body(x, total, own, scale, resid, ready, value, *, rows, norm):
    value[...] = scale[...] * total[...] - own[:, rows:, :]
    resid[...] = unpacked(value[x[0]])
    ready[...] = value[...] * scale[...] * norm


def grads_body(own, mate, *refs):
    outs = refs[-4:]
    r = jnp.concatenate([unpacked(own[...]), unpacked(mate[...])], axis=0)
    out = r.shape[2]
    r1, r2 = split2(r.reshape(-1, out).T)
    rr = jnp.concatenate([r1, r2], axis=0)
    place = 0
    for khi, klo in zip(refs[0:-4:2], refs[1:-4:2]):
        for j in range(khi.shape[0]):
            both = mm(rr, khi[j], NN) + mm(rr, klo[j], NN)
            outs[place][...] = both[:out] + both[out:]
            place += 1


def block_of(points, j, tables):
    peers, group = points.shape[0], CAP * tables
    return points[:, group * j : group * (j + 1), :].reshape(peers * group, 128)


def gather_body(points, summed, *, tables):
    cdev, part = summed.shape[0], summed.shape[1] // 2
    blocks = part // 128
    peers, lanes = points.shape[0], 128 // tables
    offs = points[:, CAP * tables * blocks :, :]
    offs = jnp.concatenate(
        [
            jnp.broadcast_to(offs[:, :, lanes * t : lanes * t + 1], (peers, CAP, 128))
            for t in range(tables)
        ],
        axis=1,
    ).reshape(peers * CAP * tables, 128).T
    center = lax.broadcasted_iota(jnp.int32, offs.shape, 0).astype(F32)
    hot = jnp.concatenate(
        [(offs == center + float(128 * k)).astype(BF) for k in range(cdev // 128)], axis=0
    )
    for j in range(blocks):
        hi, lo = split2(pick(hot, block_of(points, j, tables), NN))
        summed[:, 128 * j : 128 * (j + 1)] = hi
        summed[:, part + 128 * j : part + 128 * (j + 1)] = lo


def coeff_body(summed, grads, coeff):
    out, part = coeff.shape
    g1, g2 = split2(grads[...])
    both = mm(jnp.concatenate([g1, g2], axis=0), summed[...], NN)
    both = both[:out] + both[out:]
    coeff[...] = both[:, :part] + both[:, part:]


def corr_body(member, summed, coeff, eig_scale, grads, corr):
    out, part = coeff.shape
    scale = eig_scale[:, pl.ds(pl.multiple_of(member[0] * part, part), part)]
    c1, c2 = split2(coeff[...] * scale)
    cc = jnp.concatenate([c1, c2], axis=0)
    both = mm(cc, summed[:, :part], NT) + mm(cc, summed[:, part:], NT)
    corr[...] = both[:out] + both[out:] - grads[...] * 0.25


def shape(*dims, dtype=F32):
    return jax.ShapeDtypeStruct(dims, dtype)


def params(mib=16):
    return pltpu.CompilerParams(vmem_limit_bytes=mib << 20)


def call(body, outs, *args, mib=16, scalars=0, **kw):
    many = isinstance(outs, (list, tuple))
    smem = pl.BlockSpec(memory_space=pltpu.SMEM)
    return pl.pallas_call(
        body,
        out_shape=outs,
        in_specs=[smem] * scalars + [VMEM] * (len(args) - scalars),
        out_specs=[VMEM] * len(outs) if many else VMEM,
        compiler_params=params(mib),
        **kw,
    )(*args)


def exchange(v, axes):
    return add_up([v] * math.prod(SIZES[a] for a in axes), axes)


def mates(parts, axes):
    return [mate_of(parts[o], axes, o) for o in range(1, len(parts))]


def add_up(parts, axes):
    order = sorted(range(1, len(parts)), key=lambda o: o != 2)
    return functools.reduce(jnp.add, [mate_of(parts[o], axes, o) for o in order], parts[0])


def mate_of(v, axes, o):
    n = math.prod(SIZES[a] for a in axes)
    return lax.ppermute(v, axes, [(i, i ^ o) for i in range(n)])


def together(*arrays):
    return lax.optimization_barrier(arrays)


def per_device(
    pool_features, pool_targets, batch_index, centers, weights,
    eig_vectors, eig_scale, nys_owner, nys_offset,
):
    rows, dim = batch_index.shape[0], pool_features.shape[1]
    nx, ny, half = SIZES["x"], SIZES["y"], rows // 2
    cdev, out = weights.shape
    count, q = eig_vectors.shape
    tables = math.prod(SIZES[a] for a in PLANES)
    peers = math.prod(SIZES[a] for a in OWNERS)
    norm = 1.0 / math.sqrt(rows * math.prod(SIZES[a] for a in ALL))
    x = lax.axis_index("x").astype(jnp.int32)[None]
    member = lax.axis_index(PLANES).astype(jnp.int32)[None]
    wide = 2 * out

    hbm = pl.BlockSpec(memory_space=pltpu.HBM)
    drawn, pack, *parted = pl.pallas_call(
        functools.partial(front_body, tables=tables),
        out_shape=[shape(rows + half, dim), shape(cdev + cdev // 2, dim)]
        + [shape(count + 8, q // tables)] * tables,
        in_specs=[pl.BlockSpec(memory_space=pltpu.SMEM)] + [hbm] * 8,
        out_specs=[VMEM] * (2 + tables),
        scratch_shapes=[
            pltpu.VMEM((1, rows), jnp.int32),
            pltpu.VMEM(pool_features.shape, F32),
            pltpu.VMEM(pool_targets.shape[::-1], F32),
            pltpu.VMEM((out, cdev), F32),
            pltpu.VMEM(eig_vectors.shape, F32),
            pltpu.VMEM((1, count), jnp.int32),
            pltpu.VMEM((1, count), jnp.int32),
            pltpu.SemaphoreType.DMA((8,)),
        ],
        compiler_params=params(16),
    )(
        member,
        *(
            pltpu.with_memory_space_constraint(v, pltpu.HBM)
            for v in (
                batch_index.reshape(1, rows), pool_features, pool_targets.T, weights.T, centers,
                eig_vectors, nys_owner.reshape(1, count), nys_offset.reshape(1, count),
            )
        ),
    )

    hops = (2, 1, 3)
    gathered = [mate_of(drawn, ("x",), o) for o in hops]
    tile = lax.ppermute(pack, ("core", "zl"), [(0, 0), (2, 1), (1, 2), (3, 3)])
    first = mate_of(parted[3], PLANES, 3)
    tile, first, drawn, *gathered = together(tile, first, drawn, *gathered)
    own = call(
        functools.partial(order_body, offsets=(0,) + hops),
        shape(nx, rows + half, dim), x, drawn, *gathered,
        scalars=1,
    )
    others = [mate_of(tile, ("y",), o) for o in TILES[1:]]
    mate = mate_of(own, ("core",), 1)
    mate, second, third = together(mate, parted[2], parted[1])
    parted = [parted[0], first, mate_of(second, PLANES, 2), mate_of(third, PLANES, 1)]

    def kernel(packs, extra):
        nb = len(packs)
        outs = [shape(nb, 2 * nx * rows, cdev, dtype=BF)] * 2 + [shape(nx, half, wide)] * 2
        if extra:
            outs = outs + [shape(nx, half, wide), shape(8, cdev)]
        return call(
            functools.partial(kernel_body, nb=nb, rows=rows, sub=32, extra=extra),
            outs, own, mate, *packs,
            scratch_shapes=[
                pltpu.VMEM((2, nx * rows, 6 * dim), BF),
                pltpu.VMEM((nb, cdev, 6 * dim), BF),
                pltpu.VMEM((nb, cdev, wide), BF),
                pltpu.VMEM((nx * rows, cdev), F32),
                pltpu.VMEM((nx * rows, cdev), F32),
                pltpu.VMEM((2 * nx * rows, wide), F32),
            ],
            cost_estimate=pl.CostEstimate(
                flops=100_000_000 if extra else 10_000_000_000 * nb, bytes_accessed=1 << 16, transcendentals=0
            ),
        )

    khi_a, klo_a, keep_a, send_a, scale, sb = kernel([tile], True)

    keep_a, *parted = together(keep_a, *parted)
    points = call(
        functools.partial(vectors_body, cdev=cdev),
        shape(peers, CAP * (tables * (q // tables // 128) + 1), 128),
        *parted,
    )
    points = lax.all_to_all(points, OWNERS, split_axis=0, concat_axis=0, tiled=True)

    khi_b, klo_b, keep_b, send_b = kernel(others, False)

    (got,) = mates([send_a + send_b] * 2, ("core",))
    total = exchange(keep_a + keep_b + got, ("x",))
    resid, ready = call(
        functools.partial(residual_body, rows=rows, norm=norm),
        [shape(rows, out), shape(nx, half, wide)],
        x, total, own, scale,
        scalars=1, scratch_shapes=[pltpu.VMEM((nx, half, wide), F32)],
    )
    (ready_mate,) = mates([ready] * 2, ("core",))

    parts = call(
        grads_body, [shape(out, cdev)] * 4, ready, ready_mate, khi_a, klo_a, khi_b, klo_b
    )
    parts = [parts[TILES.index(o)] for o in range(ny)]
    grads = add_up(parts, ("y",)) * sb[0:1]
    points, grads = together(points, grads)
    summed = call(
        functools.partial(gather_body, tables=tables),
        shape(cdev, 2 * q // tables, dtype=BF), points,
        cost_estimate=pl.CostEstimate(
            flops=800_000_000, bytes_accessed=1 << 21, transcendentals=0
        ),
    )
    grads = exchange(grads, PLANES)
    coeff = call(coeff_body, shape(out, q // tables), summed, grads)
    for axis in OWNERS[::-1]:
        coeff = exchange(coeff, (axis,))
    corr = call(
        corr_body, shape(out, cdev), member, summed, coeff, eig_scale[None, :], grads, scalars=1
    )
    received = []
    for r in (2, 3, 1, 0):
        perm = [
            ((z // 2) * 4 + k * 2 + z % 2, ((z ^ r) // 2) * 4 + ((z ^ r) % 2) * 2 + k)
            for k in range(2) for z in range(4)
        ]
        received.append(lax.ppermute(corr, ("zh", "core", "zl"), perm))
    return resid, functools.reduce(jnp.add, received).T


def solution(mesh):
    fine = Mesh(mesh.devices.reshape(tuple(SIZES[a] for a in ALL)), ALL)
    placed = (
        P(ALL, None),
        P(ALL, None),
        P(ALL),
        P(CENTERS, None),
        P(CENTERS, None),
        P(ALL, None),
        P(),
        P(ALL, None),
        P(ALL),
    )
    return jax.shard_map(
        per_device,
        mesh=fine,
        in_specs=placed,
        out_specs=(P(ALL, None), P(CENTERS, None)),
        check_vma=False,
    )
```

```python
import functools
import math

import jax
import jax.numpy as jnp
from jax import lax
from jax.experimental import pallas as pl
from jax.experimental.pallas import tpu as pltpu
from jax.sharding import Mesh, PartitionSpec as P

EPS = 1e-06
CAP = 8
BF = jnp.bfloat16
F32 = jnp.float32
SIZES = {"zh": 2, "core": 2, "x": 4, "y": 4, "zl": 2}
ALL = ("zh", "core", "x", "y", "zl")
CENTERS = ("x", "y", "zl")
PLANES = ("zh", "zl")
TILES = (0, 1, 3, 2)
OWNERS = ("x", "y", "core")
VMEM = pl.BlockSpec(memory_space=pltpu.VMEM)

ACOS_FULL = (
    0.49999988079071045, -0.3182917535305023, 0.24954961240291595, -0.20787927508354187,
    0.1663874238729477, -0.10994759202003479, 0.04858129099011421, -0.01009112037718296,
)
ACOS_HIGH = (
    0.4998512864112854, -0.3162611424922943, 0.2378545105457306, -0.17122769355773926,
    0.09912680834533784, -0.03783833235502243, 0.006804656237363815,
)

NN = (((1,), (0,)), ((), ()))
NT = (((1,), (1,)), ((), ()))


def mm(a, b, dims):
    return lax.dot_general(a, b, dims, preferred_element_type=F32)


def split2(x):
    hi = x.astype(BF)
    return hi, (x - hi.astype(F32)).astype(BF)


def split3(x):
    hi = x.astype(BF)
    rest = x - hi.astype(F32)
    mid = rest.astype(BF)
    return hi, mid, (rest - mid.astype(F32)).astype(BF)


def pick(onehot, x, dims, flip=False):
    parts = split3(x)
    prods = [mm(p, onehot, dims) if flip else mm(onehot, p, dims) for p in parts]
    return prods[0] + prods[1] + prods[2]


def full_nt(a, b):
    a1, a2, a3 = split3(a)
    b1, b2, b3 = split3(b)
    return (
        mm(a1, b1, NT) + (mm(a1, b2, NT) + mm(a2, b1, NT))
        + (mm(a2, b2, NT) + mm(a1, b3, NT) + mm(a3, b1, NT))
    )


def horner(coefs, x):
    acc = coefs[-1] * x + coefs[-2]
    for c in coefs[-3::-1]:
        acc = acc * x + c
    return acc


def ntk_over_scale(c):
    inv_pi = 1.0 / math.pi
    ntk = c
    for layer in range(3):
        w = jnp.maximum(1.0 - c * c, 1e-30)
        root = w * lax.rsqrt(w)
        arg = jnp.abs(c) if layer == 0 else c
        angle = root * horner(ACOS_HIGH if layer == 2 else ACOS_FULL, arg)
        remain = jnp.where(c < 0.0, angle, 1.0 - angle) if layer == 0 else 1.0 - angle
        if layer == 2:
            return root * inv_pi + remain * (c + ntk)
        c = root * inv_pi + remain * c
        ntk = c + ntk * remain


def rows_hot(index, width):
    n = index.shape[1]
    col = jnp.broadcast_to(index.astype(F32), (128, n)).T
    lane = lax.broadcasted_iota(jnp.int32, (n, 128), 1).astype(F32)
    return jnp.concatenate(
        [(col == lane + float(128 * k)).astype(BF) for k in range(width // 128)], axis=1
    )


def packed(x):
    half = x.shape[0] // 2
    return jnp.concatenate([x[:half], x[half:]], axis=1)


def unpacked(x):
    wide = x.shape[-1] // 2
    return jnp.concatenate([x[..., :wide], x[..., wide:]], axis=-2)


def front_body(member, *refs, tables):
    index_h, pool_f, pool_t, weights_h, centers, eig_h, owner_h, offset_h = refs[0:8]
    drawn, pack = refs[8:10]
    parts = refs[10 : 10 + tables]
    index, feats, targs, wts, eig, owner, offset, sems = refs[10 + tables :]
    cdev = centers.shape[0]
    copies = [
        pltpu.make_async_copy(src, dst, sems.at[n])
        for n, (src, dst) in enumerate(
            (
                (index_h, index), (pool_f, feats), (pool_t, targs), (weights_h, wts),
                (centers, pack.at[0:cdev, :]), (eig_h, eig), (owner_h, owner), (offset_h, offset),
            )
        )
    ]
    for copy in copies:
        copy.start()
    rows = index.shape[1]
    copies[0].wait()
    hot = rows_hot(index[...], feats.shape[0])
    copies[1].wait()
    drawn[0:rows, :] = pick(hot, feats[...], NN)
    copies[2].wait()
    drawn[rows:, :] = packed(pick(hot, targs[...], NT, flip=True).T)
    copies[3].wait()
    pack[cdev:, :] = packed(wts[...].T)
    for copy in copies[4:]:
        copy.wait()
    count, q = eig.shape
    part = q // tables
    row = jnp.broadcast_to((owner[...] * cdev + offset[...]).astype(F32), (8, count))
    row = jnp.concatenate([row] * (part // count), axis=1)
    for o, out in enumerate(parts):
        mate = member[0] ^ o
        out[0:count, :] = eig[:, pl.ds(pl.multiple_of(mate * part, part), part)]
        out[count:, :] = row


def order_body(x, *refs, offsets):
    parts, out = refs[:-1], refs[-1]
    for o, part in zip(offsets, parts):
        out[x[0] ^ o] = part[...]


def vectors_body(*refs, cdev):
    tables, send = refs[:-1], refs[-1]
    count, part = tables[0].shape[0] - 8, tables[0].shape[1]
    peers = send.shape[0]
    blocks, group, lanes = part // 128, CAP * len(tables), 128 // len(tables)
    earlier = lax.broadcasted_iota(jnp.int32, (count, count), 0) < lax.broadcasted_iota(
        jnp.int32, (count, count), 1
    )
    shared = []
    for t, table in enumerate(tables):
        nys = table[count : count + 1, 0:count].astype(jnp.int32)
        owner = nys // cdev
        offset = nys - owner * cdev
        row = jnp.broadcast_to(owner.astype(F32), (count, count))
        same = jnp.where(row.T == row, 1.0, 0.0)
        rank = jnp.sum(jnp.where(earlier, same, 0.0), axis=0, keepdims=True).astype(jnp.int32)
        place = owner * CAP + rank == lax.broadcasted_iota(jnp.int32, (peers * CAP, count), 0)
        offs = jnp.sum(jnp.where(place, offset.astype(F32), 0.0), axis=1, keepdims=True)
        shared.append(jnp.broadcast_to(offs, (peers * CAP, lanes)))
        vectors = pick(place.astype(BF), table[0:count, :], NN)
        for o in range(peers):
            own = slice(o * CAP, (o + 1) * CAP)
            for j in range(blocks):
                at = group * j + CAP * t
                send[o, at : at + CAP, :] = vectors[own, 128 * j : 128 * (j + 1)]
    shared = jnp.concatenate(shared, axis=1)
    for o in range(peers):
        send[o, group * blocks :, :] = shared[o * CAP : (o + 1) * CAP]


def kernel_body(*refs, nb, rows, sub, extra):
    own, mate = refs[0:2]
    packs = refs[2 : 2 + nb]
    khi, klo, keep, send = refs[2 + nb : 6 + nb]
    lhs, cen, wts, cos_a, cos_b, acc = refs[-6:]
    dim, count = own.shape[2], khi.shape[2]
    block = own.shape[0] * rows
    out = dim // 2
    for h, part in enumerate((own, mate)):
        f = part[:, 0:rows, :].reshape(block, dim)
        sa = jnp.sqrt(jnp.mean(f * f, axis=1, keepdims=True) + EPS)
        a1, a2, a3 = split3(f / sa)
        lhs[h] = jnp.concatenate([a1, a2, a1, a2, a1, a3], axis=1)
        if extra and h == 0:
            wide = jnp.broadcast_to(sa, (block, out)).reshape(own.shape[0], rows, out)
            half = rows // 2
            refs[6 + nb][...] = jnp.concatenate([wide[:, :half], wide[:, half:]], axis=2)
    for j, pack in enumerate(packs):
        b = pack[0:count, :]
        sb = jnp.sqrt(jnp.mean(b * b, axis=1, keepdims=True) + EPS)
        b1, b2, b3 = split3(b / sb * (1.0 / dim))
        cen[j] = jnp.concatenate([b1, b1, b2, b2, b3, b1], axis=1)
        w1, w2 = split2(unpacked(pack[count:, :]) * sb)
        wts[j] = jnp.concatenate([w1, w2], axis=1)
        if extra:
            nb_row = full_nt(jnp.ones((8, dim), F32), b * b) * (1.0 / dim) + EPS
            refs[7 + nb][...] = jnp.sqrt(nb_row)
    acc[...] = jnp.zeros(acc.shape, F32)

    def cosines(dst, j, h, n):
        at = slice(n * (count // 2), (n + 1) * (count // 2))
        dst[:, at] = mm(lhs[h], cen[j, at, :], NT)

    def elementwise(values, j, h, n):
        at = slice(h * block + n * sub, h * block + (n + 1) * sub)
        hi, lo = split2(ntk_over_scale(values[n * sub : (n + 1) * sub, :]))
        khi[j, at, :] = hi
        klo[j, at, :] = lo

    def predict(j, h):
        at = slice(h * block, (h + 1) * block)
        both = mm(khi[j, at, :], wts[j], NN) + mm(klo[j, at, :], wts[j], NN)
        acc[at, :] = acc[at, :] + both

    def step(j, h, now, later, after):
        elems = [functools.partial(elementwise, now, j, h, n) for n in range(block // sub)]
        others = [functools.partial(cosines, later, *after, n) for n in range(2)] if after else []
        if h == 1:
            others.append(functools.partial(predict, j, 0))
        every = len(elems) // 3
        for n, f in enumerate(elems):
            if n % every == 0 and others:
                others.pop(0)()
            f()

    for n in range(2):
        cosines(cos_a, 0, 0, n)
    if nb == 1:
        step(0, 0, cos_a, cos_b, (0, 1))
        step(0, 1, cos_b, cos_a, None)
        predict(0, 1)
    else:

        def pair(j, _):
            step(j, 0, cos_a, cos_b, (j, 1))
            step(j, 1, cos_b, cos_a, (jnp.minimum(j + 1, nb - 1), 0))
            predict(j, 1)
            return 0

        lax.fori_loop(0, nb, pair, 0)
    for h, dst in enumerate((keep, send)):
        total = acc[h * block : (h + 1) * block, :]
        total = (total[:, :out] + total[:, out:]).reshape(own.shape[0], 2, rows // 2, out)
        dst[...] = jnp.concatenate([total[:, 0], total[:, 1]], axis=2)


def residual_body(x, total, own, scale, resid, ready, value, *, rows, norm):
    value[...] = scale[...] * total[...] - own[:, rows:, :]
    resid[...] = unpacked(value[x[0]])
    ready[...] = value[...] * scale[...] * norm


def grads_body(own, mate, *refs):
    outs = refs[-4:]
    r = jnp.concatenate([unpacked(own[...]), unpacked(mate[...])], axis=0)
    out = r.shape[2]
    r1, r2 = split2(r.reshape(-1, out).T)
    rr = jnp.concatenate([r1, r2], axis=0)
    place = 0
    for khi, klo in zip(refs[0:-4:2], refs[1:-4:2]):
        for j in range(khi.shape[0]):
            both = mm(rr, khi[j], NN) + mm(rr, klo[j], NN)
            outs[place][...] = both[:out] + both[out:]
            place += 1


def block_of(points, j, tables):
    peers, group = points.shape[0], CAP * tables
    return points[:, group * j : group * (j + 1), :].reshape(peers * group, 128)


def gather_body(points, summed, *, tables):
    cdev, part = summed.shape[0], summed.shape[1] // 2
    blocks = part // 128
    peers, lanes = points.shape[0], 128 // tables
    offs = points[:, CAP * tables * blocks :, :]
    offs = jnp.concatenate(
        [
            jnp.broadcast_to(offs[:, :, lanes * t : lanes * t + 1], (peers, CAP, 128))
            for t in range(tables)
        ],
        axis=1,
    ).reshape(peers * CAP * tables, 128).T
    center = lax.broadcasted_iota(jnp.int32, offs.shape, 0).astype(F32)
    hot = jnp.concatenate(
        [(offs == center + float(128 * k)).astype(BF) for k in range(cdev // 128)], axis=0
    )
    for j in range(blocks):
        hi, lo = split2(pick(hot, block_of(points, j, tables), NN))
        summed[:, 128 * j : 128 * (j + 1)] = hi
        summed[:, part + 128 * j : part + 128 * (j + 1)] = lo


def coeff_body(summed, grads, coeff):
    out, part = coeff.shape
    g1, g2 = split2(grads[...])
    both = mm(jnp.concatenate([g1, g2], axis=0), summed[...], NN)
    both = both[:out] + both[out:]
    coeff[...] = both[:, :part] + both[:, part:]


def corr_body(member, summed, coeff, eig_scale, grads, corr):
    out, part = coeff.shape
    scale = eig_scale[:, pl.ds(pl.multiple_of(member[0] * part, part), part)]
    c1, c2 = split2(coeff[...] * scale)
    cc = jnp.concatenate([c1, c2], axis=0)
    both = mm(cc, summed[:, :part], NT) + mm(cc, summed[:, part:], NT)
    corr[...] = both[:out] + both[out:] - grads[...] * 0.25


def shape(*dims, dtype=F32):
    return jax.ShapeDtypeStruct(dims, dtype)


def params(mib=16):
    return pltpu.CompilerParams(vmem_limit_bytes=mib << 20)


def call(body, outs, *args, mib=16, scalars=0, **kw):
    many = isinstance(outs, (list, tuple))
    smem = pl.BlockSpec(memory_space=pltpu.SMEM)
    return pl.pallas_call(
        body,
        out_shape=outs,
        in_specs=[smem] * scalars + [VMEM] * (len(args) - scalars),
        out_specs=[VMEM] * len(outs) if many else VMEM,
        compiler_params=params(mib),
        **kw,
    )(*args)


def exchange(v, axes):
    return add_up([v] * math.prod(SIZES[a] for a in axes), axes)


def mates(parts, axes):
    return [mate_of(parts[o], axes, o) for o in range(1, len(parts))]


def add_up(parts, axes):
    order = sorted(range(1, len(parts)), key=lambda o: o != 2)
    return functools.reduce(jnp.add, [mate_of(parts[o], axes, o) for o in order], parts[0])


def mate_of(v, axes, o):
    n = math.prod(SIZES[a] for a in axes)
    return lax.ppermute(v, axes, [(i, i ^ o) for i in range(n)])


def together(*arrays):
    return lax.optimization_barrier(arrays)


def per_device(
    pool_features, pool_targets, batch_index, centers, weights,
    eig_vectors, eig_scale, nys_owner, nys_offset,
):
    rows, dim = batch_index.shape[0], pool_features.shape[1]
    nx, ny, half = SIZES["x"], SIZES["y"], rows // 2
    cdev, out = weights.shape
    count, q = eig_vectors.shape
    tables = math.prod(SIZES[a] for a in PLANES)
    peers = math.prod(SIZES[a] for a in OWNERS)
    norm = 1.0 / math.sqrt(rows * math.prod(SIZES[a] for a in ALL))
    x = lax.axis_index("x").astype(jnp.int32)[None]
    member = lax.axis_index(PLANES).astype(jnp.int32)[None]
    wide = 2 * out

    hbm = pl.BlockSpec(memory_space=pltpu.HBM)
    drawn, pack, *parted = pl.pallas_call(
        functools.partial(front_body, tables=tables),
        out_shape=[shape(rows + half, dim), shape(cdev + cdev // 2, dim)]
        + [shape(count + 8, q // tables)] * tables,
        in_specs=[pl.BlockSpec(memory_space=pltpu.SMEM)] + [hbm] * 8,
        out_specs=[VMEM] * (2 + tables),
        scratch_shapes=[
            pltpu.VMEM((1, rows), jnp.int32),
            pltpu.VMEM(pool_features.shape, F32),
            pltpu.VMEM(pool_targets.shape[::-1], F32),
            pltpu.VMEM((out, cdev), F32),
            pltpu.VMEM(eig_vectors.shape, F32),
            pltpu.VMEM((1, count), jnp.int32),
            pltpu.VMEM((1, count), jnp.int32),
            pltpu.SemaphoreType.DMA((8,)),
        ],
        compiler_params=params(16),
    )(
        member,
        *(
            pltpu.with_memory_space_constraint(v, pltpu.HBM)
            for v in (
                batch_index.reshape(1, rows), pool_features, pool_targets.T, weights.T, centers,
                eig_vectors, nys_owner.reshape(1, count), nys_offset.reshape(1, count),
            )
        ),
    )

    hops = (2, 1, 3)
    gathered = [mate_of(drawn, ("x",), o) for o in hops]
    tile = lax.ppermute(pack, ("core", "zl"), [(0, 0), (2, 1), (1, 2), (3, 3)])
    first = mate_of(parted[2], PLANES, 2)
    tile, first, drawn, *gathered = together(tile, first, drawn, *gathered)
    own = call(
        functools.partial(order_body, offsets=(0,) + hops),
        shape(nx, rows + half, dim), x, drawn, *gathered,
        scalars=1,
    )
    others = [mate_of(tile, ("y",), o) for o in TILES[1:]]
    mate = mate_of(own, ("core",), 1)
    own, second = together(own, parted[1])
    mate, third = together(mate, parted[3])
    parted = [parted[0], first, mate_of(second, PLANES, 1), mate_of(third, PLANES, 3)]

    def kernel(packs, extra):
        nb = len(packs)
        outs = [shape(nb, 2 * nx * rows, cdev, dtype=BF)] * 2 + [shape(nx, half, wide)] * 2
        if extra:
            outs = outs + [shape(nx, half, wide), shape(8, cdev)]
        return call(
            functools.partial(kernel_body, nb=nb, rows=rows, sub=32, extra=extra),
            outs, own, mate, *packs,
            scratch_shapes=[
                pltpu.VMEM((2, nx * rows, 6 * dim), BF),
                pltpu.VMEM((nb, cdev, 6 * dim), BF),
                pltpu.VMEM((nb, cdev, wide), BF),
                pltpu.VMEM((nx * rows, cdev), F32),
                pltpu.VMEM((nx * rows, cdev), F32),
                pltpu.VMEM((2 * nx * rows, wide), F32),
            ],
            cost_estimate=pl.CostEstimate(
                flops=100_000_000 if extra else 10_000_000_000 * nb, bytes_accessed=1 << 16, transcendentals=0
            ),
        )

    khi_a, klo_a, keep_a, send_a, scale, sb = kernel([tile], True)

    keep_a, *parted = together(keep_a, *parted)
    points = call(
        functools.partial(vectors_body, cdev=cdev),
        shape(peers, CAP * (tables * (q // tables // 128) + 1), 128),
        *parted,
    )
    points = lax.all_to_all(points, OWNERS, split_axis=0, concat_axis=0, tiled=True)

    khi_b, klo_b, keep_b, send_b = kernel(others, False)

    (got,) = mates([send_a + send_b] * 2, ("core",))
    total = exchange(keep_a + keep_b + got, ("x",))
    resid, ready = call(
        functools.partial(residual_body, rows=rows, norm=norm),
        [shape(rows, out), shape(nx, half, wide)],
        x, total, own, scale,
        scalars=1, scratch_shapes=[pltpu.VMEM((nx, half, wide), F32)],
    )
    (ready_mate,) = mates([ready] * 2, ("core",))

    parts = call(
        grads_body, [shape(out, cdev)] * 4, ready, ready_mate, khi_a, klo_a, khi_b, klo_b
    )
    parts = [parts[TILES.index(o)] for o in range(ny)]
    grads = add_up(parts, ("y",)) * sb[0:1]
    points, grads = together(points, grads)
    summed = call(
        functools.partial(gather_body, tables=tables),
        shape(cdev, 2 * q // tables, dtype=BF), points,
        cost_estimate=pl.CostEstimate(
            flops=800_000_000, bytes_accessed=1 << 21, transcendentals=0
        ),
    )
    grads = exchange(grads, PLANES)
    coeff = call(coeff_body, shape(out, q // tables), summed, grads)
    for axis in OWNERS[::-1]:
        coeff = exchange(coeff, (axis,))
    corr = call(
        corr_body, shape(out, cdev), member, summed, coeff, eig_scale[None, :], grads, scalars=1
    )
    received = []
    for r in (2, 3, 1, 0):
        perm = [
            ((z // 2) * 4 + k * 2 + z % 2, ((z ^ r) // 2) * 4 + ((z ^ r) % 2) * 2 + k)
            for k in range(2) for z in range(4)
        ]
        received.append(lax.ppermute(corr, ("zh", "core", "zl"), perm))
    return resid, functools.reduce(jnp.add, received).T


def solution(mesh):
    fine = Mesh(mesh.devices.reshape(tuple(SIZES[a] for a in ALL)), ALL)
    placed = (
        P(ALL, None),
        P(ALL, None),
        P(ALL),
        P(CENTERS, None),
        P(CENTERS, None),
        P(ALL, None),
        P(),
        P(ALL, None),
        P(ALL),
    )
    return jax.shard_map(
        per_device,
        mesh=fine,
        in_specs=placed,
        out_specs=(P(ALL, None), P(CENTERS, None)),
        check_vma=False,
    )
```

```python
import functools
import math

import jax
import jax.numpy as jnp
from jax import lax
from jax.experimental import pallas as pl
from jax.experimental.pallas import tpu as pltpu
from jax.sharding import Mesh, PartitionSpec as P

EPS = 1e-06
CAP = 8
BF = jnp.bfloat16
F32 = jnp.float32
SIZES = {"zh": 2, "core": 2, "x": 4, "y": 4, "zl": 2}
ALL = ("zh", "core", "x", "y", "zl")
CENTERS = ("x", "y", "zl")
PLANES = ("zh", "zl")
TILES = (0, 1, 3, 2)
OWNERS = ("x", "y", "core")
VMEM = pl.BlockSpec(memory_space=pltpu.VMEM)

ACOS_FULL = (
    0.49999988079071045, -0.3182917535305023, 0.24954961240291595, -0.20787927508354187,
    0.1663874238729477, -0.10994759202003479, 0.04858129099011421, -0.01009112037718296,
)
ACOS_HIGH = (
    0.4998512864112854, -0.3162611424922943, 0.2378545105457306, -0.17122769355773926,
    0.09912680834533784, -0.03783833235502243, 0.006804656237363815,
)

NN = (((1,), (0,)), ((), ()))
NT = (((1,), (1,)), ((), ()))


def mm(a, b, dims):
    return lax.dot_general(a, b, dims, preferred_element_type=F32)


def split2(x):
    hi = x.astype(BF)
    return hi, (x - hi.astype(F32)).astype(BF)


def split3(x):
    hi = x.astype(BF)
    rest = x - hi.astype(F32)
    mid = rest.astype(BF)
    return hi, mid, (rest - mid.astype(F32)).astype(BF)


def pick(onehot, x, dims, flip=False):
    parts = split3(x)
    prods = [mm(p, onehot, dims) if flip else mm(onehot, p, dims) for p in parts]
    return prods[0] + prods[1] + prods[2]


def full_nt(a, b):
    a1, a2, a3 = split3(a)
    b1, b2, b3 = split3(b)
    return (
        mm(a1, b1, NT) + (mm(a1, b2, NT) + mm(a2, b1, NT))
        + (mm(a2, b2, NT) + mm(a1, b3, NT) + mm(a3, b1, NT))
    )


def horner(coefs, x):
    acc = coefs[-1] * x + coefs[-2]
    for c in coefs[-3::-1]:
        acc = acc * x + c
    return acc


def ntk_over_scale(c):
    inv_pi = 1.0 / math.pi
    ntk = c
    for layer in range(3):
        w = jnp.maximum(1.0 - c * c, 1e-30)
        root = w * lax.rsqrt(w)
        arg = jnp.abs(c) if layer == 0 else c
        angle = root * horner(ACOS_HIGH if layer == 2 else ACOS_FULL, arg)
        remain = jnp.where(c < 0.0, angle, 1.0 - angle) if layer == 0 else 1.0 - angle
        if layer == 2:
            return root * inv_pi + remain * (c + ntk)
        c = root * inv_pi + remain * c
        ntk = c + ntk * remain


def rows_hot(index, width):
    n = index.shape[1]
    col = jnp.broadcast_to(index.astype(F32), (128, n)).T
    lane = lax.broadcasted_iota(jnp.int32, (n, 128), 1).astype(F32)
    return jnp.concatenate(
        [(col == lane + float(128 * k)).astype(BF) for k in range(width // 128)], axis=1
    )


def packed(x):
    half = x.shape[0] // 2
    return jnp.concatenate([x[:half], x[half:]], axis=1)


def unpacked(x):
    wide = x.shape[-1] // 2
    return jnp.concatenate([x[..., :wide], x[..., wide:]], axis=-2)


def front_body(member, *refs, tables):
    index_h, pool_f, pool_t, weights_h, centers, eig_h, owner_h, offset_h = refs[0:8]
    drawn, pack = refs[8:10]
    parts = refs[10 : 10 + tables]
    index, feats, targs, wts, eig, owner, offset, sems = refs[10 + tables :]
    cdev = centers.shape[0]
    copies = [
        pltpu.make_async_copy(src, dst, sems.at[n])
        for n, (src, dst) in enumerate(
            (
                (index_h, index), (pool_f, feats), (pool_t, targs), (weights_h, wts),
                (centers, pack.at[0:cdev, :]), (eig_h, eig), (owner_h, owner), (offset_h, offset),
            )
        )
    ]
    for copy in copies:
        copy.start()
    rows = index.shape[1]
    copies[0].wait()
    hot = rows_hot(index[...], feats.shape[0])
    copies[1].wait()
    drawn[0:rows, :] = pick(hot, feats[...], NN)
    copies[2].wait()
    drawn[rows:, :] = packed(pick(hot, targs[...], NT, flip=True).T)
    copies[3].wait()
    pack[cdev:, :] = packed(wts[...].T)
    for copy in copies[4:]:
        copy.wait()
    count, q = eig.shape
    part = q // tables
    row = jnp.broadcast_to((owner[...] * cdev + offset[...]).astype(F32), (8, count))
    row = jnp.concatenate([row] * (part // count), axis=1)
    for o, out in enumerate(parts):
        mate = member[0] ^ o
        out[0:count, :] = eig[:, pl.ds(pl.multiple_of(mate * part, part), part)]
        out[count:, :] = row


def order_body(x, *refs, offsets):
    parts, out = refs[:-1], refs[-1]
    for o, part in zip(offsets, parts):
        out[x[0] ^ o] = part[...]


def vectors_body(*refs, cdev):
    tables, send = refs[:-1], refs[-1]
    count, part = tables[0].shape[0] - 8, tables[0].shape[1]
    peers = send.shape[0]
    blocks, group, lanes = part // 128, CAP * len(tables), 128 // len(tables)
    earlier = lax.broadcasted_iota(jnp.int32, (count, count), 0) < lax.broadcasted_iota(
        jnp.int32, (count, count), 1
    )
    shared = []
    for t, table in enumerate(tables):
        nys = table[count : count + 1, 0:count].astype(jnp.int32)
        owner = nys // cdev
        offset = nys - owner * cdev
        row = jnp.broadcast_to(owner.astype(F32), (count, count))
        same = jnp.where(row.T == row, 1.0, 0.0)
        rank = jnp.sum(jnp.where(earlier, same, 0.0), axis=0, keepdims=True).astype(jnp.int32)
        place = owner * CAP + rank == lax.broadcasted_iota(jnp.int32, (peers * CAP, count), 0)
        offs = jnp.sum(jnp.where(place, offset.astype(F32), 0.0), axis=1, keepdims=True)
        shared.append(jnp.broadcast_to(offs, (peers * CAP, lanes)))
        vectors = pick(place.astype(BF), table[0:count, :], NN)
        for o in range(peers):
            own = slice(o * CAP, (o + 1) * CAP)
            for j in range(blocks):
                at = group * j + CAP * t
                send[o, at : at + CAP, :] = vectors[own, 128 * j : 128 * (j + 1)]
    shared = jnp.concatenate(shared, axis=1)
    for o in range(peers):
        send[o, group * blocks :, :] = shared[o * CAP : (o + 1) * CAP]


def kernel_body(*refs, nb, rows, sub, extra):
    own, mate = refs[0:2]
    packs = refs[2 : 2 + nb]
    khi, klo, keep, send = refs[2 + nb : 6 + nb]
    lhs, cen, wts, cos_a, cos_b, acc = refs[-6:]
    dim, count = own.shape[2], khi.shape[2]
    block = own.shape[0] * rows
    out = dim // 2
    for h, part in enumerate((own, mate)):
        f = part[:, 0:rows, :].reshape(block, dim)
        sa = jnp.sqrt(jnp.mean(f * f, axis=1, keepdims=True) + EPS)
        a1, a2, a3 = split3(f / sa)
        lhs[h] = jnp.concatenate([a1, a2, a1, a2, a1, a3], axis=1)
        if extra and h == 0:
            wide = jnp.broadcast_to(sa, (block, out)).reshape(own.shape[0], rows, out)
            half = rows // 2
            refs[6 + nb][...] = jnp.concatenate([wide[:, :half], wide[:, half:]], axis=2)
    for j, pack in enumerate(packs):
        b = pack[0:count, :]
        sb = jnp.sqrt(jnp.mean(b * b, axis=1, keepdims=True) + EPS)
        b1, b2, b3 = split3(b / sb * (1.0 / dim))
        cen[j] = jnp.concatenate([b1, b1, b2, b2, b3, b1], axis=1)
        w1, w2 = split2(unpacked(pack[count:, :]) * sb)
        wts[j] = jnp.concatenate([w1, w2], axis=1)
        if extra:
            nb_row = full_nt(jnp.ones((8, dim), F32), b * b) * (1.0 / dim) + EPS
            refs[7 + nb][...] = jnp.sqrt(nb_row)
    acc[...] = jnp.zeros(acc.shape, F32)

    def cosines(dst, j, h, n):
        at = slice(n * (count // 2), (n + 1) * (count // 2))
        dst[:, at] = mm(lhs[h], cen[j, at, :], NT)

    def elementwise(values, j, h, n):
        at = slice(h * block + n * sub, h * block + (n + 1) * sub)
        hi, lo = split2(ntk_over_scale(values[n * sub : (n + 1) * sub, :]))
        khi[j, at, :] = hi
        klo[j, at, :] = lo

    def predict(j, h):
        at = slice(h * block, (h + 1) * block)
        both = mm(khi[j, at, :], wts[j], NN) + mm(klo[j, at, :], wts[j], NN)
        acc[at, :] = acc[at, :] + both

    def step(j, h, now, later, after):
        elems = [functools.partial(elementwise, now, j, h, n) for n in range(block // sub)]
        others = [functools.partial(cosines, later, *after, n) for n in range(2)] if after else []
        if h == 1:
            others.append(functools.partial(predict, j, 0))
        every = len(elems) // 3
        for n, f in enumerate(elems):
            if n % every == 0 and others:
                others.pop(0)()
            f()

    for n in range(2):
        cosines(cos_a, 0, 0, n)
    if nb == 1:
        step(0, 0, cos_a, cos_b, (0, 1))
        step(0, 1, cos_b, cos_a, None)
        predict(0, 1)
    else:

        def pair(j, _):
            step(j, 0, cos_a, cos_b, (j, 1))
            step(j, 1, cos_b, cos_a, (jnp.minimum(j + 1, nb - 1), 0))
            predict(j, 1)
            return 0

        lax.fori_loop(0, nb, pair, 0)
    for h, dst in enumerate((keep, send)):
        total = acc[h * block : (h + 1) * block, :]
        total = (total[:, :out] + total[:, out:]).reshape(own.shape[0], 2, rows // 2, out)
        dst[...] = jnp.concatenate([total[:, 0], total[:, 1]], axis=2)


def residual_body(x, total, own, scale, resid, ready, value, *, rows, norm):
    value[...] = scale[...] * total[...] - own[:, rows:, :]
    resid[...] = unpacked(value[x[0]])
    ready[...] = value[...] * scale[...] * norm


def grads_body(own, mate, *refs):
    outs = refs[-4:]
    r = jnp.concatenate([unpacked(own[...]), unpacked(mate[...])], axis=0)
    out = r.shape[2]
    r1, r2 = split2(r.reshape(-1, out).T)
    rr = jnp.concatenate([r1, r2], axis=0)
    place = 0
    for khi, klo in zip(refs[0:-4:2], refs[1:-4:2]):
        for j in range(khi.shape[0]):
            both = mm(rr, khi[j], NN) + mm(rr, klo[j], NN)
            outs[place][...] = both[:out] + both[out:]
            place += 1


def block_of(points, j, tables):
    peers, group = points.shape[0], CAP * tables
    return points[:, group * j : group * (j + 1), :].reshape(peers * group, 128)


def gather_body(points, summed, *, tables):
    cdev, part = summed.shape[0], summed.shape[1] // 2
    blocks = part // 128
    peers, lanes = points.shape[0], 128 // tables
    offs = points[:, CAP * tables * blocks :, :]
    offs = jnp.concatenate(
        [
            jnp.broadcast_to(offs[:, :, lanes * t : lanes * t + 1], (peers, CAP, 128))
            for t in range(tables)
        ],
        axis=1,
    ).reshape(peers * CAP * tables, 128).T
    center = lax.broadcasted_iota(jnp.int32, offs.shape, 0).astype(F32)
    hot = jnp.concatenate(
        [(offs == center + float(128 * k)).astype(BF) for k in range(cdev // 128)], axis=0
    )
    for j in range(blocks):
        hi, lo = split2(pick(hot, block_of(points, j, tables), NN))
        summed[:, 128 * j : 128 * (j + 1)] = hi
        summed[:, part + 128 * j : part + 128 * (j + 1)] = lo


def coeff_body(summed, grads, coeff):
    out, part = coeff.shape
    g1, g2 = split2(grads[...])
    both = mm(jnp.concatenate([g1, g2], axis=0), summed[...], NN)
    both = both[:out] + both[out:]
    coeff[...] = both[:, :part] + both[:, part:]


def corr_body(member, summed, coeff, eig_scale, grads, corr):
    out, part = coeff.shape
    scale = eig_scale[:, pl.ds(pl.multiple_of(member[0] * part, part), part)]
    c1, c2 = split2(coeff[...] * scale)
    cc = jnp.concatenate([c1, c2], axis=0)
    both = mm(cc, summed[:, :part], NT) + mm(cc, summed[:, part:], NT)
    corr[...] = both[:out] + both[out:] - grads[...] * 0.25


def shape(*dims, dtype=F32):
    return jax.ShapeDtypeStruct(dims, dtype)


def params(mib=16):
    return pltpu.CompilerParams(vmem_limit_bytes=mib << 20)


def call(body, outs, *args, mib=16, scalars=0, **kw):
    many = isinstance(outs, (list, tuple))
    smem = pl.BlockSpec(memory_space=pltpu.SMEM)
    return pl.pallas_call(
        body,
        out_shape=outs,
        in_specs=[smem] * scalars + [VMEM] * (len(args) - scalars),
        out_specs=[VMEM] * len(outs) if many else VMEM,
        compiler_params=params(mib),
        **kw,
    )(*args)


def exchange(v, axes):
    return add_up([v] * math.prod(SIZES[a] for a in axes), axes)


def mates(parts, axes):
    return [mate_of(parts[o], axes, o) for o in range(1, len(parts))]


def add_up(parts, axes):
    order = sorted(range(1, len(parts)), key=lambda o: o != 2)
    return functools.reduce(jnp.add, [mate_of(parts[o], axes, o) for o in order], parts[0])


def mate_of(v, axes, o):
    n = math.prod(SIZES[a] for a in axes)
    return lax.ppermute(v, axes, [(i, i ^ o) for i in range(n)])


def together(*arrays):
    return lax.optimization_barrier(arrays)


def per_device(
    pool_features, pool_targets, batch_index, centers, weights,
    eig_vectors, eig_scale, nys_owner, nys_offset,
):
    rows, dim = batch_index.shape[0], pool_features.shape[1]
    nx, ny, half = SIZES["x"], SIZES["y"], rows // 2
    cdev, out = weights.shape
    count, q = eig_vectors.shape
    tables = math.prod(SIZES[a] for a in PLANES)
    peers = math.prod(SIZES[a] for a in OWNERS)
    norm = 1.0 / math.sqrt(rows * math.prod(SIZES[a] for a in ALL))
    x = lax.axis_index("x").astype(jnp.int32)[None]
    member = lax.axis_index(PLANES).astype(jnp.int32)[None]
    wide = 2 * out

    hbm = pl.BlockSpec(memory_space=pltpu.HBM)
    drawn, pack, *parted = pl.pallas_call(
        functools.partial(front_body, tables=tables),
        out_shape=[shape(rows + half, dim), shape(cdev + cdev // 2, dim)]
        + [shape(count + 8, q // tables)] * tables,
        in_specs=[pl.BlockSpec(memory_space=pltpu.SMEM)] + [hbm] * 8,
        out_specs=[VMEM] * (2 + tables),
        scratch_shapes=[
            pltpu.VMEM((1, rows), jnp.int32),
            pltpu.VMEM(pool_features.shape, F32),
            pltpu.VMEM(pool_targets.shape[::-1], F32),
            pltpu.VMEM((out, cdev), F32),
            pltpu.VMEM(eig_vectors.shape, F32),
            pltpu.VMEM((1, count), jnp.int32),
            pltpu.VMEM((1, count), jnp.int32),
            pltpu.SemaphoreType.DMA((8,)),
        ],
        compiler_params=params(16),
    )(
        member,
        *(
            pltpu.with_memory_space_constraint(v, pltpu.HBM)
            for v in (
                batch_index.reshape(1, rows), pool_features, pool_targets.T, weights.T, centers,
                eig_vectors, nys_owner.reshape(1, count), nys_offset.reshape(1, count),
            )
        ),
    )

    hops = (2, 1, 3)
    gathered = [mate_of(drawn, ("x",), o) for o in hops]
    tile = lax.ppermute(pack, ("core", "zl"), [(0, 0), (2, 1), (1, 2), (3, 3)])
    first = mate_of(parted[2], PLANES, 2)
    tile, first, drawn, *gathered = together(tile, first, drawn, *gathered)
    own = call(
        functools.partial(order_body, offsets=(0,) + hops),
        shape(nx, rows + half, dim), x, drawn, *gathered,
        scalars=1,
    )
    others = [mate_of(tile, ("y",), o) for o in TILES[1:]]
    mate = mate_of(own, ("core",), 1)
    own, second = together(own, parted[1])
    mate, third = together(mate, parted[3])
    parted = [parted[0], first, mate_of(second, PLANES, 1), mate_of(third, PLANES, 3)]

    def kernel(packs, extra):
        nb = len(packs)
        outs = [shape(nb, 2 * nx * rows, cdev, dtype=BF)] * 2 + [shape(nx, half, wide)] * 2
        if extra:
            outs = outs + [shape(nx, half, wide), shape(8, cdev)]
        return call(
            functools.partial(kernel_body, nb=nb, rows=rows, sub=16, extra=extra),
            outs, own, mate, *packs,
            scratch_shapes=[
                pltpu.VMEM((2, nx * rows, 6 * dim), BF),
                pltpu.VMEM((nb, cdev, 6 * dim), BF),
                pltpu.VMEM((nb, cdev, wide), BF),
                pltpu.VMEM((nx * rows, cdev), F32),
                pltpu.VMEM((nx * rows, cdev), F32),
                pltpu.VMEM((2 * nx * rows, wide), F32),
            ],
            cost_estimate=pl.CostEstimate(
                flops=100_000_000 if extra else 10_000_000_000 * nb, bytes_accessed=1 << 16, transcendentals=0
            ),
        )

    khi_a, klo_a, keep_a, send_a, scale, sb = kernel([tile], True)

    keep_a, *parted = together(keep_a, *parted)
    points = call(
        functools.partial(vectors_body, cdev=cdev),
        shape(peers, CAP * (tables * (q // tables // 128) + 1), 128),
        *parted,
    )
    points = lax.all_to_all(points, OWNERS, split_axis=0, concat_axis=0, tiled=True)

    khi_b, klo_b, keep_b, send_b = kernel(others, False)

    (got,) = mates([send_a + send_b] * 2, ("core",))
    total = exchange(keep_a + keep_b + got, ("x",))
    resid, ready = call(
        functools.partial(residual_body, rows=rows, norm=norm),
        [shape(rows, out), shape(nx, half, wide)],
        x, total, own, scale,
        scalars=1, scratch_shapes=[pltpu.VMEM((nx, half, wide), F32)],
    )
    (ready_mate,) = mates([ready] * 2, ("core",))

    parts = call(
        grads_body, [shape(out, cdev)] * 4, ready, ready_mate, khi_a, klo_a, khi_b, klo_b
    )
    parts = [parts[TILES.index(o)] for o in range(ny)]
    grads = add_up(parts, ("y",)) * sb[0:1]
    points, grads = together(points, grads)
    summed = call(
        functools.partial(gather_body, tables=tables),
        shape(cdev, 2 * q // tables, dtype=BF), points,
        cost_estimate=pl.CostEstimate(
            flops=800_000_000, bytes_accessed=1 << 21, transcendentals=0
        ),
    )
    grads = exchange(grads, PLANES)
    coeff = call(coeff_body, shape(out, q // tables), summed, grads)
    for axis in OWNERS[::-1]:
        coeff = exchange(coeff, (axis,))
    corr = call(
        corr_body, shape(out, cdev), member, summed, coeff, eig_scale[None, :], grads, scalars=1
    )
    received = []
    for r in (2, 3, 1, 0):
        perm = [
            ((z // 2) * 4 + k * 2 + z % 2, ((z ^ r) // 2) * 4 + ((z ^ r) % 2) * 2 + k)
            for k in range(2) for z in range(4)
        ]
        received.append(lax.ppermute(corr, ("zh", "core", "zl"), perm))
    return resid, functools.reduce(jnp.add, received).T


def solution(mesh):
    fine = Mesh(mesh.devices.reshape(tuple(SIZES[a] for a in ALL)), ALL)
    placed = (
        P(ALL, None),
        P(ALL, None),
        P(ALL),
        P(CENTERS, None),
        P(CENTERS, None),
        P(ALL, None),
        P(),
        P(ALL, None),
        P(ALL),
    )
    return jax.shard_map(
        per_device,
        mesh=fine,
        in_specs=placed,
        out_specs=(P(ALL, None), P(CENTERS, None)),
        check_vma=False,
    )
```
